32 devices in a mesh: sec: 8 (over z, x), op: 4 (over y, core).
Axes of the slice: x: 2, y: 2, z: 4, core: 2. Of those that a mesh axis runs over, the one named last changes fastest.
Arguments:
- wavefunction: bfloat16 [64, 384, 384], P('sec'), may hold values from -6 to 6
- left_ops: bfloat16 [32, 384, 384], P('op'), may hold values from -0.3125 to 0.3125
- right_ops: bfloat16 [32, 384, 384], P('op'), may hold values from -0.3125 to 0.3125
- charge: int32 [32], P('op'), may hold values from -1 to 1
- couple: int32 [32, 64], P('op', 'sec'), may hold values from 0 to 1, as said below
- amplitude: float32 [32, 64], P('op', 'sec'), may hold values from -0.6 to 0.6
Outputs:
- sigma: float32 [64, 384, 384], P('sec', 'op')
The draws below stay inside these ranges and needn't reach their ends.
Inputs may be any that keep to these rules, and one draw needn't show every extreme that they name: `couple`: 1 where operator k acts into target sector t, else 0.
All inputs are finite; a program needn't handle non-finite values.
Results may differ from the reference program's by a relative error of at most 0.0029.
Values may be sent and summed in bfloat16 or wider, within the bound.
No kernel may reach another device: no remote copies, remote signals or barrier semaphores. Data moves between devices by JAX's collectives and lax.ppermute only.
A program may use at most 64 MiB of HBM per device.

```python
import jax
import jax.numpy as jnp
from jax import lax

M = 384
NSEC = 64
K = 32


def draw_couple(key, part):
    levels = 10 + 80 * jnp.arange(NSEC, dtype=jnp.int32) // max(NSEC - 1, 1)
    rolled = jax.random.randint(key, (K, NSEC), 0, 100)
    return (rolled < levels[None, :]).astype(jnp.int32)


def with_ends(entries, stream_key, least, high):
    extent = entries.shape
    place = [jax.random.randint(jax.random.fold_in(stream_key, axis), (), 0, extent[axis]) for axis in range(len(extent))]
    entries = entries.at[tuple(place)].set(least)
    longest = extent.index(max(extent))
    place[longest] = (place[longest] + 1) % extent[longest]
    return entries.at[tuple(place)].set(high)


def block_scale(own_key, dims, cuts, least, top_value):
    factor_of = 1.0
    for dim, shards_of in cuts:
        draws = jax.random.uniform(jax.random.fold_in(jax.random.fold_in(own_key, 6), dim), (shards_of,), jnp.float32, least / len(cuts), top_value / len(cuts))
        factor_of = factor_of * jnp.repeat(jnp.exp(draws), dims[dim] // shards_of).reshape((-1,) + (1,) * (len(dims) - 1 - dim))
    return factor_of


def noise(rng, extent, width, bound, shards=(), held_as=jnp.bfloat16):
    array = width * jax.random.normal(rng, extent, jnp.float32)
    if shards:
        array = array * block_scale(rng, extent, shards, -0.22, 0.18)
    return jnp.clip(array, -bound, bound).astype(held_as)


def setup_inputs(seed: int = 0) -> dict:
    keys = jax.random.split(jax.random.key(seed), 7)
    return {
        "wavefunction": noise(keys[0], (NSEC, M, M), 1.0, 6.0, ((0, 8),)),
        "left_ops": noise(keys[1], (K, M, M), M ** -0.5, 0.3125, ((0, 4),)),
        "right_ops": noise(keys[2], (K, M, M), M ** -0.5, 0.3125, ((0, 4),)),
        "charge": with_ends(jax.random.randint(keys[3], (K,), -1, 2), jax.random.fold_in(keys[3], 1), -1, 1).astype(jnp.int32),
        "couple": draw_couple(jax.random.fold_in(keys[6], 71), 0),
        "amplitude": noise(keys[5], (K, NSEC), 0.1, 0.6, ((0, 4), (1, 8)), jnp.float32),
    }


def reference(wavefunction, left_ops, right_ops, charge, couple, amplitude):
    factor = amplitude * couple.astype(jnp.float32)
    blocks = wavefunction.astype(jnp.float32)

    def apply_op(accumulated, operands):
        left_op, right_op, sector_shift, factor_row = operands
        source = jnp.roll(blocks, sector_shift, axis=0)
        middle = jnp.matmul(left_op.astype(jnp.float32), source).astype(jnp.bfloat16)
        contribution = jnp.matmul(middle.astype(jnp.float32), right_op.astype(jnp.float32).T)
        return accumulated + factor_row[:, None, None] * contribution, None

    initial = jnp.zeros(wavefunction.shape, jnp.float32)
    sigma, unused = lax.scan(apply_op, initial, (left_ops, right_ops, charge, factor))
    return sigma
```

```python
import functools

import jax
import jax.numpy as jnp
from jax import lax
from jax.experimental import pallas as pl
from jax.experimental.pallas import tpu as pltpu
from jax.sharding import PartitionSpec as P

CORES = 2
EDGE = 2


def padded(cells, sides, width):
    for axis, dim in sides:
        count = lax.axis_size(axis)
        head = lax.slice_in_dim(cells, 0, width, axis=dim)
        tail = lax.slice_in_dim(cells, cells.shape[dim] - width, cells.shape[dim], axis=dim)
        cells = jnp.concatenate(
            [
                lax.ppermute(tail, axis, [(i, (i + 1) % count) for i in range(count)]),
                cells,
                lax.ppermute(head, axis, [((i + 1) % count, i) for i in range(count)]),
            ],
            axis=dim,
        )
    return cells


def batched(left_op, sources, right_op, factor_values):
    middle = jnp.einsum("ij,sjk->sik", left_op, sources, preferred_element_type=jnp.float32).astype(
        jnp.bfloat16
    )
    contribution = jnp.einsum("sik,lk->sil", middle, right_op, preferred_element_type=jnp.float32)
    return contribution * factor_values[:, None, None]


def plain_shards(wavefunction, left_ops, right_ops, charge, couple, amplitude):
    factor = amplitude * couple.astype(jnp.float32)
    sectors = wavefunction.shape[0]
    states = wavefunction.shape[1]
    extended = padded(wavefunction, (("sec", 0),), 1)

    def accumulate(accumulated, operands):
        left_op, right_op, sector_shift, factor_row = operands
        start = 1 - sector_shift
        sources = lax.dynamic_slice_in_dim(extended, start, sectors, 0)
        return (accumulated + batched(left_op, sources, right_op, factor_row), None)

    initial = jnp.zeros((sectors, states, states), jnp.float32)
    accumulated, unused = lax.scan(accumulate, initial, (left_ops, right_ops, charge, factor))
    return lax.psum_scatter(accumulated, "op", scatter_dimension=1, tiled=True)


def products(groups, sources, lefts, middles, rights, first_target, targets, waits, results):
    operators, rows, states = lefts.shape
    half = rows // CORES
    per_group = operators // len(groups)
    for k in range(operators):
        charge, couple, amplitude = groups[k // per_group]
        own = k % per_group
        waits(k)
        shift = 1 - charge[own]
        wide = jnp.concatenate([sources[shift + t] for t in range(targets)], axis=1)
        middle = jnp.dot(lefts[k], wide, preferred_element_type=jnp.float32)
        for t in range(targets):
            at = first_target + t
            factor = amplitude[own, at] * couple[own, at].astype(jnp.float32)
            block = middle[:, t * states : (t + 1) * states].astype(jnp.bfloat16)
            block = (block.astype(jnp.float32) * factor).astype(jnp.bfloat16)
            for core in range(CORES):
                row = (core * targets + t) * half
                middles[row : row + half, k * states : (k + 1) * states] = block[
                    core * half : (core + 1) * half
                ]
    waits(operators)
    right = jnp.concatenate([rights[k] for k in range(operators)], axis=1)
    width = targets * half
    step = 256
    for low in range(0, CORES * width, step):
        high = min(low + step, CORES * width)
        total = lax.dot_general(
            right, middles[low:high, :], (((1,), (1,)), ((), ())), preferred_element_type=jnp.float32
        ).T
        for core in range(CORES):
            begin, end = max(low, core * width), min(high, (core + 1) * width)
            if begin < end:
                results[core][begin - core * width : end - core * width, :] = total[
                    begin - low : end - low, :
                ].astype(results[core].dtype)


def position():
    place = lax.axis_index("op")
    return place // CORES, place % CORES


def row_of(chip, core, half):
    return pl.multiple_of((chip * CORES + core) * half, 16)


def inner_kernel(
    remote, charge, couple, amplitude, left, right, cells, keep, send, lefts, rights, sources, middles,
    cell_sem, left_sem, right_sem,
):
    chip, core = position()
    chip = 1 - chip if remote else chip
    operators, rows, states = lefts.shape
    half = rows // CORES
    slabs = sources.shape[0]
    targets = slabs - 2
    first = EDGE - 1
    cell_copy = pltpu.make_async_copy(cells.at[pl.ds(first, slabs)], sources, cell_sem)
    cell_copy.start()
    left_copies = []
    right_copies = []
    for k in range(operators):
        for part, owner in enumerate((core, 1 - core)):
            copy = pltpu.make_async_copy(
                left.at[k, pl.ds(row_of(chip, owner, half), half)],
                lefts.at[k, pl.ds(part * half, half)],
                left_sem.at[k, part],
            )
            copy.start()
            left_copies.append(copy)
    for k in range(operators):
        copy = pltpu.make_async_copy(right.at[k], rights.at[k], right_sem.at[k])
        copy.start()
        right_copies.append(copy)

    def waits(k):
        if k == 0:
            cell_copy.wait()
            for copy in left_copies[: 2 * CORES]:
                copy.wait()
        elif k == 2:
            for copy in left_copies[2 * CORES :]:
                copy.wait()
        elif k == operators:
            for copy in right_copies:
                copy.wait()

    products(
        [(charge, couple, amplitude)], sources, lefts, middles, rights, EDGE, targets, waits, (keep, send)
    )


def edge_kernel(
    remote, charge, couple, amplitude, charge_in, couple_in, amplitude_in, left, right, left_in, right_in,
    cells, low_halo, high_halo, keep, send, lefts, rights, sources, middles,
    cell_sem, left_sem, right_sem,
):
    chip, core = position()
    chip = 1 - chip if remote else chip
    operators, rows, states = lefts.shape
    half = rows // CORES
    sectors = cells.shape[0]
    inside = EDGE + 1
    cell_copy = pltpu.make_async_copy(
        cells.at[pl.ds((sectors - inside) * core, inside)], sources.at[pl.ds(1 - core, inside)], cell_sem.at[0]
    )
    cell_copy.start()

    @pl.when(core == 0)
    def low():
        pltpu.make_async_copy(low_halo.at[0], sources.at[0], cell_sem.at[1]).start()

    @pl.when(core != 0)
    def high():
        pltpu.make_async_copy(high_halo.at[0], sources.at[inside], cell_sem.at[1]).start()

    left_copies = []
    right_copies = []
    per_group = operators // CORES
    for k in range(operators):
        origin = left if k < per_group else left_in
        for part, owner in enumerate((core, 1 - core)):
            copy = pltpu.make_async_copy(
                origin.at[k % per_group, pl.ds(row_of(chip, owner, half), half)],
                lefts.at[k, pl.ds(part * half, half)],
                left_sem.at[k, part],
            )
            copy.start()
            left_copies.append(copy)
    for k in range(operators):
        origin = right if k < per_group else right_in
        copy = pltpu.make_async_copy(origin.at[k % per_group], rights.at[k], right_sem.at[k])
        copy.start()
        right_copies.append(copy)

    def waits(k):
        if k == 0:
            cell_copy.wait()
            pltpu.make_async_copy(low_halo.at[0], sources.at[0], cell_sem.at[1]).wait()
            for copy in left_copies[: 2 * CORES]:
                copy.wait()
        elif k == 2:
            for copy in left_copies[2 * CORES :]:
                copy.wait()
        elif k == operators:
            for copy in right_copies:
                copy.wait()

    products(
        [(charge, couple, amplitude), (charge_in, couple_in, amplitude_in)],
        sources, lefts, middles, rights, (sectors - EDGE) * core, EDGE, waits, (keep, send),
    )


def sum_kernel(inner_own, inner_chip, inner_far, near_own, near_far, other_chip, other_far, sigma):
    core = lax.axis_index("op") % CORES
    sectors = sigma.shape[0]
    far = sectors - EDGE
    sigma[EDGE:far] = inner_own[...] + inner_chip[...] + inner_far[...].astype(jnp.float32)
    sigma[pl.ds(far * core, EDGE)] = near_own[...] + near_far[...].astype(jnp.float32)
    sigma[pl.ds(far * (1 - core), EDGE)] = other_chip[...] + other_far[...].astype(jnp.float32)


SMALL = pl.BlockSpec(memory_space=pltpu.SMEM)
LARGE = pl.BlockSpec(memory_space=pl.ANY)
BLOCK = pl.BlockSpec(memory_space=pltpu.VMEM)


def call(kernel, name, small, large, operators, slabs, targets, half, states, dtypes, cell_sems):
    rows = CORES * half
    flops = operators * targets * rows * states * states * 4
    results = [jax.ShapeDtypeStruct((targets * half, states), dtype) for dtype in dtypes]
    outs = pl.pallas_call(
        kernel,
        out_shape=results,
        in_specs=[SMALL] * len(small) + [LARGE] * len(large),
        out_specs=[BLOCK] * len(results),
        scratch_shapes=[
            pltpu.VMEM((operators, rows, states), jnp.bfloat16),
            pltpu.VMEM((operators, states, states), jnp.bfloat16),
            pltpu.VMEM((slabs, states, states), jnp.bfloat16),
            pltpu.VMEM((targets * rows, operators * states), jnp.bfloat16),
            pltpu.SemaphoreType.DMA(cell_sems),
            pltpu.SemaphoreType.DMA((operators, CORES)),
            pltpu.SemaphoreType.DMA((operators,)),
        ],
        compiler_params=pltpu.CompilerParams(vmem_limit_bytes=40 * 1024 * 1024),
        cost_estimate=pl.CostEstimate(flops=flops, bytes_accessed=operators * states * states * 4, transcendentals=0),
        name=name,
    )(*small, *large)
    return [out.reshape(targets, half, states) for out in outs]


def shards(wavefunction, left_ops, right_ops, charge, couple, amplitude):
    sec = lax.axis_size("sec")
    op = lax.axis_size("op")
    sectors, states = wavefunction.shape[:2]
    operators = left_ops.shape[0]
    half = states // op
    inner = sectors - 2 * EDGE

    across = [(i, i ^ 1) for i in range(op)]
    far = [(i, i ^ CORES) for i in range(op)]
    far_across = [(i, i ^ (CORES + 1)) for i in range(op)]

    def chip_mate(value):
        return lax.ppermute(value, "op", across)

    up = [
        (s * op + o, ((s + 1) % sec) * op + o) for s in range(sec) for o in range(op) if o % CORES == 0
    ]
    down = [
        (s * op + o, ((s - 1) % sec) * op + o) for s in range(sec) for o in range(op) if o % CORES != 0
    ]
    low_halo = lax.ppermute(wavefunction[sectors - 1 :], ("sec", "op"), up)
    high_halo = lax.ppermute(wavefunction[:1], ("sec", "op"), down)
    left_in = chip_mate(left_ops)
    right_in = chip_mate(right_ops)
    small = (charge, couple, amplitude)
    small_in = tuple(chip_mate(value) for value in small)

    def inner_part(remote, name):
        return call(
            functools.partial(inner_kernel, remote), name, small, (left_ops, right_ops, wavefunction),
            operators, inner + 2, inner, half, states, (jnp.float32, jnp.float32), (),
        )

    def edge_part(remote, name, dtype):
        return call(
            functools.partial(edge_kernel, remote), name, small + small_in,
            (left_ops, right_ops, left_in, right_in, wavefunction, low_halo, high_halo),
            CORES * operators, EDGE + 2, EDGE, half, states, (dtype, dtype), (2,),
        )

    inner_far_keep, inner_far_send = inner_part(True, "inner_far")
    inner_far_in = chip_mate(inner_far_send)
    inner_own, inner_send = inner_part(False, "inner_own")
    inner_chip = chip_mate(inner_send)
    inner_far = lax.ppermute((inner_far_keep + inner_far_in).astype(jnp.bfloat16), "op", far)
    near_send, other_send = edge_part(True, "edge_far", jnp.bfloat16)
    near_far = lax.ppermute(near_send, "op", far)
    other_far = lax.ppermute(other_send, "op", far_across)
    near_own, near_mate = edge_part(False, "edge_own", jnp.float32)
    other_chip = chip_mate(near_mate)
    return pl.pallas_call(
        sum_kernel,
        out_shape=jax.ShapeDtypeStruct((sectors, half, states), jnp.float32),
        in_specs=[BLOCK] * 7,
        out_specs=BLOCK,
        compiler_params=pltpu.CompilerParams(vmem_limit_bytes=16 * 1024 * 1024),
        name="total",
    )(inner_own, inner_chip, inner_far, near_own, near_far, other_chip, other_far)


def solution(mesh):
    placed = (
        P("sec", None, None),
        P("op", None, None),
        P("op", None, None),
        P("op"),
        P("op", "sec"),
        P("op", "sec"),
    )
    body = shards if mesh.shape["op"] == CORES * CORES else plain_shards
    return jax.shard_map(
        body, mesh=mesh, in_specs=placed, out_specs=P("sec", "op", None), check_vma=False
    )
```

```python
import jax
import jax.numpy as jnp
from jax import lax
from jax.experimental import pallas as pl
from jax.experimental.pallas import tpu as pltpu
from jax.sharding import PartitionSpec as P


CORES = 2
EDGE = 2


def padded(cells, sides, width):
    for axis, dim in sides:
        count = lax.axis_size(axis)
        head = lax.slice_in_dim(cells, 0, width, axis=dim)
        tail = lax.slice_in_dim(cells, cells.shape[dim] - width, cells.shape[dim], axis=dim)
        cells = jnp.concatenate(
            [
                lax.ppermute(tail, axis, [(i, (i + 1) % count) for i in range(count)]),
                cells,
                lax.ppermute(head, axis, [((i + 1) % count, i) for i in range(count)]),
            ],
            axis=dim,
        )
    return cells


def batched(left_op, sources, right_op, factor_values):
    middle = jnp.einsum("ij,sjk->sik", left_op, sources, preferred_element_type=jnp.float32).astype(
        jnp.bfloat16
    )
    contribution = jnp.einsum("sik,lk->sil", middle, right_op, preferred_element_type=jnp.float32)
    return contribution * factor_values[:, None, None]


def plain_shards(wavefunction, left_ops, right_ops, charge, couple, amplitude):
    factor = amplitude * couple.astype(jnp.float32)
    sectors = wavefunction.shape[0]
    states = wavefunction.shape[1]
    extended = padded(wavefunction, (("sec", 0),), 1)

    def accumulate(accumulated, operands):
        left_op, right_op, sector_shift, factor_row = operands
        start = 1 - sector_shift
        sources = lax.dynamic_slice_in_dim(extended, start, sectors, 0)
        return (accumulated + batched(left_op, sources, right_op, factor_row), None)

    initial = jnp.zeros((sectors, states, states), jnp.float32)
    accumulated, _ = lax.scan(accumulate, initial, (left_ops, right_ops, charge, factor))
    return lax.psum_scatter(accumulated, "op", scatter_dimension=1, tiled=True)


def middle_of(k, factors, own, left, sources, middles, first_target, targets, chip, core):
    states = sources.shape[-1]
    half = middles.shape[0] // (CORES * targets)
    shift = 1 - factors[own, factors.shape[1] - 1].astype(jnp.int32)
    wide = jnp.concatenate([sources[shift + t] for t in range(targets)], axis=1)
    rows = jnp.concatenate(
        [left[own, pl.ds(row_of(chip, owner, half), half)] for owner in (core, 1 - core)], axis=0
    )
    middle = jnp.dot(rows, wide, preferred_element_type=jnp.float32)
    for t in range(targets):
        factor = factors[own, first_target + t]
        block = middle[:, t * states : (t + 1) * states].astype(jnp.bfloat16)
        block = (block.astype(jnp.float32) * factor).astype(jnp.bfloat16)
        for part in range(CORES):
            row = (part * targets + t) * half
            middles[row : row + half, k * states : (k + 1) * states] = block[part * half : (part + 1) * half]


def summed(right, middles, results):
    width = middles.shape[0] // CORES
    step = 256
    for low in range(0, CORES * width, step):
        high = min(low + step, CORES * width)
        total = lax.dot_general(
            right, middles[low:high, :], (((1,), (1,)), ((), ())), preferred_element_type=jnp.float32
        ).T
        for part in range(CORES):
            begin, end = max(low, part * width), min(high, (part + 1) * width)
            if begin < end:
                results[part][begin - part * width : end - part * width, :] = total[
                    begin - low : end - low, :
                ].astype(results[part].dtype)


def position():
    place = lax.axis_index("op")
    return place // CORES, place % CORES


def row_of(chip, core, half):
    return pl.multiple_of((chip * CORES + core) * half, 32)


def inner_far_kernel(
    charge, couple, amplitude, left_far, right_far, cells_far, keep, send, factors, left, right, cells,
    middles, charge_here, couple_here, amplitude_here, small_sem, cell_sem, left_sem, right_sem,
):
    chip, core = position()
    operators, _ = left.shape[:2]
    sectors = cells.shape[0]
    targets = sectors - 2 * EDGE
    half = keep.shape[0] // targets
    first = EDGE - 1
    slabs = targets + 2
    chip_rows = CORES * half

    def rows(k, place):
        at = pl.ds(pl.multiple_of(place * chip_rows, 64), chip_rows)
        return left_far.at[k, at], left.at[k, at]

    def begin(source, target, sem):
        copy = pltpu.make_async_copy(source, target, sem)
        copy.start()
        return copy

    small = [
        begin(charge, charge_here, small_sem.at[0]),
        begin(couple, couple_here, small_sem.at[1]),
        begin(amplitude, amplitude_here, small_sem.at[2]),
    ]
    inside = pl.ds(first, slabs)
    cell = begin(cells_far.at[inside], cells.at[inside], cell_sem.at[0])
    lefts = [begin(*rows(k, 1 - chip), left_sem.at[0, k]) for k in range(operators)]
    rights = [begin(right_far.at[k], right.at[k], right_sem.at[k]) for k in range(operators)]
    later = [begin(*rows(k, chip), left_sem.at[1, k]) for k in range(operators)]
    later.append(begin(cells_far.at[pl.ds(0, first)], cells.at[pl.ds(0, first)], cell_sem.at[1]))
    last = pl.ds(first + slabs, first)
    later.append(begin(cells_far.at[last], cells.at[last], cell_sem.at[2]))
    for copy in small:
        copy.wait()
    for k in range(operators):
        for t in range(sectors):
            factors[k, t] = amplitude_here[k, t] * couple_here[k, t].astype(jnp.float32)
        factors[k, sectors] = charge_here[k].astype(jnp.float32)
    cell.wait()
    for k in range(operators):
        if k == 0:
            for copy in lefts[:2]:
                copy.wait()
        elif k == 2:
            for copy in lefts[2:]:
                copy.wait()
        middle_of(k, factors, k, left, cells.at[inside], middles, EDGE, targets, 1 - chip, core)
    for copy in rights:
        copy.wait()
    summed(jnp.concatenate([right[k] for k in range(operators)], axis=1), middles, (keep, send))
    for copy in later:
        copy.wait()


def inner_own_kernel(factors, left, right, cells, keep, send, middles):
    chip, core = position()
    operators = left.shape[0]
    targets = cells.shape[0] - 2 * EDGE
    inside = cells.at[pl.ds(EDGE - 1, targets + 2)]
    for k in range(operators):
        middle_of(k, factors, k, left, inside, middles, EDGE, targets, chip, core)
    summed(jnp.concatenate([right[k] for k in range(operators)], axis=1), middles, (keep, send))


def edge_products(groups, sources, middles, results, first_target, chip, core):
    k = 0
    for factors, left, right in groups:
        for own in range(left.shape[0]):
            middle_of(k, factors, own, left, sources, middles, first_target, EDGE, chip, core)
            k += 1
    wide = jnp.concatenate([right[own] for _, _, right in groups for own in range(right.shape[0])], axis=1)
    summed(wide, middles, results)


def edge_far_kernel(
    factors, factors_in, left, right, left_in, right_in, cells, halo, keep, send, sources, middles, sem
):
    chip, core = position()
    sectors = cells.shape[0]
    inside = EDGE + 1
    copies = [
        pltpu.make_async_copy(
            cells.at[pl.ds((sectors - inside) * core, inside)], sources.at[pl.ds(1 - core, inside)], sem.at[0]
        ),
        pltpu.make_async_copy(halo.at[0], sources.at[inside * core], sem.at[1]),
    ]
    for copy in copies:
        copy.start()
    for copy in copies:
        copy.wait()
    groups = ((factors, left, right), (factors_in, left_in, right_in))
    edge_products(groups, sources, middles, (keep, send), (sectors - EDGE) * core, 1 - chip, core)


def edge_own_kernel(factors, factors_in, left, right, left_in, right_in, sources, keep, send, middles):
    chip, core = position()
    sectors = factors.shape[1] - 1
    groups = ((factors, left, right), (factors_in, left_in, right_in))
    edge_products(groups, sources, middles, (keep, send), (sectors - EDGE) * core, chip, core)


def sum_kernel(inner_own, inner_chip, inner_far, near_own, near_far, other_chip, other_far, sigma):
    core = lax.axis_index("op") % CORES
    sectors = sigma.shape[0]
    far = sectors - EDGE
    sigma[EDGE:far] = inner_own[...] + inner_chip[...] + inner_far[...].astype(jnp.float32)
    sigma[pl.ds(far * core, EDGE)] = near_own[...] + near_far[...].astype(jnp.float32)
    sigma[pl.ds(far * (1 - core), EDGE)] = other_chip[...] + other_far[...].astype(jnp.float32)


SMALL = pl.BlockSpec(memory_space=pltpu.SMEM)
LARGE = pl.BlockSpec(memory_space=pl.ANY)
BLOCK = pl.BlockSpec(memory_space=pltpu.VMEM)
MIB = 1024 * 1024


def shards(wavefunction, left_ops, right_ops, charge, couple, amplitude):
    sec = lax.axis_size("sec")
    op = lax.axis_size("op")
    sectors, states = wavefunction.shape[:2]
    operators = left_ops.shape[0]
    half = states // op
    inner = sectors - 2 * EDGE
    wide, narrow = jnp.float32, jnp.bfloat16

    def shape(*dims, dtype=wide):
        return jax.ShapeDtypeStruct(dims, dtype)

    def run(kernel, ops, targets, operands, in_specs, outs, out_specs, scratch):
        return pl.pallas_call(
            kernel,
            out_shape=outs,
            in_specs=in_specs,
            out_specs=out_specs,
            scratch_shapes=[pltpu.VMEM((targets * CORES * half, ops * states), narrow)] + scratch,
            compiler_params=pltpu.CompilerParams(vmem_limit_bytes=20 * MIB),
            cost_estimate=pl.CostEstimate(
                flops=ops * targets * CORES * half * states * states * 4,
                bytes_accessed=ops * states * states * 4,
                transcendentals=0,
            ),
        )(*operands)

    def over_op(value, flip):
        return lax.ppermute(value, "op", [(i, i ^ flip) for i in range(op)])


    def per_target(value):
        return value.reshape(-1, half, states)

    core = lax.axis_index("op") & (CORES - 1)
    ring = []
    for s in range(sec):
        for o in range(op):
            ring.append((s * op + o, (s + 1 if o % CORES == 0 else s - 1) % sec * op + o))
    border = lax.dynamic_slice_in_dim(wavefunction, (sectors - 1) * (1 - core), 1, 0)
    halo = lax.ppermute(border, ("sec", "op"), ring)
    left_in = over_op(left_ops, 1)
    right_in = over_op(right_ops, 1)

    block = shape(inner * half, states)
    far_keep, far_send, factors, left, right, cells = run(
        inner_far_kernel,
        operators,
        inner,
        [
            pltpu.with_memory_space_constraint(value, pltpu.HBM)
            for value in (charge, couple, amplitude, left_ops, right_ops, wavefunction)
        ],
        [LARGE] * 6,
        [
            block,
            block,
            shape(operators, sectors + 1),
            pltpu.VMEM(left_ops.shape, narrow),
            pltpu.VMEM(right_ops.shape, narrow),
            pltpu.VMEM(wavefunction.shape, narrow),
        ],
        [BLOCK, BLOCK, SMALL, BLOCK, BLOCK, BLOCK],
        [
            pltpu.SMEM(charge.shape, charge.dtype),
            pltpu.SMEM(couple.shape, couple.dtype),
            pltpu.SMEM(amplitude.shape, amplitude.dtype),
            pltpu.SemaphoreType.DMA((3,)),
            pltpu.SemaphoreType.DMA((3,)),
            pltpu.SemaphoreType.DMA((2, operators)),
            pltpu.SemaphoreType.DMA((operators,)),
        ],
    )
    far_in = over_op(far_send, 1)
    factors_in = over_op(factors, 1)
    inner_own, inner_send = run(
        inner_own_kernel,
        operators,
        inner,
        [factors, left, right, cells],
        [SMALL, BLOCK, BLOCK, BLOCK],
        [block, block],
        [BLOCK, BLOCK],
        [],
    )
    inner_chip = over_op(inner_send, 1)
    inner_far = over_op((far_keep + far_in).astype(narrow), CORES)

    held = [factors, factors_in, left, right, left_in, right_in]
    held_specs = [SMALL, SMALL, BLOCK, BLOCK, BLOCK, BLOCK]
    edge_narrow = shape(EDGE * half, states, dtype=narrow)
    near_send, other_send, sources = run(
        edge_far_kernel,
        CORES * operators,
        EDGE,
        held + [cells, halo],
        held_specs + [BLOCK, LARGE],
        [edge_narrow, edge_narrow, shape(EDGE + 2, states, states, dtype=narrow)],
        [BLOCK, BLOCK, BLOCK],
        [pltpu.SemaphoreType.DMA((2,))],
    )
    near_far = over_op(near_send, CORES)
    other_far = over_op(other_send, CORES + 1)
    edge_wide = shape(EDGE * half, states)
    near_own, near_mate = run(
        edge_own_kernel,
        CORES * operators,
        EDGE,
        held + [sources],
        held_specs + [BLOCK],
        [edge_wide, edge_wide],
        [BLOCK, BLOCK],
        [],
    )
    other_chip = over_op(near_mate, 1)
    parts = (inner_own, inner_chip, inner_far, near_own, near_far, other_chip, other_far)
    return pl.pallas_call(
        sum_kernel,
        out_shape=shape(sectors, half, states),
        in_specs=[BLOCK] * len(parts),
        out_specs=BLOCK,
        compiler_params=pltpu.CompilerParams(vmem_limit_bytes=16 * MIB),
        name="total",
    )(*[per_target(part) for part in parts])


def solution(mesh):
    placed = (
        P("sec", None, None),
        P("op", None, None),
        P("op", None, None),
        P("op"),
        P("op", "sec"),
        P("op", "sec"),
    )
    two_chips = mesh.shape["op"] == CORES * CORES
    return jax.shard_map(
        shards if two_chips else plain_shards,
        mesh=mesh, in_specs=placed, out_specs=P("sec", "op", None), check_vma=False,
    )
```

```python
import jax
import jax.numpy as jnp
from jax import lax
from jax.experimental import pallas as pl
from jax.experimental.pallas import tpu as pltpu
from jax.sharding import PartitionSpec as P


CORES = 2
AHEAD = 2
LANES = 128
EDGE = 2


def padded(cells, sides, width):
    for axis, dim in sides:
        count = lax.axis_size(axis)
        head = lax.slice_in_dim(cells, 0, width, axis=dim)
        tail = lax.slice_in_dim(cells, cells.shape[dim] - width, cells.shape[dim], axis=dim)
        cells = jnp.concatenate(
            [
                lax.ppermute(tail, axis, [(i, (i + 1) % count) for i in range(count)]),
                cells,
                lax.ppermute(head, axis, [((i + 1) % count, i) for i in range(count)]),
            ],
            axis=dim,
        )
    return cells


def batched(left_op, sources, right_op, factor_values):
    middle = jnp.einsum("ij,sjk->sik", left_op, sources, preferred_element_type=jnp.float32).astype(
        jnp.bfloat16
    )
    contribution = jnp.einsum("sik,lk->sil", middle, right_op, preferred_element_type=jnp.float32)
    return contribution * factor_values[:, None, None]


def plain_shards(wavefunction, left_ops, right_ops, charge, couple, amplitude):
    factor = amplitude * couple.astype(jnp.float32)
    sectors = wavefunction.shape[0]
    states = wavefunction.shape[1]
    extended = padded(wavefunction, (("sec", 0),), 1)

    def accumulate(accumulated, operands):
        left_op, right_op, sector_shift, factor_row = operands
        start = 1 - sector_shift
        sources = lax.dynamic_slice_in_dim(extended, start, sectors, 0)
        return (accumulated + batched(left_op, sources, right_op, factor_row), None)

    initial = jnp.zeros((sectors, states, states), jnp.float32)
    accumulated, _ = lax.scan(accumulate, initial, (left_ops, right_ops, charge, factor))
    return lax.psum_scatter(accumulated, "op", scatter_dimension=1, tiled=True)


def middle_of(k, factors, own, left, sources, middles, sectors, first_target, targets, chip, core):
    states = sources.shape[-1]
    half = middles.shape[0] // (CORES * targets)
    shift = 1 - factors[own, sectors].astype(jnp.int32)
    wide = jnp.concatenate([sources[shift + t] for t in range(targets)], axis=1)
    rows = jnp.concatenate(
        [left[own, pl.ds(row_of(chip, owner, half), half)] for owner in (core, 1 - core)], axis=0
    )
    middle = jnp.dot(rows, wide, preferred_element_type=jnp.float32)
    for t in range(targets):
        factor = factors[own, first_target + t]
        block = middle[:, t * states : (t + 1) * states].astype(jnp.bfloat16)
        block = (block.astype(jnp.float32) * factor).astype(jnp.bfloat16)
        for part in range(CORES):
            row = (part * targets + t) * half
            middles[row : row + half, k * states : (k + 1) * states] = block[part * half : (part + 1) * half]


def summed(right, middles, results):
    width = middles.shape[0] // CORES
    step = 256
    for low in range(0, CORES * width, step):
        high = min(low + step, CORES * width)
        total = lax.dot_general(
            right, middles[low:high, :], (((1,), (1,)), ((), ())), preferred_element_type=jnp.float32
        ).T
        for part in range(CORES):
            begin, end = max(low, part * width), min(high, (part + 1) * width)
            if begin < end:
                results[part][begin - part * width : end - part * width, :] = total[
                    begin - low : end - low, :
                ].astype(results[part].dtype)


def position():
    place = lax.axis_index("op")
    return lax.shift_right_logical(place, CORES - 1), place & (CORES - 1)


def row_of(chip, core, half):
    return pl.multiple_of((chip * CORES + core) * half, 32)


def inner_far_kernel(
    charge, couple, amplitude, left_far, right_far, cells_far,
    keep, send, factors, left, right, cells, border,
    middles, charge_here, couple_here, amplitude_here, small_sem, cell_sem, left_sem, right_sem,
):
    chip, core = position()
    operators, states = left.shape[:2]
    sectors = cells.shape[0]
    targets = sectors - 2 * EDGE
    half = keep.shape[0] // targets
    first = EDGE - 1
    slabs = targets + 2
    chip_rows = CORES * half

    def rows(k, place):
        at = pl.ds(pl.multiple_of(place * chip_rows, 64), chip_rows)
        return left_far.at[k, at], left.at[k, at]

    def begin(source, target, sem):
        copy = pltpu.make_async_copy(source, target, sem)
        copy.start()
        return copy

    small = [
        begin(charge, charge_here, small_sem.at[0]),
        begin(couple, couple_here, small_sem.at[1]),
        begin(amplitude, amplitude_here, small_sem.at[2]),
    ]
    inside = pl.ds(first, slabs)
    cell = begin(cells_far.at[inside], cells.at[inside], cell_sem.at[0])
    lefts = [begin(*rows(k, 1 - chip), left_sem.at[0, k]) for k in range(AHEAD)]
    for copy in small:
        copy.wait()
    lefts += [begin(*rows(k, 1 - chip), left_sem.at[0, k]) for k in range(AHEAD, operators)]
    row = lax.broadcasted_iota(jnp.int32, (operators, LANES), 0)
    column = lax.broadcasted_iota(jnp.int32, (operators, LANES), 1)
    table = jnp.zeros((operators, LANES), jnp.float32)
    for k in range(operators):
        for t in range(sectors + 1):
            if t < sectors:
                entry = amplitude_here[k, t] * couple_here[k, t].astype(jnp.float32)
            else:
                entry = charge_here[k].astype(jnp.float32)
            factors[k, t] = entry
            table = jnp.where((row == k) & (column == t), entry, table)
    width = keep.shape[0]
    send[width:, :] = jnp.concatenate(
        [table, jnp.zeros((operators, states - LANES), jnp.float32)], axis=1
    )
    cell.wait()
    for copy in lefts[:AHEAD]:
        copy.wait()
    rights = [begin(right_far.at[k], right.at[k], right_sem.at[k]) for k in range(operators)]
    later = [begin(*rows(k, chip), left_sem.at[1, k]) for k in range(operators)]
    later.append(begin(cells_far.at[pl.ds(0, first)], cells.at[pl.ds(0, first)], cell_sem.at[1]))
    last = pl.ds(first + slabs, first)
    later.append(begin(cells_far.at[last], cells.at[last], cell_sem.at[2]))
    later.append(begin(cells_far.at[(sectors - 1) * (1 - core)], border.at[0], cell_sem.at[3]))
    for k in range(operators):
        if k == AHEAD:
            for copy in lefts[AHEAD:]:
                copy.wait()
        middle_of(k, factors, k, left, cells.at[inside], middles, sectors, EDGE, targets, 1 - chip, core)
    for copy in rights:
        copy.wait()
    summed(jnp.concatenate([right[k] for k in range(operators)], axis=1), middles, (keep, send))
    for copy in later:
        copy.wait()


def inner_own_kernel(factors, left, right, cells, keep, send, middles):
    chip, core = position()
    operators = left.shape[0]
    targets = cells.shape[0] - 2 * EDGE
    inside = cells.at[pl.ds(EDGE - 1, targets + 2)]
    for k in range(operators):
        middle_of(k, factors, k, left, inside, middles, cells.shape[0], EDGE, targets, chip, core)
    summed(jnp.concatenate([right[k] for k in range(operators)], axis=1), middles, (keep, send))


def edge_products(groups, sources, middles, results, sectors, chip, core):
    k = 0
    first_target = (sectors - EDGE) * core
    for factors, left, right in groups:
        for own in range(left.shape[0]):
            middle_of(k, factors, own, left, sources, middles, sectors, first_target, EDGE, chip, core)
            k += 1
    wide = jnp.concatenate([right[own] for _, _, right in groups for own in range(right.shape[0])], axis=1)
    summed(wide, middles, results)


def table_copy(mate, factors_in, sem):
    operators = factors_in.shape[0]
    place = mate.at[pl.ds(mate.shape[0] - operators, operators), pl.ds(0, LANES)]
    return pltpu.make_async_copy(place, factors_in, sem)


def edge_far_kernel(
    factors, mate, left, right, left_in, right_in, cells, halo, send, sources, middles, factors_in, sem
):
    chip, core = position()
    sectors = cells.shape[0]
    inside = EDGE + 1
    copies = [
        pltpu.make_async_copy(
            cells.at[pl.ds((sectors - inside) * core, inside)], sources.at[pl.ds(1 - core, inside)], sem.at[0]
        ),
        pltpu.make_async_copy(halo.at[0], sources.at[inside * core], sem.at[1]),
        table_copy(mate, factors_in, sem.at[2]),
    ]
    for copy in copies:
        copy.start()
    for copy in copies:
        copy.wait()
    groups = ((factors, left, right), (factors_in, left_in, right_in))
    width = send.shape[0] // CORES
    halves = [send.at[pl.ds(part * width, width)] for part in range(CORES)]
    edge_products(groups, sources, middles, halves, sectors, 1 - chip, core)


def edge_own_kernel(
    factors, mate, left, right, left_in, right_in, sources, keep, send, middles, factors_in, sem
):
    chip, core = position()
    sectors = factors.shape[1] - 1
    copy = table_copy(mate, factors_in, sem)
    copy.start()
    copy.wait()
    groups = ((factors, left, right), (factors_in, left_in, right_in))
    edge_products(groups, sources, middles, (keep, send), sectors, chip, core)


def sum_kernel(inner_own, inner_chip, inner_far, near_own, edge_far, other, sigma):
    core = lax.axis_index("op") & (CORES - 1)
    sectors = sigma.shape[0]
    far = sectors - EDGE
    sigma[EDGE:far] = inner_own[...] + inner_chip[...] + inner_far[...].astype(jnp.float32)
    sigma[pl.ds(far * core, EDGE)] = near_own[...] + edge_far[:EDGE].astype(jnp.float32)
    sigma[pl.ds(far * (1 - core), EDGE)] = other[...]


SMALL = pl.BlockSpec(memory_space=pltpu.SMEM)
LARGE = pl.BlockSpec(memory_space=pl.ANY)
BLOCK = pl.BlockSpec(memory_space=pltpu.VMEM)
MIB = 1024 * 1024


def shards(wavefunction, left_ops, right_ops, charge, couple, amplitude):
    sec = lax.axis_size("sec")
    op = lax.axis_size("op")
    sectors, states = wavefunction.shape[:2]
    operators = left_ops.shape[0]
    half = states // op
    inner = sectors - 2 * EDGE
    wide, narrow = jnp.float32, jnp.bfloat16

    def shape(*dims, dtype=wide):
        return jax.ShapeDtypeStruct(dims, dtype)

    def run(kernel, ops, targets, operands, in_specs, outs, out_specs, scratch):
        return pl.pallas_call(
            kernel,
            out_shape=outs,
            in_specs=in_specs,
            out_specs=out_specs,
            scratch_shapes=[pltpu.VMEM((targets * CORES * half, ops * states), narrow)] + scratch,
            compiler_params=pltpu.CompilerParams(vmem_limit_bytes=20 * MIB),
            cost_estimate=pl.CostEstimate(
                flops=ops * targets * CORES * half * states * states * 4,
                bytes_accessed=ops * states * states * 4,
                transcendentals=0,
            ),
        )(*operands)

    def over_op(value, flip):
        return lax.ppermute(value, "op", [(i, i ^ flip) for i in range(op)])


    def per_target(value):
        return value.reshape(-1, half, states)

    ring = []
    for s in range(sec):
        for o in range(op):
            ring.append((s * op + o, (s + 1 if o % CORES == 0 else s - 1) % sec * op + o))
    left_in = over_op(left_ops, 1)
    right_in = over_op(right_ops, 1)

    block = shape(inner * half, states)
    block_and_table = shape(inner * half + operators, states)
    far_keep, far_send, factors, left, right, cells, border = run(
        inner_far_kernel,
        operators,
        inner,
        [
            pltpu.with_memory_space_constraint(value, pltpu.HBM)
            for value in (charge, couple, amplitude, left_ops, right_ops, wavefunction)
        ],
        [LARGE] * 6,
        [
            block,
            block_and_table,
            shape(operators, sectors + 1),
            pltpu.VMEM(left_ops.shape, narrow),
            pltpu.VMEM(right_ops.shape, narrow),
            pltpu.VMEM(wavefunction.shape, narrow),
            pltpu.VMEM((1, states, states), narrow),
        ],
        [BLOCK, BLOCK, SMALL, BLOCK, BLOCK, BLOCK, BLOCK],
        [
            pltpu.SMEM(charge.shape, charge.dtype),
            pltpu.SMEM(couple.shape, couple.dtype),
            pltpu.SMEM(amplitude.shape, amplitude.dtype),
            pltpu.SemaphoreType.DMA((3,)),
            pltpu.SemaphoreType.DMA((4,)),
            pltpu.SemaphoreType.DMA((2, operators)),
            pltpu.SemaphoreType.DMA((operators,)),
        ],
    )
    far_in = over_op(far_send, 1)
    halo = lax.ppermute(border, ("sec", "op"), ring)
    inner_own, inner_send = run(
        inner_own_kernel,
        operators,
        inner,
        [factors, left, right, cells],
        [SMALL, BLOCK, BLOCK, BLOCK],
        [block, block],
        [BLOCK, BLOCK],
        [],
    )
    inner_chip = over_op(inner_send, 1)
    inner_far = over_op((far_keep + far_in[: inner * half]).astype(narrow), CORES)

    held = [factors, far_in, left, right, left_in, right_in]
    held_specs = [SMALL, BLOCK, BLOCK, BLOCK, BLOCK, BLOCK]
    table = pltpu.SMEM((operators, LANES), wide)
    edge_send, sources = run(
        edge_far_kernel,
        CORES * operators,
        EDGE,
        held + [cells, halo],
        held_specs + [BLOCK, BLOCK],
        [shape(CORES * EDGE * half, states, dtype=narrow), shape(EDGE + 2, states, states, dtype=narrow)],
        [BLOCK, BLOCK],
        [table, pltpu.SemaphoreType.DMA((3,))],
    )
    edge_far = over_op(edge_send, CORES)
    edge_wide = shape(EDGE * half, states)
    near_own, near_mate = run(
        edge_own_kernel,
        CORES * operators,
        EDGE,
        held + [sources],
        held_specs + [BLOCK],
        [edge_wide, edge_wide],
        [BLOCK, BLOCK],
        [table, pltpu.SemaphoreType.DMA],
    )
    other = over_op(near_mate + edge_far[EDGE * half :].astype(wide), 1)
    parts = (inner_own, inner_chip, inner_far, near_own, edge_far, other)
    return pl.pallas_call(
        sum_kernel,
        out_shape=shape(sectors, half, states),
        in_specs=[BLOCK] * len(parts),
        out_specs=BLOCK,
        compiler_params=pltpu.CompilerParams(vmem_limit_bytes=16 * MIB),
        name="total",
    )(*[per_target(part) for part in parts])


def solution(mesh):
    placed = (
        P("sec", None, None),
        P("op", None, None),
        P("op", None, None),
        P("op"),
        P("op", "sec"),
        P("op", "sec"),
    )
    two_chips = mesh.shape["op"] == CORES * CORES
    return jax.shard_map(
        shards if two_chips else plain_shards,
        mesh=mesh, in_specs=placed, out_specs=P("sec", "op", None), check_vma=False,
    )
```

```python
import jax
import jax.numpy as jnp
from jax import lax
from jax.experimental import pallas as pl
from jax.experimental.pallas import tpu as pltpu
from jax.sharding import PartitionSpec as P


CORES = 2
AHEAD = 2
EDGE = 2


def padded(cells, sides, width):
    for axis, dim in sides:
        count = lax.axis_size(axis)
        head = lax.slice_in_dim(cells, 0, width, axis=dim)
        tail = lax.slice_in_dim(cells, cells.shape[dim] - width, cells.shape[dim], axis=dim)
        cells = jnp.concatenate(
            [
                lax.ppermute(tail, axis, [(i, (i + 1) % count) for i in range(count)]),
                cells,
                lax.ppermute(head, axis, [((i + 1) % count, i) for i in range(count)]),
            ],
            axis=dim,
        )
    return cells


def batched(left_op, sources, right_op, factor_values):
    middle = jnp.einsum("ij,sjk->sik", left_op, sources, preferred_element_type=jnp.float32).astype(
        jnp.bfloat16
    )
    contribution = jnp.einsum("sik,lk->sil", middle, right_op, preferred_element_type=jnp.float32)
    return contribution * factor_values[:, None, None]


def plain_shards(wavefunction, left_ops, right_ops, charge, couple, amplitude):
    factor = amplitude * couple.astype(jnp.float32)
    sectors = wavefunction.shape[0]
    states = wavefunction.shape[1]
    extended = padded(wavefunction, (("sec", 0),), 1)

    def accumulate(accumulated, operands):
        left_op, right_op, sector_shift, factor_row = operands
        start = 1 - sector_shift
        sources = lax.dynamic_slice_in_dim(extended, start, sectors, 0)
        return (accumulated + batched(left_op, sources, right_op, factor_row), None)

    initial = jnp.zeros((sectors, states, states), jnp.float32)
    accumulated, _ = lax.scan(accumulate, initial, (left_ops, right_ops, charge, factor))
    return lax.psum_scatter(accumulated, "op", scatter_dimension=1, tiled=True)


def middle_of(k, factors, own, left, sources, middles, sectors, first_target, targets, chip, core):
    states = sources.shape[-1]
    half = middles.shape[0] // (CORES * targets)
    shift = 1 - factors[own, sectors].astype(jnp.int32)
    wide = jnp.concatenate([sources[shift + t] for t in range(targets)], axis=1)
    rows = jnp.concatenate(
        [left[own, pl.ds(row_of(chip, owner, half), half)] for owner in (core, 1 - core)], axis=0
    )
    middle = jnp.dot(rows, wide, preferred_element_type=jnp.float32)
    for t in range(targets):
        factor = factors[own, first_target + t]
        block = middle[:, t * states : (t + 1) * states].astype(jnp.bfloat16)
        block = (block.astype(jnp.float32) * factor).astype(jnp.bfloat16)
        for part in range(CORES):
            row = (part * targets + t) * half
            middles[row : row + half, k * states : (k + 1) * states] = block[part * half : (part + 1) * half]


def summed(right, middles, results):
    width = middles.shape[0] // CORES
    step = 256
    for low in range(0, CORES * width, step):
        high = min(low + step, CORES * width)
        total = lax.dot_general(
            right, middles[low:high, :], (((1,), (1,)), ((), ())), preferred_element_type=jnp.float32
        ).T
        for part in range(CORES):
            begin, end = max(low, part * width), min(high, (part + 1) * width)
            if begin < end:
                results[part][begin - part * width : end - part * width, :] = total[
                    begin - low : end - low, :
                ].astype(results[part].dtype)


def position():
    place = lax.axis_index("op")
    return lax.shift_right_logical(place, CORES - 1), place & (CORES - 1)


def row_of(chip, core, half):
    return pl.multiple_of((chip * CORES + core) * half, 32)


def begin(source, target, sem):
    copy = pltpu.make_async_copy(source, target, sem)
    copy.start()
    return copy


def load_kernel(
    charge, couple, amplitude, cells_far, factors, cells, border,
    charge_here, couple_here, amplitude_here, small_sem, cell_sem,
):
    _, core = position()
    operators, sectors = couple.shape
    small = [
        begin(charge, charge_here, small_sem.at[0]),
        begin(couple, couple_here, small_sem.at[1]),
        begin(amplitude, amplitude_here, small_sem.at[2]),
    ]
    large = [begin(cells_far.at[(sectors - 1) * (1 - core)], border.at[0], cell_sem.at[sectors])]
    large += [begin(cells_far.at[s], cells.at[s], cell_sem.at[s]) for s in range(sectors)]
    for copy in small:
        copy.wait()
    for k in range(operators):
        for t in range(sectors):
            factors[k, t] = amplitude_here[k, t] * couple_here[k, t].astype(jnp.float32)
        factors[k, sectors] = charge_here[k].astype(jnp.float32)
    for copy in large:
        copy.wait()


def inner_far_kernel(
    factors, left_far, right_far, cells, keep, send, left, right, middles, left_sem, right_sem
):
    chip, core = position()
    operators = left.shape[0]
    sectors = cells.shape[0]
    targets = sectors - 2 * EDGE
    chip_rows = keep.shape[0] // targets * CORES

    def rows(k, place):
        at = pl.ds(pl.multiple_of(place * chip_rows, 64), chip_rows)
        return left_far.at[k, at], left.at[k, at]

    lefts = [begin(*rows(k, 1 - chip), left_sem.at[0, k]) for k in range(operators)]
    rights = [begin(right_far.at[k], right.at[k], right_sem.at[k]) for k in range(operators)]
    later = [begin(*rows(k, chip), left_sem.at[1, k]) for k in range(operators)]
    inside = cells.at[pl.ds(EDGE - 1, targets + 2)]
    for k in range(operators):
        if k == 0:
            for copy in lefts[:AHEAD]:
                copy.wait()
        if k == AHEAD:
            for copy in lefts[AHEAD:]:
                copy.wait()
        middle_of(k, factors, k, left, inside, middles, sectors, EDGE, targets, 1 - chip, core)
    for copy in rights:
        copy.wait()
    summed(jnp.concatenate([right[k] for k in range(operators)], axis=1), middles, (keep, send))
    for copy in later:
        copy.wait()


def inner_own_kernel(factors, left, right, cells, keep, send, middles):
    chip, core = position()
    operators = left.shape[0]
    targets = cells.shape[0] - 2 * EDGE
    inside = cells.at[pl.ds(EDGE - 1, targets + 2)]
    for k in range(operators):
        middle_of(k, factors, k, left, inside, middles, cells.shape[0], EDGE, targets, chip, core)
    summed(jnp.concatenate([right[k] for k in range(operators)], axis=1), middles, (keep, send))


def edge_products(groups, sources, middles, results, sectors, chip, core):
    k = 0
    first_target = (sectors - EDGE) * core
    for factors, left, right in groups:
        for own in range(left.shape[0]):
            middle_of(k, factors, own, left, sources, middles, sectors, first_target, EDGE, chip, core)
            k += 1
    wide = jnp.concatenate([right[own] for _, _, right in groups for own in range(right.shape[0])], axis=1)
    summed(wide, middles, results)


def edge_far_kernel(
    factors, factors_in, left, right, left_in, right_in, cells, halo, send, sources, middles, sem
):
    chip, core = position()
    sectors = cells.shape[0]
    inside = EDGE + 1
    copies = [
        pltpu.make_async_copy(
            cells.at[pl.ds((sectors - inside) * core, inside)], sources.at[pl.ds(1 - core, inside)], sem.at[0]
        ),
        pltpu.make_async_copy(halo.at[0], sources.at[inside * core], sem.at[1]),
    ]
    for copy in copies:
        copy.start()
    for copy in copies:
        copy.wait()
    groups = ((factors, left, right), (factors_in, left_in, right_in))
    width = send.shape[0] // CORES
    halves = [send.at[pl.ds(part * width, width)] for part in range(CORES)]
    edge_products(groups, sources, middles, halves, sectors, 1 - chip, core)


def edge_own_kernel(
    factors, factors_in, left, right, left_in, right_in, sources, keep, send, middles
):
    chip, core = position()
    sectors = factors.shape[1] - 1
    groups = ((factors, left, right), (factors_in, left_in, right_in))
    edge_products(groups, sources, middles, (keep, send), sectors, chip, core)


def sum_kernel(inner_own, inner_chip, inner_far, near_own, edge_far, other, sigma):
    core = lax.axis_index("op") & (CORES - 1)
    sectors = sigma.shape[0]
    far = sectors - EDGE
    sigma[EDGE:far] = inner_own[...] + inner_chip[...] + inner_far[...].astype(jnp.float32)
    sigma[pl.ds(far * core, EDGE)] = near_own[...] + edge_far[:EDGE].astype(jnp.float32)
    sigma[pl.ds(far * (1 - core), EDGE)] = other[...]


SMALL = pl.BlockSpec(memory_space=pltpu.SMEM)
LARGE = pl.BlockSpec(memory_space=pl.ANY)
BLOCK = pl.BlockSpec(memory_space=pltpu.VMEM)
MIB = 1024 * 1024


def shards(wavefunction, left_ops, right_ops, charge, couple, amplitude):
    sec = lax.axis_size("sec")
    op = lax.axis_size("op")
    sectors, states = wavefunction.shape[:2]
    operators = left_ops.shape[0]
    half = states // op
    inner = sectors - 2 * EDGE
    wide, narrow = jnp.float32, jnp.bfloat16

    def shape(*dims, dtype=wide):
        return jax.ShapeDtypeStruct(dims, dtype)

    def run(kernel, ops, targets, operands, in_specs, outs, out_specs, scratch):
        return pl.pallas_call(
            kernel,
            out_shape=outs,
            in_specs=in_specs,
            out_specs=out_specs,
            scratch_shapes=[pltpu.VMEM((targets * CORES * half, ops * states), narrow)] + scratch,
            compiler_params=pltpu.CompilerParams(vmem_limit_bytes=20 * MIB),
            cost_estimate=pl.CostEstimate(
                flops=ops * targets * CORES * half * states * states * 4,
                bytes_accessed=ops * states * states * 4,
                transcendentals=0,
            ),
        )(*operands)

    def over_op(value, flip):
        return lax.ppermute(value, "op", [(i, i ^ flip) for i in range(op)])


    def per_target(value):
        return value.reshape(-1, half, states)

    ring = []
    for s in range(sec):
        for o in range(op):
            ring.append((s * op + o, (s + 1 if o % CORES == 0 else s - 1) % sec * op + o))
    left_in = over_op(left_ops, 1)
    right_in = over_op(right_ops, 1)

    def in_hbm(*values):
        return [pltpu.with_memory_space_constraint(value, pltpu.HBM) for value in values]

    factors, cells, border = pl.pallas_call(
        load_kernel,
        out_shape=[
            shape(operators, sectors + 1),
            pltpu.VMEM(wavefunction.shape, narrow),
            pltpu.VMEM((1, states, states), narrow),
        ],
        in_specs=[LARGE] * 4,
        out_specs=[SMALL, BLOCK, BLOCK],
        scratch_shapes=[
            pltpu.SMEM(charge.shape, charge.dtype),
            pltpu.SMEM(couple.shape, couple.dtype),
            pltpu.SMEM(amplitude.shape, amplitude.dtype),
            pltpu.SemaphoreType.DMA((3,)),
            pltpu.SemaphoreType.DMA((sectors + 1,)),
        ],
        compiler_params=pltpu.CompilerParams(vmem_limit_bytes=4 * MIB),
        name="load_kernel",
    )(*in_hbm(charge, couple, amplitude, wavefunction))
    halo = lax.ppermute(border, ("sec", "op"), ring)
    factors_in = over_op(factors, 1)

    block = shape(inner * half, states)
    far_keep, far_send, left, right = run(
        inner_far_kernel,
        operators,
        inner,
        [factors, *in_hbm(left_ops, right_ops), cells],
        [SMALL, LARGE, LARGE, BLOCK],
        [block, block, pltpu.VMEM(left_ops.shape, narrow), pltpu.VMEM(right_ops.shape, narrow)],
        [BLOCK] * 4,
        [pltpu.SemaphoreType.DMA((2, operators)), pltpu.SemaphoreType.DMA((operators,))],
    )
    far_in = over_op(far_send, 1)

    held = [factors, factors_in, left, right, left_in, right_in]
    held_specs = [SMALL, SMALL, BLOCK, BLOCK, BLOCK, BLOCK]
    edge_send, sources = run(
        edge_far_kernel,
        CORES * operators,
        EDGE,
        held + [cells, halo],
        held_specs + [BLOCK, BLOCK],
        [shape(CORES * EDGE * half, states, dtype=narrow), shape(EDGE + 2, states, states, dtype=narrow)],
        [BLOCK, BLOCK],
        [pltpu.SemaphoreType.DMA((2,))],
    )
    edge_far = over_op(edge_send, CORES)
    inner_far = over_op((far_keep + far_in).astype(narrow), CORES)
    inner_own, inner_send = run(
        inner_own_kernel,
        operators,
        inner,
        [factors, left, right, cells],
        [SMALL, BLOCK, BLOCK, BLOCK],
        [block, block],
        [BLOCK, BLOCK],
        [],
    )
    inner_chip = over_op(inner_send, 1)
    edge_wide = shape(EDGE * half, states)
    near_own, near_mate = run(
        edge_own_kernel,
        CORES * operators,
        EDGE,
        held + [sources],
        held_specs + [BLOCK],
        [edge_wide, edge_wide],
        [BLOCK, BLOCK],
        [],
    )
    other = over_op(near_mate + edge_far[EDGE * half :].astype(wide), 1)
    parts = (inner_own, inner_chip, inner_far, near_own, edge_far, other)
    return pl.pallas_call(
        sum_kernel,
        out_shape=shape(sectors, half, states),
        in_specs=[BLOCK] * len(parts),
        out_specs=BLOCK,
        compiler_params=pltpu.CompilerParams(vmem_limit_bytes=16 * MIB),
        name="total",
    )(*[per_target(part) for part in parts])


def solution(mesh):
    placed = (
        P("sec", None, None),
        P("op", None, None),
        P("op", None, None),
        P("op"),
        P("op", "sec"),
        P("op", "sec"),
    )
    two_chips = mesh.shape["op"] == CORES * CORES
    return jax.shard_map(
        shards if two_chips else plain_shards,
        mesh=mesh, in_specs=placed, out_specs=P("sec", "op", None), check_vma=False,
    )
```

```python
import jax
import jax.numpy as jnp
from jax import lax
from jax.experimental import pallas as pl
from jax.experimental.pallas import tpu as pltpu
from jax.sharding import PartitionSpec as P


CORES = 2
AHEAD = 2
EDGE = 2


def padded(cells, sides, width):
    for axis, dim in sides:
        count = lax.axis_size(axis)
        head = lax.slice_in_dim(cells, 0, width, axis=dim)
        tail = lax.slice_in_dim(cells, cells.shape[dim] - width, cells.shape[dim], axis=dim)
        cells = jnp.concatenate(
            [
                lax.ppermute(tail, axis, [(i, (i + 1) % count) for i in range(count)]),
                cells,
                lax.ppermute(head, axis, [((i + 1) % count, i) for i in range(count)]),
            ],
            axis=dim,
        )
    return cells


def batched(left_op, sources, right_op, factor_values):
    middle = jnp.einsum("ij,sjk->sik", left_op, sources, preferred_element_type=jnp.float32).astype(
        jnp.bfloat16
    )
    contribution = jnp.einsum("sik,lk->sil", middle, right_op, preferred_element_type=jnp.float32)
    return contribution * factor_values[:, None, None]


def plain_shards(wavefunction, left_ops, right_ops, charge, couple, amplitude):
    factor = amplitude * couple.astype(jnp.float32)
    sectors = wavefunction.shape[0]
    states = wavefunction.shape[1]
    extended = padded(wavefunction, (("sec", 0),), 1)

    def accumulate(accumulated, operands):
        left_op, right_op, sector_shift, factor_row = operands
        start = 1 - sector_shift
        sources = lax.dynamic_slice_in_dim(extended, start, sectors, 0)
        return (accumulated + batched(left_op, sources, right_op, factor_row), None)

    initial = jnp.zeros((sectors, states, states), jnp.float32)
    accumulated, _ = lax.scan(accumulate, initial, (left_ops, right_ops, charge, factor))
    return lax.psum_scatter(accumulated, "op", scatter_dimension=1, tiled=True)


def middle_of(k, factors, own, left, sources, middles, sectors, first_target, targets, chip, core):
    states = sources.shape[-1]
    half = middles.shape[0] // (CORES * targets)
    shift = 1 - factors[own, sectors].astype(jnp.int32)
    wide = jnp.concatenate([sources[shift + t] for t in range(targets)], axis=1)
    rows = jnp.concatenate(
        [left[own, pl.ds(row_of(chip, owner, half), half)] for owner in (core, 1 - core)], axis=0
    )
    middle = jnp.dot(rows, wide, preferred_element_type=jnp.float32)
    for t in range(targets):
        factor = factors[own, first_target + t]
        block = middle[:, t * states : (t + 1) * states].astype(jnp.bfloat16)
        block = (block.astype(jnp.float32) * factor).astype(jnp.bfloat16)
        for part in range(CORES):
            row = (part * targets + t) * half
            middles[row : row + half, k * states : (k + 1) * states] = block[part * half : (part + 1) * half]


def summed(right, middles, results):
    width = middles.shape[0] // CORES
    step = 256
    for low in range(0, CORES * width, step):
        high = min(low + step, CORES * width)
        total = lax.dot_general(
            right, middles[low:high, :], (((1,), (1,)), ((), ())), preferred_element_type=jnp.float32
        ).T
        for part in range(CORES):
            begin, end = max(low, part * width), min(high, (part + 1) * width)
            if begin < end:
                results[part][begin - part * width : end - part * width, :] = total[
                    begin - low : end - low, :
                ].astype(results[part].dtype)


def position():
    place = lax.axis_index("op")
    return lax.shift_right_logical(place, CORES - 1), place & (CORES - 1)


def row_of(chip, core, half):
    return pl.multiple_of((chip * CORES + core) * half, 32)


def begin(source, target, sem):
    copy = pltpu.make_async_copy(source, target, sem)
    copy.start()
    return copy


def inner_far_kernel(
    charge, couple, amplitude, left_far, right_far, cells_far,
    keep, send, factors, left, right, cells,
    middles, charge_here, couple_here, amplitude_here, small_sem, cell_sem, left_sem, right_sem,
):
    chip, core = position()
    operators = left.shape[0]
    sectors = cells.shape[0]
    targets = sectors - 2 * EDGE
    chip_rows = keep.shape[0] // targets * CORES
    inside = range(EDGE - 1, sectors - EDGE + 1)

    def rows(k, place):
        at = pl.ds(pl.multiple_of(place * chip_rows, 64), chip_rows)
        return left_far.at[k, at], left.at[k, at]

    def cell(s):
        return begin(cells_far.at[s], cells.at[s], cell_sem.at[s])

    small = [
        begin(charge, charge_here, small_sem.at[0]),
        begin(couple, couple_here, small_sem.at[1]),
        begin(amplitude, amplitude_here, small_sem.at[2]),
    ]
    first = [cell(s) for s in inside]
    lefts = [begin(*rows(k, 1 - chip), left_sem.at[0, k]) for k in range(operators)]
    for copy in small:
        copy.wait()
    for k in range(operators):
        for t in range(sectors):
            factors[k, t] = amplitude_here[k, t] * couple_here[k, t].astype(jnp.float32)
        factors[k, sectors] = charge_here[k].astype(jnp.float32)
    for copy in first + lefts[:AHEAD]:
        copy.wait()
    rights = [begin(right_far.at[k], right.at[k], right_sem.at[k]) for k in range(operators)]
    later = [begin(*rows(k, chip), left_sem.at[1, k]) for k in range(operators)]
    later += [cell(s) for s in range(sectors) if s not in inside]
    sources = cells.at[pl.ds(EDGE - 1, targets + 2)]
    for k in range(operators):
        if k == AHEAD:
            for copy in lefts[AHEAD:]:
                copy.wait()
        middle_of(k, factors, k, left, sources, middles, sectors, EDGE, targets, 1 - chip, core)
    for copy in rights:
        copy.wait()
    summed(jnp.concatenate([right[k] for k in range(operators)], axis=1), middles, (keep, send))
    for copy in later:
        copy.wait()


def inner_own_kernel(factors, left, right, cells, keep, send, middles):
    chip, core = position()
    operators = left.shape[0]
    targets = cells.shape[0] - 2 * EDGE
    inside = cells.at[pl.ds(EDGE - 1, targets + 2)]
    for k in range(operators):
        middle_of(k, factors, k, left, inside, middles, cells.shape[0], EDGE, targets, chip, core)
    summed(jnp.concatenate([right[k] for k in range(operators)], axis=1), middles, (keep, send))


def edge_products(groups, sources, middles, results, sectors, chip, core):
    k = 0
    first_target = (sectors - EDGE) * core
    for factors, left, right in groups:
        for own in range(left.shape[0]):
            middle_of(k, factors, own, left, sources, middles, sectors, first_target, EDGE, chip, core)
            k += 1
    wide = jnp.concatenate([right[own] for _, _, right in groups for own in range(right.shape[0])], axis=1)
    summed(wide, middles, results)


def edge_far_kernel(
    factors, factors_in, left, right, left_in, right_in, cells, halo, send, sources, middles, sem
):
    chip, core = position()
    sectors = cells.shape[0]
    inside = EDGE + 1
    copies = [
        pltpu.make_async_copy(
            cells.at[pl.ds((sectors - inside) * core, inside)], sources.at[pl.ds(1 - core, inside)], sem.at[0]
        ),
        pltpu.make_async_copy(halo.at[0], sources.at[inside * core], sem.at[1]),
    ]
    for copy in copies:
        copy.start()
    for copy in copies:
        copy.wait()
    groups = ((factors, left, right), (factors_in, left_in, right_in))
    width = send.shape[0] // CORES
    halves = [send.at[pl.ds(part * width, width)] for part in range(CORES)]
    edge_products(groups, sources, middles, halves, sectors, 1 - chip, core)


def edge_own_kernel(
    factors, factors_in, left, right, left_in, right_in, sources, keep, send, middles
):
    chip, core = position()
    sectors = factors.shape[1] - 1
    groups = ((factors, left, right), (factors_in, left_in, right_in))
    edge_products(groups, sources, middles, (keep, send), sectors, chip, core)


def sum_kernel(inner_own, inner_chip, inner_far, near_own, edge_far, other, sigma):
    core = lax.axis_index("op") & (CORES - 1)
    sectors = sigma.shape[0]
    far = sectors - EDGE
    sigma[EDGE:far] = inner_own[...] + inner_chip[...] + inner_far[...].astype(jnp.float32)
    sigma[pl.ds(far * core, EDGE)] = near_own[...] + edge_far[:EDGE].astype(jnp.float32)
    sigma[pl.ds(far * (1 - core), EDGE)] = other[...]


SMALL = pl.BlockSpec(memory_space=pltpu.SMEM)
LARGE = pl.BlockSpec(memory_space=pl.ANY)
BLOCK = pl.BlockSpec(memory_space=pltpu.VMEM)
MIB = 1024 * 1024


def shards(wavefunction, left_ops, right_ops, charge, couple, amplitude):
    sec = lax.axis_size("sec")
    op = lax.axis_size("op")
    sectors, states = wavefunction.shape[:2]
    operators = left_ops.shape[0]
    half = states // op
    inner = sectors - 2 * EDGE
    wide, narrow = jnp.float32, jnp.bfloat16

    def shape(*dims, dtype=wide):
        return jax.ShapeDtypeStruct(dims, dtype)

    def run(kernel, ops, targets, operands, in_specs, outs, out_specs, scratch):
        return pl.pallas_call(
            kernel,
            out_shape=outs,
            in_specs=in_specs,
            out_specs=out_specs,
            scratch_shapes=[pltpu.VMEM((targets * CORES * half, ops * states), narrow)] + scratch,
            compiler_params=pltpu.CompilerParams(vmem_limit_bytes=20 * MIB),
            cost_estimate=pl.CostEstimate(
                flops=ops * targets * CORES * half * states * states * 4,
                bytes_accessed=ops * states * states * 4,
                transcendentals=0,
            ),
        )(*operands)

    def over_op(value, flip):
        return lax.ppermute(value, "op", [(i, i ^ flip) for i in range(op)])


    def per_target(value):
        return value.reshape(-1, half, states)

    ring = []
    for s in range(sec):
        for o in range(op):
            ring.append((s * op + o, (s + 1 if o % CORES == 0 else s - 1) % sec * op + o))
    core = lax.axis_index("op") & (CORES - 1)
    border = lax.dynamic_slice_in_dim(wavefunction, (sectors - 1) * (1 - core), 1, 0)
    halo = lax.ppermute(border, ("sec", "op"), ring)
    left_in = over_op(left_ops, 1)
    right_in = over_op(right_ops, 1)

    def in_hbm(*values):
        return [pltpu.with_memory_space_constraint(value, pltpu.HBM) for value in values]

    block = shape(inner * half, states)
    far_keep, far_send, factors, left, right, cells = run(
        inner_far_kernel,
        operators,
        inner,
        in_hbm(charge, couple, amplitude, left_ops, right_ops, wavefunction),
        [LARGE] * 6,
        [
            block,
            block,
            shape(operators, sectors + 1),
            pltpu.VMEM(left_ops.shape, narrow),
            pltpu.VMEM(right_ops.shape, narrow),
            pltpu.VMEM(wavefunction.shape, narrow),
        ],
        [BLOCK, BLOCK, SMALL, BLOCK, BLOCK, BLOCK],
        [
            pltpu.SMEM(charge.shape, charge.dtype),
            pltpu.SMEM(couple.shape, couple.dtype),
            pltpu.SMEM(amplitude.shape, amplitude.dtype),
            pltpu.SemaphoreType.DMA((3,)),
            pltpu.SemaphoreType.DMA((sectors,)),
            pltpu.SemaphoreType.DMA((2, operators)),
            pltpu.SemaphoreType.DMA((operators,)),
        ],
    )
    factors_in = over_op(factors, 1)
    far_in = over_op(far_send, 1)

    held = [factors, factors_in, left, right, left_in, right_in]
    held_specs = [SMALL, SMALL, BLOCK, BLOCK, BLOCK, BLOCK]
    edge_send, sources = run(
        edge_far_kernel,
        CORES * operators,
        EDGE,
        held + [cells, halo],
        held_specs + [BLOCK, BLOCK],
        [shape(CORES * EDGE * half, states, dtype=narrow), shape(EDGE + 2, states, states, dtype=narrow)],
        [BLOCK, BLOCK],
        [pltpu.SemaphoreType.DMA((2,))],
    )
    edge_far = over_op(edge_send, CORES)
    inner_far = over_op((far_keep + far_in).astype(narrow), CORES)
    inner_own, inner_send = run(
        inner_own_kernel,
        operators,
        inner,
        [factors, left, right, cells],
        [SMALL, BLOCK, BLOCK, BLOCK],
        [block, block],
        [BLOCK, BLOCK],
        [],
    )
    inner_chip = over_op(inner_send, 1)
    edge_wide = shape(EDGE * half, states)
    near_own, near_mate = run(
        edge_own_kernel,
        CORES * operators,
        EDGE,
        held + [sources],
        held_specs + [BLOCK],
        [edge_wide, edge_wide],
        [BLOCK, BLOCK],
        [],
    )
    other = over_op(near_mate + edge_far[EDGE * half :].astype(wide), 1)
    parts = (inner_own, inner_chip, inner_far, near_own, edge_far, other)
    return pl.pallas_call(
        sum_kernel,
        out_shape=shape(sectors, half, states),
        in_specs=[BLOCK] * len(parts),
        out_specs=BLOCK,
        compiler_params=pltpu.CompilerParams(vmem_limit_bytes=16 * MIB),
        name="total",
    )(*[per_target(part) for part in parts])


def solution(mesh):
    placed = (
        P("sec", None, None),
        P("op", None, None),
        P("op", None, None),
        P("op"),
        P("op", "sec"),
        P("op", "sec"),
    )
    two_chips = mesh.shape["op"] == CORES * CORES
    return jax.shard_map(
        shards if two_chips else plain_shards,
        mesh=mesh, in_specs=placed, out_specs=P("sec", "op", None), check_vma=False,
    )
```

```python
import jax
import jax.numpy as jnp
from jax import lax
from jax.experimental import pallas as pl
from jax.experimental.pallas import tpu as pltpu
from jax.sharding import PartitionSpec as P


CORES = 2
AHEAD = 2
EDGE = 2


def padded(cells, sides, width):
    for axis, dim in sides:
        count = lax.axis_size(axis)
        head = lax.slice_in_dim(cells, 0, width, axis=dim)
        tail = lax.slice_in_dim(cells, cells.shape[dim] - width, cells.shape[dim], axis=dim)
        cells = jnp.concatenate(
            [
                lax.ppermute(tail, axis, [(i, (i + 1) % count) for i in range(count)]),
                cells,
                lax.ppermute(head, axis, [((i + 1) % count, i) for i in range(count)]),
            ],
            axis=dim,
        )
    return cells


def batched(left_op, sources, right_op, factor_values):
    middle = jnp.einsum("ij,sjk->sik", left_op, sources, preferred_element_type=jnp.float32).astype(
        jnp.bfloat16
    )
    contribution = jnp.einsum("sik,lk->sil", middle, right_op, preferred_element_type=jnp.float32)
    return contribution * factor_values[:, None, None]


def plain_shards(wavefunction, left_ops, right_ops, charge, couple, amplitude):
    factor = amplitude * couple.astype(jnp.float32)
    sectors = wavefunction.shape[0]
    states = wavefunction.shape[1]
    extended = padded(wavefunction, (("sec", 0),), 1)

    def accumulate(accumulated, operands):
        left_op, right_op, sector_shift, factor_row = operands
        start = 1 - sector_shift
        sources = lax.dynamic_slice_in_dim(extended, start, sectors, 0)
        return (accumulated + batched(left_op, sources, right_op, factor_row), None)

    initial = jnp.zeros((sectors, states, states), jnp.float32)
    accumulated, _ = lax.scan(accumulate, initial, (left_ops, right_ops, charge, factor))
    return lax.psum_scatter(accumulated, "op", scatter_dimension=1, tiled=True)


def middle_of(k, small, own, left, sources, middles, first_target, targets, chip, core):
    charge, couple, amplitude = small
    states = sources.shape[-1]
    half = middles.shape[0] // (CORES * targets)
    shift = 1 - charge[own]
    wide = jnp.concatenate([sources[shift + t] for t in range(targets)], axis=1)
    rows = jnp.concatenate(
        [left[own, pl.ds(row_of(chip, owner, half), half)] for owner in (core, 1 - core)], axis=0
    )
    middle = jnp.dot(rows, wide, preferred_element_type=jnp.float32)
    for t in range(targets):
        at = first_target + t
        factor = amplitude[own, at] * couple[own, at].astype(jnp.float32)
        block = middle[:, t * states : (t + 1) * states].astype(jnp.bfloat16)
        block = (block.astype(jnp.float32) * factor).astype(jnp.bfloat16)
        for part in range(CORES):
            row = (part * targets + t) * half
            middles[row : row + half, k * states : (k + 1) * states] = block[part * half : (part + 1) * half]


def summed(right, middles, results):
    width = middles.shape[0] // CORES
    step = 256
    for low in range(0, CORES * width, step):
        high = min(low + step, CORES * width)
        total = lax.dot_general(
            right, middles[low:high, :], (((1,), (1,)), ((), ())), preferred_element_type=jnp.float32
        ).T
        for part in range(CORES):
            begin, end = max(low, part * width), min(high, (part + 1) * width)
            if begin < end:
                results[part][begin - part * width : end - part * width, :] = total[
                    begin - low : end - low, :
                ].astype(results[part].dtype)


def halves(results):
    width = results.shape[0] // CORES
    return [results.at[pl.ds(part * width, width)] for part in range(CORES)]


def position():
    place = lax.axis_index("op")
    return lax.shift_right_logical(place, CORES - 1), place & (CORES - 1)


def row_of(chip, core, half):
    return pl.multiple_of((chip * CORES + core) * half, 32)


def begin(source, target, sem):
    copy = pltpu.make_async_copy(source, target, sem)
    copy.start()
    return copy


def inner_far_kernel(
    charge, couple, amplitude, left_far, right_far, cells_far, send, left, right, cells, middles,
    charge_here, couple_here, amplitude_here, small_sem, cell_sem, left_sem, right_sem,
):
    chip, core = position()
    operators = left.shape[0]
    sectors = cells.shape[0]
    targets = sectors - 2 * EDGE
    chip_rows = send.shape[0] // targets
    inside = range(EDGE - 1, sectors - EDGE + 1)

    def rows(k, place):
        at = pl.ds(pl.multiple_of(place * chip_rows, 64), chip_rows)
        return left_far.at[k, at], left.at[k, at]

    def cell(s):
        return begin(cells_far.at[s], cells.at[s], cell_sem.at[s])

    small = [
        begin(charge, charge_here, small_sem.at[0]),
        begin(couple, couple_here, small_sem.at[1]),
        begin(amplitude, amplitude_here, small_sem.at[2]),
    ]
    first = [cell(s) for s in inside]
    lefts = [begin(*rows(k, 1 - chip), left_sem.at[0, k]) for k in range(operators)]
    for copy in small:
        copy.wait()
    for copy in first + lefts[:AHEAD]:
        copy.wait()
    rights = [begin(right_far.at[k], right.at[k], right_sem.at[k]) for k in range(operators)]
    later = [begin(*rows(k, chip), left_sem.at[1, k]) for k in range(operators)]
    later += [cell(s) for s in range(sectors) if s not in inside]
    sources = cells.at[pl.ds(EDGE - 1, targets + 2)]
    here = (charge_here, couple_here, amplitude_here)
    for k in range(operators):
        if k == AHEAD:
            for copy in lefts[AHEAD:]:
                copy.wait()
        middle_of(k, here, k, left, sources, middles, EDGE, targets, 1 - chip, core)
    for copy in rights:
        copy.wait()
    summed(jnp.concatenate([right[k] for k in range(operators)], axis=1), middles, halves(send))
    for copy in later:
        copy.wait()


def inner_own_kernel(charge, couple, amplitude, left, right, cells, keep, send, middles):
    chip, core = position()
    operators = left.shape[0]
    targets = cells.shape[0] - 2 * EDGE
    inside = cells.at[pl.ds(EDGE - 1, targets + 2)]
    for k in range(operators):
        middle_of(k, (charge, couple, amplitude), k, left, inside, middles, EDGE, targets, chip, core)
    summed(jnp.concatenate([right[k] for k in range(operators)], axis=1), middles, (keep, send))


def edge_products(groups, sources, middles, results, sectors, chip, core):
    k = 0
    first_target = (sectors - EDGE) * core
    for small, left, right in groups:
        for own in range(left.shape[0]):
            middle_of(k, small, own, left, sources, middles, first_target, EDGE, chip, core)
            k += 1
    wide = jnp.concatenate([right[own] for _, _, right in groups for own in range(right.shape[0])], axis=1)
    summed(wide, middles, results)


def edge_far_kernel(
    charge, couple, amplitude, charge_in, couple_in, amplitude_in, left, right, left_in, right_in,
    cells, halo, send, sources, middles, sem,
):
    chip, core = position()
    sectors = cells.shape[0]
    inside = EDGE + 1
    copies = [
        pltpu.make_async_copy(
            cells.at[pl.ds((sectors - inside) * core, inside)], sources.at[pl.ds(1 - core, inside)], sem.at[0]
        ),
        pltpu.make_async_copy(halo.at[0], sources.at[inside * core], sem.at[1]),
    ]
    for copy in copies:
        copy.start()
    for copy in copies:
        copy.wait()
    groups = (
        ((charge, couple, amplitude), left, right),
        ((charge_in, couple_in, amplitude_in), left_in, right_in),
    )
    edge_products(groups, sources, middles, halves(send), sectors, 1 - chip, core)


def edge_own_kernel(
    charge, couple, amplitude, charge_in, couple_in, amplitude_in, left, right, left_in, right_in,
    sources, keep, send, middles,
):
    chip, core = position()
    sectors = couple.shape[1]
    groups = (
        ((charge, couple, amplitude), left, right),
        ((charge_in, couple_in, amplitude_in), left_in, right_in),
    )
    edge_products(groups, sources, middles, (keep, send), sectors, chip, core)


def sum_kernel(inner_own, inner_chip, inner_far, near_own, edge_far, other, sigma):
    core = lax.axis_index("op") & (CORES - 1)
    sectors = sigma.shape[0]
    far = sectors - EDGE
    sigma[EDGE:far] = inner_own[...] + inner_chip[...] + inner_far[: far - EDGE].astype(jnp.float32)
    sigma[pl.ds(far * core, EDGE)] = near_own[...] + edge_far[:EDGE].astype(jnp.float32)
    sigma[pl.ds(far * (1 - core), EDGE)] = other[...]


SMALL = pl.BlockSpec(memory_space=pltpu.SMEM)
LARGE = pl.BlockSpec(memory_space=pl.ANY)
BLOCK = pl.BlockSpec(memory_space=pltpu.VMEM)
MIB = 1024 * 1024


def shards(wavefunction, left_ops, right_ops, charge, couple, amplitude):
    sec = lax.axis_size("sec")
    op = lax.axis_size("op")
    sectors, states = wavefunction.shape[:2]
    operators = left_ops.shape[0]
    half = states // op
    inner = sectors - 2 * EDGE
    wide, narrow = jnp.float32, jnp.bfloat16

    def shape(*dims, dtype=wide):
        return jax.ShapeDtypeStruct(dims, dtype)

    def run(kernel, ops, targets, operands, in_specs, outs, out_specs, scratch):
        return pl.pallas_call(
            kernel,
            out_shape=outs,
            in_specs=in_specs,
            out_specs=out_specs,
            scratch_shapes=[pltpu.VMEM((targets * CORES * half, ops * states), narrow)] + scratch,
            compiler_params=pltpu.CompilerParams(vmem_limit_bytes=20 * MIB),
            cost_estimate=pl.CostEstimate(
                flops=ops * targets * CORES * half * states * states * 4,
                bytes_accessed=ops * states * states * 4,
                transcendentals=0,
            ),
        )(*operands)

    def over_op(value, flip):
        return lax.ppermute(value, "op", [(i, i ^ flip) for i in range(op)])


    def per_target(value):
        return value.reshape(-1, half, states)

    ring = []
    for s in range(sec):
        for o in range(op):
            ring.append((s * op + o, (s + 1 if o % CORES == 0 else s - 1) % sec * op + o))
    core = lax.axis_index("op") & (CORES - 1)
    border = lax.dynamic_slice_in_dim(wavefunction, (sectors - 1) * (1 - core), 1, 0)
    halo = lax.ppermute(border, ("sec", "op"), ring)
    left_in = over_op(left_ops, 1)
    right_in = over_op(right_ops, 1)

    small = (charge, couple, amplitude)
    small_in = [over_op(value, 1) for value in small]

    def in_hbm(*values):
        return [pltpu.with_memory_space_constraint(value, pltpu.HBM) for value in values]

    far_send, left, right, cells = run(
        inner_far_kernel,
        operators,
        inner,
        in_hbm(*small, left_ops, right_ops, wavefunction),
        [LARGE] * 6,
        [
            shape(CORES * inner * half, states, dtype=narrow),
            pltpu.VMEM(left_ops.shape, narrow),
            pltpu.VMEM(right_ops.shape, narrow),
            pltpu.VMEM(wavefunction.shape, narrow),
        ],
        [BLOCK] * 4,
        [
            pltpu.SMEM(charge.shape, charge.dtype),
            pltpu.SMEM(couple.shape, couple.dtype),
            pltpu.SMEM(amplitude.shape, amplitude.dtype),
            pltpu.SemaphoreType.DMA((3,)),
            pltpu.SemaphoreType.DMA((sectors,)),
            pltpu.SemaphoreType.DMA((2, operators)),
            pltpu.SemaphoreType.DMA((operators,)),
        ],
    )
    inner_far = over_op(far_send, CORES)

    here = in_hbm(*small)
    held = [*here, *small_in, left, right, left_in, right_in]
    held_specs = [SMALL] * 6 + [BLOCK] * 4
    edge_send, sources = run(
        edge_far_kernel,
        CORES * operators,
        EDGE,
        held + [cells, halo],
        held_specs + [BLOCK, BLOCK],
        [shape(CORES * EDGE * half, states, dtype=narrow), shape(EDGE + 2, states, states, dtype=narrow)],
        [BLOCK, BLOCK],
        [pltpu.SemaphoreType.DMA((2,))],
    )
    edge_far = over_op(edge_send, CORES)
    block = shape(inner * half, states)
    inner_own, inner_send = run(
        inner_own_kernel,
        operators,
        inner,
        [*here, left, right, cells],
        [SMALL] * 3 + [BLOCK] * 3,
        [block, block],
        [BLOCK, BLOCK],
        [],
    )
    inner_chip = over_op(inner_send + inner_far[inner * half :].astype(wide), 1)
    edge_wide = shape(EDGE * half, states)
    near_own, near_mate = run(
        edge_own_kernel,
        CORES * operators,
        EDGE,
        held + [sources],
        held_specs + [BLOCK],
        [edge_wide, edge_wide],
        [BLOCK, BLOCK],
        [],
    )
    other = over_op(near_mate + edge_far[EDGE * half :].astype(wide), 1)
    parts = (inner_own, inner_chip, inner_far, near_own, edge_far, other)
    return pl.pallas_call(
        sum_kernel,
        out_shape=shape(sectors, half, states),
        in_specs=[BLOCK] * len(parts),
        out_specs=BLOCK,
        compiler_params=pltpu.CompilerParams(vmem_limit_bytes=16 * MIB),
        name="total",
    )(*[per_target(part) for part in parts])


def solution(mesh):
    placed = (
        P("sec", None, None),
        P("op", None, None),
        P("op", None, None),
        P("op"),
        P("op", "sec"),
        P("op", "sec"),
    )
    two_chips = mesh.shape["op"] == CORES * CORES
    return jax.shard_map(
        shards if two_chips else plain_shards,
        mesh=mesh, in_specs=placed, out_specs=P("sec", "op", None), check_vma=False,
    )
```

```python
import jax
import jax.numpy as jnp
from jax import lax
from jax.experimental import pallas as pl
from jax.experimental.pallas import tpu as pltpu
from jax.sharding import PartitionSpec as P


CORES = 2
AHEAD = 2
EDGE = 2


def padded(cells, sides, width):
    for axis, dim in sides:
        count = lax.axis_size(axis)
        head = lax.slice_in_dim(cells, 0, width, axis=dim)
        tail = lax.slice_in_dim(cells, cells.shape[dim] - width, cells.shape[dim], axis=dim)
        cells = jnp.concatenate(
            [
                lax.ppermute(tail, axis, [(i, (i + 1) % count) for i in range(count)]),
                cells,
                lax.ppermute(head, axis, [((i + 1) % count, i) for i in range(count)]),
            ],
            axis=dim,
        )
    return cells


def batched(left_op, sources, right_op, factor_values):
    middle = jnp.einsum("ij,sjk->sik", left_op, sources, preferred_element_type=jnp.float32).astype(
        jnp.bfloat16
    )
    contribution = jnp.einsum("sik,lk->sil", middle, right_op, preferred_element_type=jnp.float32)
    return contribution * factor_values[:, None, None]


def plain_shards(wavefunction, left_ops, right_ops, charge, couple, amplitude):
    factor = amplitude * couple.astype(jnp.float32)
    sectors = wavefunction.shape[0]
    states = wavefunction.shape[1]
    extended = padded(wavefunction, (("sec", 0),), 1)

    def accumulate(accumulated, operands):
        left_op, right_op, sector_shift, factor_row = operands
        start = 1 - sector_shift
        sources = lax.dynamic_slice_in_dim(extended, start, sectors, 0)
        return (accumulated + batched(left_op, sources, right_op, factor_row), None)

    initial = jnp.zeros((sectors, states, states), jnp.float32)
    accumulated, _ = lax.scan(accumulate, initial, (left_ops, right_ops, charge, factor))
    return lax.psum_scatter(accumulated, "op", scatter_dimension=1, tiled=True)


def middle_of(k, small, own, left, sources, middles, first_target, targets, chip, core):
    charge, couple, amplitude = small
    states = sources.shape[-1]
    half = middles.shape[0] // (CORES * targets)
    shift = 1 - charge[own]
    wide = jnp.concatenate([sources[shift + t] for t in range(targets)], axis=1)
    rows = jnp.concatenate(
        [left[own, pl.ds(row_of(chip, owner, half), half)] for owner in (core, 1 - core)], axis=0
    )
    middle = jnp.dot(rows, wide, preferred_element_type=jnp.float32)
    for t in range(targets):
        at = first_target + t
        factor = amplitude[own, at] * couple[own, at].astype(jnp.float32)
        block = middle[:, t * states : (t + 1) * states].astype(jnp.bfloat16)
        block = (block.astype(jnp.float32) * factor).astype(jnp.bfloat16)
        for part in range(CORES):
            row = (part * targets + t) * half
            middles[row : row + half, k * states : (k + 1) * states] = block[part * half : (part + 1) * half]


def summed(right, middles, results):
    width = middles.shape[0] // CORES
    step = 256
    for low in range(0, CORES * width, step):
        high = min(low + step, CORES * width)
        total = lax.dot_general(
            right, middles[low:high, :], (((1,), (1,)), ((), ())), preferred_element_type=jnp.float32
        ).T
        for part in range(CORES):
            begin, end = max(low, part * width), min(high, (part + 1) * width)
            if begin < end:
                results[part][begin - part * width : end - part * width, :] = total[
                    begin - low : end - low, :
                ].astype(results[part].dtype)


def halves(results):
    width = results.shape[0] // CORES
    return [results.at[pl.ds(part * width, width)] for part in range(CORES)]


def position():
    place = lax.axis_index("op")
    return lax.shift_right_logical(place, CORES - 1), place & (CORES - 1)


def row_of(chip, core, half):
    return pl.multiple_of((chip * CORES + core) * half, 32)


def begin(source, target, sem):
    copy = pltpu.make_async_copy(source, target, sem)
    copy.start()
    return copy


def inner_far_kernel(
    charge, couple, amplitude, left_far, right_far, cells_far, send, left, right, cells, middles,
    charge_here, couple_here, amplitude_here, small_sem, cell_sem, left_sem, right_sem,
):
    chip, core = position()
    operators = left.shape[0]
    sectors = cells.shape[0]
    targets = sectors - 2 * EDGE
    chip_rows = send.shape[0] // targets
    inside = range(EDGE - 1, sectors - EDGE + 1)

    def rows(k, place):
        at = pl.ds(pl.multiple_of(place * chip_rows, 64), chip_rows)
        return left_far.at[k, at], left.at[k, at]

    def cell(s):
        return begin(cells_far.at[s], cells.at[s], cell_sem.at[s])

    small = [
        begin(charge, charge_here, small_sem.at[0]),
        begin(couple, couple_here, small_sem.at[1]),
        begin(amplitude, amplitude_here, small_sem.at[2]),
    ]
    first = [cell(s) for s in inside]
    lefts = [begin(*rows(k, 1 - chip), left_sem.at[0, k]) for k in range(AHEAD)]
    for copy in small:
        copy.wait()
    lefts += [begin(*rows(k, 1 - chip), left_sem.at[0, k]) for k in range(AHEAD, operators)]
    for copy in first + lefts[:AHEAD]:
        copy.wait()
    rights = [begin(right_far.at[k], right.at[k], right_sem.at[k]) for k in range(operators)]
    later = [begin(*rows(k, chip), left_sem.at[1, k]) for k in range(operators)]
    later += [cell(s) for s in range(sectors) if s not in inside]
    sources = cells.at[pl.ds(EDGE - 1, targets + 2)]
    here = (charge_here, couple_here, amplitude_here)
    for k in range(operators):
        if k == AHEAD:
            for copy in lefts[AHEAD:]:
                copy.wait()
        middle_of(k, here, k, left, sources, middles, EDGE, targets, 1 - chip, core)
    for copy in rights:
        copy.wait()
    summed(jnp.concatenate([right[k] for k in range(operators)], axis=1), middles, halves(send))
    for copy in later:
        copy.wait()


def inner_own_kernel(charge, couple, amplitude, left, right, cells, keep, send, middles):
    chip, core = position()
    operators = left.shape[0]
    targets = cells.shape[0] - 2 * EDGE
    inside = cells.at[pl.ds(EDGE - 1, targets + 2)]
    for k in range(operators):
        middle_of(k, (charge, couple, amplitude), k, left, inside, middles, EDGE, targets, chip, core)
    summed(jnp.concatenate([right[k] for k in range(operators)], axis=1), middles, (keep, send))


def edge_products(groups, sources, middles, results, sectors, chip, core):
    k = 0
    first_target = (sectors - EDGE) * core
    for small, left, right in groups:
        for own in range(left.shape[0]):
            middle_of(k, small, own, left, sources, middles, first_target, EDGE, chip, core)
            k += 1
    wide = jnp.concatenate([right[own] for _, _, right in groups for own in range(right.shape[0])], axis=1)
    summed(wide, middles, results)


def edge_far_kernel(
    charge, couple, amplitude, charge_in, couple_in, amplitude_in, left, right, left_in, right_in,
    cells, halo, send, sources, middles, sem,
):
    chip, core = position()
    sectors = cells.shape[0]
    inside = EDGE + 1
    copies = [
        pltpu.make_async_copy(
            cells.at[pl.ds((sectors - inside) * core, inside)], sources.at[pl.ds(1 - core, inside)], sem.at[0]
        ),
        pltpu.make_async_copy(halo.at[0], sources.at[inside * core], sem.at[1]),
    ]
    for copy in copies:
        copy.start()
    for copy in copies:
        copy.wait()
    groups = (
        ((charge, couple, amplitude), left, right),
        ((charge_in, couple_in, amplitude_in), left_in, right_in),
    )
    edge_products(groups, sources, middles, halves(send), sectors, 1 - chip, core)


def edge_own_kernel(
    charge, couple, amplitude, charge_in, couple_in, amplitude_in, left, right, left_in, right_in,
    sources, keep, send, middles,
):
    chip, core = position()
    sectors = couple.shape[1]
    groups = (
        ((charge, couple, amplitude), left, right),
        ((charge_in, couple_in, amplitude_in), left_in, right_in),
    )
    edge_products(groups, sources, middles, (keep, send), sectors, chip, core)


def sum_kernel(inner_own, inner_chip, inner_far, passed_on, near_own, edge_far, other, sigma):
    core = lax.axis_index("op") & (CORES - 1)
    sectors = sigma.shape[0]
    far = sectors - EDGE
    received = inner_far[: far - EDGE].astype(jnp.float32) + passed_on[...].astype(jnp.float32)
    sigma[EDGE:far] = inner_own[...] + inner_chip[...] + received
    sigma[pl.ds(far * core, EDGE)] = near_own[...] + edge_far[:EDGE].astype(jnp.float32)
    sigma[pl.ds(far * (1 - core), EDGE)] = other[...]


SMALL = pl.BlockSpec(memory_space=pltpu.SMEM)
LARGE = pl.BlockSpec(memory_space=pl.ANY)
BLOCK = pl.BlockSpec(memory_space=pltpu.VMEM)
MIB = 1024 * 1024


def shards(wavefunction, left_ops, right_ops, charge, couple, amplitude):
    sec = lax.axis_size("sec")
    op = lax.axis_size("op")
    sectors, states = wavefunction.shape[:2]
    operators = left_ops.shape[0]
    half = states // op
    inner = sectors - 2 * EDGE
    wide, narrow = jnp.float32, jnp.bfloat16

    def shape(*dims, dtype=wide):
        return jax.ShapeDtypeStruct(dims, dtype)

    def run(kernel, ops, targets, operands, in_specs, outs, out_specs, scratch):
        return pl.pallas_call(
            kernel,
            out_shape=outs,
            in_specs=in_specs,
            out_specs=out_specs,
            scratch_shapes=[pltpu.VMEM((targets * CORES * half, ops * states), narrow)] + scratch,
            compiler_params=pltpu.CompilerParams(vmem_limit_bytes=20 * MIB),
            cost_estimate=pl.CostEstimate(
                flops=ops * targets * CORES * half * states * states * 4,
                bytes_accessed=ops * states * states * 4,
                transcendentals=0,
            ),
        )(*operands)

    def over_op(value, flip):
        return lax.ppermute(value, "op", [(i, i ^ flip) for i in range(op)])


    def per_target(value):
        return value.reshape(-1, half, states)

    ring = []
    for s in range(sec):
        for o in range(op):
            ring.append((s * op + o, (s + 1 if o % CORES == 0 else s - 1) % sec * op + o))
    core = lax.axis_index("op") & (CORES - 1)
    border = lax.dynamic_slice_in_dim(wavefunction, (sectors - 1) * (1 - core), 1, 0)
    halo = lax.ppermute(border, ("sec", "op"), ring)
    left_in = over_op(left_ops, 1)
    right_in = over_op(right_ops, 1)

    small = (charge, couple, amplitude)
    small_in = [over_op(value, 1) for value in small]

    def in_hbm(*values):
        return [pltpu.with_memory_space_constraint(value, pltpu.HBM) for value in values]

    far_send, left, right, cells = run(
        inner_far_kernel,
        operators,
        inner,
        in_hbm(*small, left_ops, right_ops, wavefunction),
        [LARGE] * 6,
        [
            shape(CORES * inner * half, states, dtype=narrow),
            pltpu.VMEM(left_ops.shape, narrow),
            pltpu.VMEM(right_ops.shape, narrow),
            pltpu.VMEM(wavefunction.shape, narrow),
        ],
        [BLOCK] * 4,
        [
            pltpu.SMEM(charge.shape, charge.dtype),
            pltpu.SMEM(couple.shape, couple.dtype),
            pltpu.SMEM(amplitude.shape, amplitude.dtype),
            pltpu.SemaphoreType.DMA((3,)),
            pltpu.SemaphoreType.DMA((sectors,)),
            pltpu.SemaphoreType.DMA((2, operators)),
            pltpu.SemaphoreType.DMA((operators,)),
        ],
    )
    inner_far = over_op(far_send, CORES)

    here = in_hbm(*small)
    held = [*here, *small_in, left, right, left_in, right_in]
    held_specs = [SMALL] * 6 + [BLOCK] * 4
    edge_send, sources = run(
        edge_far_kernel,
        CORES * operators,
        EDGE,
        held + [cells, halo],
        held_specs + [BLOCK, BLOCK],
        [shape(CORES * EDGE * half, states, dtype=narrow), shape(EDGE + 2, states, states, dtype=narrow)],
        [BLOCK, BLOCK],
        [pltpu.SemaphoreType.DMA((2,))],
    )
    edge_far = over_op(edge_send, CORES)
    block = shape(inner * half, states)
    inner_own, inner_send = run(
        inner_own_kernel,
        operators,
        inner,
        [*here, left, right, cells],
        [SMALL] * 3 + [BLOCK] * 3,
        [block, block],
        [BLOCK, BLOCK],
        [],
    )
    inner_chip = over_op(inner_send, 1)
    edge_wide = shape(EDGE * half, states)
    near_own, near_mate = run(
        edge_own_kernel,
        CORES * operators,
        EDGE,
        held + [sources],
        held_specs + [BLOCK],
        [edge_wide, edge_wide],
        [BLOCK, BLOCK],
        [],
    )
    other = over_op(near_mate + edge_far[EDGE * half :].astype(wide), 1)
    passed_on = over_op(inner_far[inner * half :], 1)
    parts = (inner_own, inner_chip, inner_far, passed_on, near_own, edge_far, other)
    return pl.pallas_call(
        sum_kernel,
        out_shape=shape(sectors, half, states),
        in_specs=[BLOCK] * len(parts),
        out_specs=BLOCK,
        compiler_params=pltpu.CompilerParams(vmem_limit_bytes=16 * MIB),
        name="total",
    )(*[per_target(part) for part in parts])


def solution(mesh):
    placed = (
        P("sec", None, None),
        P("op", None, None),
        P("op", None, None),
        P("op"),
        P("op", "sec"),
        P("op", "sec"),
    )
    two_chips = mesh.shape["op"] == CORES * CORES
    return jax.shard_map(
        shards if two_chips else plain_shards,
        mesh=mesh, in_specs=placed, out_specs=P("sec", "op", None), check_vma=False,
    )
```

```python
import jax
import jax.numpy as jnp
from jax import lax
from jax.experimental import pallas as pl
from jax.experimental.pallas import tpu as pltpu
from jax.sharding import PartitionSpec as P


CORES = 2
AHEAD = 2
EDGE = 2


def padded(cells, sides, width):
    for axis, dim in sides:
        count = lax.axis_size(axis)
        head = lax.slice_in_dim(cells, 0, width, axis=dim)
        tail = lax.slice_in_dim(cells, cells.shape[dim] - width, cells.shape[dim], axis=dim)
        cells = jnp.concatenate(
            [
                lax.ppermute(tail, axis, [(i, (i + 1) % count) for i in range(count)]),
                cells,
                lax.ppermute(head, axis, [((i + 1) % count, i) for i in range(count)]),
            ],
            axis=dim,
        )
    return cells


def batched(left_op, sources, right_op, factor_values):
    middle = jnp.einsum("ij,sjk->sik", left_op, sources, preferred_element_type=jnp.float32).astype(
        jnp.bfloat16
    )
    contribution = jnp.einsum("sik,lk->sil", middle, right_op, preferred_element_type=jnp.float32)
    return contribution * factor_values[:, None, None]


def plain_shards(wavefunction, left_ops, right_ops, charge, couple, amplitude):
    factor = amplitude * couple.astype(jnp.float32)
    sectors = wavefunction.shape[0]
    states = wavefunction.shape[1]
    extended = padded(wavefunction, (("sec", 0),), 1)

    def accumulate(accumulated, operands):
        left_op, right_op, sector_shift, factor_row = operands
        start = 1 - sector_shift
        sources = lax.dynamic_slice_in_dim(extended, start, sectors, 0)
        return (accumulated + batched(left_op, sources, right_op, factor_row), None)

    initial = jnp.zeros((sectors, states, states), jnp.float32)
    accumulated, _ = lax.scan(accumulate, initial, (left_ops, right_ops, charge, factor))
    return lax.psum_scatter(accumulated, "op", scatter_dimension=1, tiled=True)


def middle_of(k, small, own, left, sources, middles, first_target, targets, chip, core):
    charge, couple, amplitude = small
    states = sources.shape[-1]
    half = middles.shape[0] // (CORES * targets)
    shift = 1 - charge[own]
    wide = jnp.concatenate([sources[shift + t] for t in range(targets)], axis=1)
    rows = jnp.concatenate(
        [left[own, pl.ds(row_of(chip, owner, half), half)] for owner in (core, 1 - core)], axis=0
    )
    middle = jnp.dot(rows, wide, preferred_element_type=jnp.float32)
    for t in range(targets):
        at = first_target + t
        factor = amplitude[own, at] * couple[own, at].astype(jnp.float32)
        block = middle[:, t * states : (t + 1) * states].astype(jnp.bfloat16)
        block = (block.astype(jnp.float32) * factor).astype(jnp.bfloat16)
        for part in range(CORES):
            row = (part * targets + t) * half
            middles[row : row + half, k * states : (k + 1) * states] = block[part * half : (part + 1) * half]


def summed(right, middles, results):
    count = middles.shape[0]
    step = 256
    for low in range(0, count, step):
        high = min(low + step, count)
        total = lax.dot_general(
            right, middles[low:high, :], (((1,), (1,)), ((), ())), preferred_element_type=jnp.float32
        ).T
        first = 0
        for result in results:
            last = first + result.shape[0]
            start, end = max(low, first), min(high, last)
            if start < end:
                result[start - first : end - first, :] = total[start - low : end - low, :].astype(result.dtype)
            first = last


def halves(results):
    width = results.shape[0] // CORES
    return [results.at[pl.ds(part * width, width)] for part in range(CORES)]


def position():
    place = lax.axis_index("op")
    return lax.shift_right_logical(place, CORES - 1), place & (CORES - 1)


def row_of(chip, core, half):
    return pl.multiple_of((chip * CORES + core) * half, 32)


def begin(source, target, sem):
    copy = pltpu.make_async_copy(source, target, sem)
    copy.start()
    return copy


def inner_far_kernel(
    charge, couple, amplitude, left_far, right_far, cells_far,
    direct, keep, send, left, right, cells, charge_kept, couple_kept, amplitude_kept, middles,
    charge_here, couple_here, amplitude_here, small_sem, cell_sem, left_sem, right_sem,
):
    chip, core = position()
    operators = left.shape[0]
    sectors = cells.shape[0]
    targets = sectors - 2 * EDGE
    chip_rows = (direct.shape[0] + keep.shape[0] + send.shape[0]) // targets
    inside = range(EDGE - 1, sectors - EDGE + 1)

    def rows(k, place):
        at = pl.ds(pl.multiple_of(place * chip_rows, 64), chip_rows)
        return left_far.at[k, at], left.at[k, at]

    def cell(s):
        return begin(cells_far.at[s], cells.at[s], cell_sem.at[s])

    small = [
        begin(charge, charge_here, small_sem.at[0]),
        begin(couple, couple_here, small_sem.at[1]),
        begin(amplitude, amplitude_here, small_sem.at[2]),
    ]
    first = [cell(s) for s in inside]
    lefts = [begin(*rows(k, 1 - chip), left_sem.at[0, k]) for k in range(AHEAD)]
    for copy in small:
        copy.wait()
    lefts += [begin(*rows(k, 1 - chip), left_sem.at[0, k]) for k in range(AHEAD, operators)]
    for copy in first + lefts[:AHEAD]:
        copy.wait()
    rights = [begin(right_far.at[k], right.at[k], right_sem.at[k]) for k in range(operators)]
    later = [begin(*rows(k, chip), left_sem.at[1, k]) for k in range(operators)]
    later += [cell(s) for s in range(sectors) if s not in inside]
    later += [
        begin(charge, charge_kept, small_sem.at[3]),
        begin(couple, couple_kept, small_sem.at[4]),
        begin(amplitude, amplitude_kept, small_sem.at[5]),
    ]
    sources = cells.at[pl.ds(EDGE - 1, targets + 2)]
    here = (charge_here, couple_here, amplitude_here)
    for k in range(operators):
        if k == AHEAD:
            for copy in lefts[AHEAD:]:
                copy.wait()
        middle_of(k, here, k, left, sources, middles, EDGE, targets, 1 - chip, core)
    for copy in rights:
        copy.wait()
    near, far = halves(direct)
    summed(jnp.concatenate([right[k] for k in range(operators)], axis=1), middles, (near, keep, far, send))
    for copy in later:
        copy.wait()


def inner_own_kernel(charge, couple, amplitude, left, right, cells, keep, send, middles):
    chip, core = position()
    operators = left.shape[0]
    targets = cells.shape[0] - 2 * EDGE
    inside = cells.at[pl.ds(EDGE - 1, targets + 2)]
    for k in range(operators):
        middle_of(k, (charge, couple, amplitude), k, left, inside, middles, EDGE, targets, chip, core)
    summed(jnp.concatenate([right[k] for k in range(operators)], axis=1), middles, (keep, send))


def edge_products(groups, sources, middles, results, sectors, chip, core):
    k = 0
    first_target = (sectors - EDGE) * core
    for small, left, right in groups:
        for own in range(left.shape[0]):
            middle_of(k, small, own, left, sources, middles, first_target, EDGE, chip, core)
            k += 1
    wide = jnp.concatenate([right[own] for _, _, right in groups for own in range(right.shape[0])], axis=1)
    summed(wide, middles, results)


def edge_far_kernel(
    charge, couple, amplitude, charge_in, couple_in, amplitude_in, left, right, left_in, right_in,
    cells, halo, send, sources, middles, sem,
):
    chip, core = position()
    sectors = cells.shape[0]
    inside = EDGE + 1
    copies = [
        pltpu.make_async_copy(
            cells.at[pl.ds((sectors - inside) * core, inside)], sources.at[pl.ds(1 - core, inside)], sem.at[0]
        ),
        pltpu.make_async_copy(halo.at[0], sources.at[inside * core], sem.at[1]),
    ]
    for copy in copies:
        copy.start()
    for copy in copies:
        copy.wait()
    groups = (
        ((charge, couple, amplitude), left, right),
        ((charge_in, couple_in, amplitude_in), left_in, right_in),
    )
    edge_products(groups, sources, middles, halves(send), sectors, 1 - chip, core)


def edge_own_kernel(
    charge, couple, amplitude, charge_in, couple_in, amplitude_in, left, right, left_in, right_in,
    sources, keep, send, middles,
):
    chip, core = position()
    sectors = couple.shape[1]
    groups = (
        ((charge, couple, amplitude), left, right),
        ((charge_in, couple_in, amplitude_in), left_in, right_in),
    )
    edge_products(groups, sources, middles, (keep, send), sectors, chip, core)


def sum_kernel(inner_own, inner_chip, direct_far, later_far, near_own, other, sigma):
    core = lax.axis_index("op") & (CORES - 1)
    sectors = sigma.shape[0]
    far = sectors - EDGE
    split = EDGE + direct_far.shape[0] // CORES
    direct = split - EDGE
    sigma[EDGE:split] = inner_own[:direct] + inner_chip[:direct] + direct_far[:direct].astype(jnp.float32)
    sigma[split:far] = inner_own[direct:] + inner_chip[direct:] + later_far[CORES * EDGE :].astype(jnp.float32)
    sigma[pl.ds(far * core, EDGE)] = near_own[...] + later_far[:EDGE].astype(jnp.float32)
    sigma[pl.ds(far * (1 - core), EDGE)] = other[...]


SMALL = pl.BlockSpec(memory_space=pltpu.SMEM)
LARGE = pl.BlockSpec(memory_space=pl.ANY)
BLOCK = pl.BlockSpec(memory_space=pltpu.VMEM)
MIB = 1024 * 1024


def shards(wavefunction, left_ops, right_ops, charge, couple, amplitude):
    sec = lax.axis_size("sec")
    op = lax.axis_size("op")
    sectors, states = wavefunction.shape[:2]
    operators = left_ops.shape[0]
    half = states // op
    inner = sectors - 2 * EDGE
    wide, narrow = jnp.float32, jnp.bfloat16

    def shape(*dims, dtype=wide):
        return jax.ShapeDtypeStruct(dims, dtype)

    def run(kernel, ops, targets, operands, in_specs, outs, out_specs, scratch):
        return pl.pallas_call(
            kernel,
            out_shape=outs,
            in_specs=in_specs,
            out_specs=out_specs,
            scratch_shapes=[pltpu.VMEM((targets * CORES * half, ops * states), narrow)] + scratch,
            compiler_params=pltpu.CompilerParams(vmem_limit_bytes=20 * MIB),
            cost_estimate=pl.CostEstimate(
                flops=ops * targets * CORES * half * states * states * 4,
                bytes_accessed=ops * states * states * 4,
                transcendentals=0,
            ),
        )(*operands)

    def over_op(value, flip):
        return lax.ppermute(value, "op", [(i, i ^ flip) for i in range(op)])


    def per_target(value):
        return value.reshape(-1, half, states)

    ring = []
    for s in range(sec):
        for o in range(op):
            ring.append((s * op + o, (s + 1 if o % CORES == 0 else s - 1) % sec * op + o))
    core = lax.axis_index("op") & (CORES - 1)
    border = lax.dynamic_slice_in_dim(wavefunction, (sectors - 1) * (1 - core), 1, 0)
    halo = lax.ppermute(border, ("sec", "op"), ring)
    left_in = over_op(left_ops, 1)
    right_in = over_op(right_ops, 1)

    small = (charge, couple, amplitude)
    small_in = [over_op(value, 1) for value in small]

    def in_hbm(*values):
        return [pltpu.with_memory_space_constraint(value, pltpu.HBM) for value in values]

    direct_rows = inner // 2 * half
    reduced = shape(inner * half - direct_rows, states)
    direct, keep, send, left, right, cells, *here = run(
        inner_far_kernel,
        operators,
        inner,
        in_hbm(*small, left_ops, right_ops, wavefunction),
        [LARGE] * 6,
        [
            shape(CORES * direct_rows, states, dtype=narrow),
            reduced,
            reduced,
            pltpu.VMEM(left_ops.shape, narrow),
            pltpu.VMEM(right_ops.shape, narrow),
            pltpu.VMEM(wavefunction.shape, narrow),
            *[pltpu.VMEM(value.shape, value.dtype) for value in small],
        ],
        [BLOCK] * 9,
        [
            pltpu.SMEM(charge.shape, charge.dtype),
            pltpu.SMEM(couple.shape, couple.dtype),
            pltpu.SMEM(amplitude.shape, amplitude.dtype),
            pltpu.SemaphoreType.DMA((6,)),
            pltpu.SemaphoreType.DMA((sectors,)),
            pltpu.SemaphoreType.DMA((2, operators)),
            pltpu.SemaphoreType.DMA((operators,)),
        ],
    )
    direct_far = over_op(direct, CORES)
    send_in = over_op(send, 1)

    held = [*here, *small_in, left, right, left_in, right_in]
    held_specs = [SMALL] * 6 + [BLOCK] * 4
    edge_send, sources = run(
        edge_far_kernel,
        CORES * operators,
        EDGE,
        held + [cells, halo],
        held_specs + [BLOCK, BLOCK],
        [shape(CORES * EDGE * half, states, dtype=narrow), shape(EDGE + 2, states, states, dtype=narrow)],
        [BLOCK, BLOCK],
        [pltpu.SemaphoreType.DMA((2,))],
    )
    later = jnp.concatenate([edge_send, (keep + send_in).astype(narrow)], axis=0)
    later_far = over_op(later, CORES)
    block = shape(inner * half, states)
    inner_own, inner_send = run(
        inner_own_kernel,
        operators,
        inner,
        [*here, left, right, cells],
        [SMALL] * 3 + [BLOCK] * 3,
        [block, block],
        [BLOCK, BLOCK],
        [],
    )
    mate = inner_send[:direct_rows] + direct_far[direct_rows:].astype(wide)
    inner_chip = over_op(jnp.concatenate([mate, inner_send[direct_rows:]], axis=0), 1)
    edge_wide = shape(EDGE * half, states)
    near_own, near_mate = run(
        edge_own_kernel,
        CORES * operators,
        EDGE,
        held + [sources],
        held_specs + [BLOCK],
        [edge_wide, edge_wide],
        [BLOCK, BLOCK],
        [],
    )
    passed = later_far[EDGE * half : CORES * EDGE * half].astype(wide)
    other = over_op(near_mate + passed, 1)
    parts = (inner_own, inner_chip, direct_far, later_far, near_own, other)
    return pl.pallas_call(
        sum_kernel,
        out_shape=shape(sectors, half, states),
        in_specs=[BLOCK] * len(parts),
        out_specs=BLOCK,
        compiler_params=pltpu.CompilerParams(vmem_limit_bytes=16 * MIB),
        name="total",
    )(*[per_target(part) for part in parts])


def solution(mesh):
    placed = (
        P("sec", None, None),
        P("op", None, None),
        P("op", None, None),
        P("op"),
        P("op", "sec"),
        P("op", "sec"),
    )
    two_chips = mesh.shape["op"] == CORES * CORES
    return jax.shard_map(
        shards if two_chips else plain_shards,
        mesh=mesh, in_specs=placed, out_specs=P("sec", "op", None), check_vma=False,
    )
```

```python
import jax
import jax.numpy as jnp
from jax import lax
from jax.experimental import pallas as pl
from jax.experimental.pallas import tpu as pltpu
from jax.sharding import PartitionSpec as P


CORES = 2
AHEAD = 2
EDGE = 2


def padded(cells, sides, width):
    for axis, dim in sides:
        count = lax.axis_size(axis)
        head = lax.slice_in_dim(cells, 0, width, axis=dim)
        tail = lax.slice_in_dim(cells, cells.shape[dim] - width, cells.shape[dim], axis=dim)
        cells = jnp.concatenate(
            [
                lax.ppermute(tail, axis, [(i, (i + 1) % count) for i in range(count)]),
                cells,
                lax.ppermute(head, axis, [((i + 1) % count, i) for i in range(count)]),
            ],
            axis=dim,
        )
    return cells


def batched(left_op, sources, right_op, factor_values):
    middle = jnp.einsum("ij,sjk->sik", left_op, sources, preferred_element_type=jnp.float32).astype(
        jnp.bfloat16
    )
    contribution = jnp.einsum("sik,lk->sil", middle, right_op, preferred_element_type=jnp.float32)
    return contribution * factor_values[:, None, None]


def plain_shards(wavefunction, left_ops, right_ops, charge, couple, amplitude):
    factor = amplitude * couple.astype(jnp.float32)
    sectors = wavefunction.shape[0]
    states = wavefunction.shape[1]
    extended = padded(wavefunction, (("sec", 0),), 1)

    def accumulate(accumulated, operands):
        left_op, right_op, sector_shift, factor_row = operands
        start = 1 - sector_shift
        sources = lax.dynamic_slice_in_dim(extended, start, sectors, 0)
        return (accumulated + batched(left_op, sources, right_op, factor_row), None)

    initial = jnp.zeros((sectors, states, states), jnp.float32)
    accumulated, _ = lax.scan(accumulate, initial, (left_ops, right_ops, charge, factor))
    return lax.psum_scatter(accumulated, "op", scatter_dimension=1, tiled=True)


def own_rows(left, own, chip, core, half):
    return [left[own, pl.ds(row_of(chip, owner, half), half)] for owner in (core, 1 - core)]


def middle_of(k, small, own, parts, sources, middles, first_target, targets):
    charge, couple, amplitude = small
    states = sources.shape[-1]
    half = middles.shape[0] // (CORES * targets)
    shift = 1 - charge[own]
    wide = jnp.concatenate([sources[shift + t] for t in range(targets)], axis=1)
    rows = jnp.concatenate(parts, axis=0)
    middle = jnp.dot(rows, wide, preferred_element_type=jnp.float32)
    for t in range(targets):
        at = first_target + t
        factor = amplitude[own, at] * couple[own, at].astype(jnp.float32)
        block = middle[:, t * states : (t + 1) * states].astype(jnp.bfloat16)
        block = (block.astype(jnp.float32) * factor).astype(jnp.bfloat16)
        for part in range(CORES):
            row = (part * targets + t) * half
            middles[row : row + half, k * states : (k + 1) * states] = block[part * half : (part + 1) * half]


def summed(right, middles, results):
    count = middles.shape[0]
    step = 256
    for low in range(0, count, step):
        high = min(low + step, count)
        total = lax.dot_general(
            right, middles[low:high, :], (((1,), (1,)), ((), ())), preferred_element_type=jnp.float32
        ).T
        first = 0
        for result in results:
            last = first + result.shape[0]
            start, end = max(low, first), min(high, last)
            if start < end:
                result[start - first : end - first, :] = total[start - low : end - low, :].astype(result.dtype)
            first = last


def halves(results):
    width = results.shape[0] // CORES
    return [results.at[pl.ds(part * width, width)] for part in range(CORES)]


def position():
    place = lax.axis_index("op")
    return lax.shift_right_logical(place, CORES - 1), place & (CORES - 1)


def row_of(chip, core, half):
    return pl.multiple_of((chip * CORES + core) * half, 32)


def rows_of_chip(ops, chip, rows):
    return ops.at[pl.ds(pl.multiple_of(chip * rows, 64), rows)]


def begin(source, target, sem):
    copy = pltpu.make_async_copy(source, target, sem)
    copy.start()
    return copy


def first_kernel(left_far, cells_far, border, head, sem):
    chip, core = position()
    copies = [begin(cells_far.at[(cells_far.shape[0] - 1) * (1 - core)], border.at[0], sem.at[0])]
    for k in range(head.shape[0]):
        rows = rows_of_chip(left_far.at[k], 1 - chip, head.shape[1])
        copies.append(begin(rows, head.at[k], sem.at[1 + k]))
    for copy in copies:
        copy.wait()


def inner_far_kernel(
    charge, couple, amplitude, left_far, right_far, cells, head,
    direct, keep, send, left, right, middles, left_sem, right_sem,
):
    chip, core = position()
    operators = left.shape[0]
    targets = cells.shape[0] - 2 * EDGE
    ahead, chip_rows = head.shape[:2]
    half = chip_rows // CORES

    def rows(k, place, which):
        origin = rows_of_chip(left_far.at[k], place, chip_rows)
        return begin(origin, rows_of_chip(left.at[k], place, chip_rows), left_sem.at[which, k])

    lefts = [rows(k, 1 - chip, 0) for k in range(ahead, operators)]
    rights = [begin(right_far.at[k], right.at[k], right_sem.at[k]) for k in range(operators)]
    inside = cells.at[pl.ds(EDGE - 1, targets + 2)]
    later = []
    for k in range(operators):
        if k < ahead:
            parts = [head[k, pl.ds(pl.multiple_of(o * half, 32), half)] for o in (core, 1 - core)]
        else:
            if k == ahead:
                for copy in lefts:
                    copy.wait()
                later += [rows(own, 1 - chip, 0) for own in range(ahead)]
                later += [rows(own, chip, 1) for own in range(operators)]
            parts = own_rows(left, k, 1 - chip, core, half)
        middle_of(k, (charge, couple, amplitude), k, parts, inside, middles, EDGE, targets)
    for copy in rights:
        copy.wait()
    near, far = halves(direct)
    summed(jnp.concatenate([right[k] for k in range(operators)], axis=1), middles, (near, keep, far, send))
    for copy in later:
        copy.wait()


def inner_own_kernel(charge, couple, amplitude, left, right, cells, keep, send, middles):
    chip, core = position()
    operators = left.shape[0]
    targets = cells.shape[0] - 2 * EDGE
    inside = cells.at[pl.ds(EDGE - 1, targets + 2)]
    half = keep.shape[0] // targets
    for k in range(operators):
        parts = own_rows(left, k, chip, core, half)
        middle_of(k, (charge, couple, amplitude), k, parts, inside, middles, EDGE, targets)
    summed(jnp.concatenate([right[k] for k in range(operators)], axis=1), middles, (keep, send))


def edge_products(groups, sources, middles, results, sectors, chip, core):
    k = 0
    first_target = (sectors - EDGE) * core
    half = middles.shape[0] // (CORES * EDGE)
    for small, left, right in groups:
        for own in range(left.shape[0]):
            parts = own_rows(left, own, chip, core, half)
            middle_of(k, small, own, parts, sources, middles, first_target, EDGE)
            k += 1
    wide = jnp.concatenate([right[own] for _, _, right in groups for own in range(right.shape[0])], axis=1)
    summed(wide, middles, results)


def edge_far_kernel(
    charge, couple, amplitude, charge_in, couple_in, amplitude_in, left, right, left_in, right_in,
    cells, halo, send, sources, middles, sem,
):
    chip, core = position()
    sectors = cells.shape[0]
    inside = EDGE + 1
    copies = [
        pltpu.make_async_copy(
            cells.at[pl.ds((sectors - inside) * core, inside)], sources.at[pl.ds(1 - core, inside)], sem.at[0]
        ),
        pltpu.make_async_copy(halo.at[0], sources.at[inside * core], sem.at[1]),
    ]
    for copy in copies:
        copy.start()
    for copy in copies:
        copy.wait()
    groups = (
        ((charge, couple, amplitude), left, right),
        ((charge_in, couple_in, amplitude_in), left_in, right_in),
    )
    edge_products(groups, sources, middles, halves(send), sectors, 1 - chip, core)


def edge_own_kernel(
    charge, couple, amplitude, charge_in, couple_in, amplitude_in, left, right, left_in, right_in,
    sources, keep, send, middles,
):
    chip, core = position()
    sectors = couple.shape[1]
    groups = (
        ((charge, couple, amplitude), left, right),
        ((charge_in, couple_in, amplitude_in), left_in, right_in),
    )
    edge_products(groups, sources, middles, (keep, send), sectors, chip, core)


def sum_kernel(inner_own, inner_chip, direct_far, later_far, near_own, other, sigma):
    core = lax.axis_index("op") & (CORES - 1)
    sectors = sigma.shape[0]
    far = sectors - EDGE
    split = EDGE + direct_far.shape[0] // CORES
    direct = split - EDGE
    sigma[EDGE:split] = inner_own[:direct] + inner_chip[:direct] + direct_far[:direct].astype(jnp.float32)
    sigma[split:far] = inner_own[direct:] + inner_chip[direct:] + later_far[CORES * EDGE :].astype(jnp.float32)
    sigma[pl.ds(far * core, EDGE)] = near_own[...] + later_far[:EDGE].astype(jnp.float32)
    sigma[pl.ds(far * (1 - core), EDGE)] = other[...]


SMALL = pl.BlockSpec(memory_space=pltpu.SMEM)
LARGE = pl.BlockSpec(memory_space=pl.ANY)
BLOCK = pl.BlockSpec(memory_space=pltpu.VMEM)
MIB = 1024 * 1024


def shards(wavefunction, left_ops, right_ops, charge, couple, amplitude):
    sec = lax.axis_size("sec")
    op = lax.axis_size("op")
    sectors, states = wavefunction.shape[:2]
    operators = left_ops.shape[0]
    half = states // op
    inner = sectors - 2 * EDGE
    wide, narrow = jnp.float32, jnp.bfloat16

    def shape(*dims, dtype=wide):
        return jax.ShapeDtypeStruct(dims, dtype)

    def run(kernel, ops, targets, operands, in_specs, outs, out_specs, scratch):
        return pl.pallas_call(
            kernel,
            out_shape=outs,
            in_specs=in_specs,
            out_specs=out_specs,
            scratch_shapes=[pltpu.VMEM((targets * CORES * half, ops * states), narrow)] + scratch,
            compiler_params=pltpu.CompilerParams(vmem_limit_bytes=20 * MIB),
            cost_estimate=pl.CostEstimate(
                flops=ops * targets * CORES * half * states * states * 4,
                bytes_accessed=ops * states * states * 4,
                transcendentals=0,
            ),
        )(*operands)

    def over_op(value, flip):
        return lax.ppermute(value, "op", [(i, i ^ flip) for i in range(op)])


    def per_target(value):
        return value.reshape(-1, half, states)

    ring = []
    for s in range(sec):
        for o in range(op):
            ring.append((s * op + o, (s + 1 if o % CORES == 0 else s - 1) % sec * op + o))

    def in_hbm(*values):
        return [pltpu.with_memory_space_constraint(value, pltpu.HBM) for value in values]

    border, head = pl.pallas_call(
        first_kernel,
        out_shape=[
            pltpu.VMEM((1, states, states), narrow),
            pltpu.VMEM((AHEAD, CORES * half, states), narrow),
        ],
        in_specs=[LARGE] * 2,
        out_specs=[BLOCK] * 2,
        scratch_shapes=[pltpu.SemaphoreType.DMA((1 + AHEAD,))],
        compiler_params=pltpu.CompilerParams(vmem_limit_bytes=4 * MIB),
        name="first_kernel",
    )(*in_hbm(left_ops, wavefunction))
    halo = lax.ppermute(border, ("sec", "op"), ring)
    left_far, right_far = in_hbm(left_ops, right_ops)
    left_in = over_op(left_ops, 1)
    right_in = over_op(right_ops, 1)
    small = (charge, couple, amplitude)
    small_in = [over_op(value, 1) for value in small]

    direct_rows = inner // 2 * half
    reduced = shape(inner * half - direct_rows, states)
    direct, keep, send, left, right = run(
        inner_far_kernel,
        operators,
        inner,
        (*small, left_far, right_far, wavefunction, head),
        [SMALL] * 3 + [LARGE] * 2 + [BLOCK] * 2,
        [
            shape(CORES * direct_rows, states, dtype=narrow),
            reduced,
            reduced,
            pltpu.VMEM(left_ops.shape, narrow),
            pltpu.VMEM(right_ops.shape, narrow),
        ],
        [BLOCK] * 5,
        [pltpu.SemaphoreType.DMA((2, operators)), pltpu.SemaphoreType.DMA((operators,))],
    )
    direct_far = over_op(direct, CORES)
    send_in = over_op(send, 1)

    held = [*small, *small_in, left, right, left_in, right_in]
    held_specs = [SMALL] * 6 + [BLOCK] * 4
    edge_send, sources = run(
        edge_far_kernel,
        CORES * operators,
        EDGE,
        held + [wavefunction, halo],
        held_specs + [BLOCK, BLOCK],
        [shape(CORES * EDGE * half, states, dtype=narrow), shape(EDGE + 2, states, states, dtype=narrow)],
        [BLOCK, BLOCK],
        [pltpu.SemaphoreType.DMA((2,))],
    )
    later = jnp.concatenate([edge_send, (keep + send_in).astype(narrow)], axis=0)
    later_far = over_op(later, CORES)
    block = shape(inner * half, states)
    inner_own, inner_send = run(
        inner_own_kernel,
        operators,
        inner,
        [*small, left, right, wavefunction],
        [SMALL] * 3 + [BLOCK] * 3,
        [block, block],
        [BLOCK, BLOCK],
        [],
    )
    mate = inner_send[:direct_rows] + direct_far[direct_rows:].astype(wide)
    inner_chip = over_op(jnp.concatenate([mate, inner_send[direct_rows:]], axis=0), 1)
    edge_wide = shape(EDGE * half, states)
    near_own, near_mate = run(
        edge_own_kernel,
        CORES * operators,
        EDGE,
        held + [sources],
        held_specs + [BLOCK],
        [edge_wide, edge_wide],
        [BLOCK, BLOCK],
        [],
    )
    passed = later_far[EDGE * half : CORES * EDGE * half].astype(wide)
    other = over_op(near_mate + passed, 1)
    parts = (inner_own, inner_chip, direct_far, later_far, near_own, other)
    return pl.pallas_call(
        sum_kernel,
        out_shape=shape(sectors, half, states),
        in_specs=[BLOCK] * len(parts),
        out_specs=BLOCK,
        compiler_params=pltpu.CompilerParams(vmem_limit_bytes=16 * MIB),
        name="total",
    )(*[per_target(part) for part in parts])


def solution(mesh):
    placed = (
        P("sec", None, None),
        P("op", None, None),
        P("op", None, None),
        P("op"),
        P("op", "sec"),
        P("op", "sec"),
    )
    two_chips = mesh.shape["op"] == CORES * CORES
    return jax.shard_map(
        shards if two_chips else plain_shards,
        mesh=mesh, in_specs=placed, out_specs=P("sec", "op", None), check_vma=False,
    )
```

```python
import functools

import jax
import jax.numpy as jnp
from jax import lax
from jax.experimental import pallas as pl
from jax.experimental.pallas import tpu as pltpu
from jax.sharding import PartitionSpec as P


CORES = 2
AHEAD = 2
EDGE = 2


def padded(cells, sides, width):
    for axis, dim in sides:
        count = lax.axis_size(axis)
        head = lax.slice_in_dim(cells, 0, width, axis=dim)
        tail = lax.slice_in_dim(cells, cells.shape[dim] - width, cells.shape[dim], axis=dim)
        cells = jnp.concatenate(
            [
                lax.ppermute(tail, axis, [(i, (i + 1) % count) for i in range(count)]),
                cells,
                lax.ppermute(head, axis, [((i + 1) % count, i) for i in range(count)]),
            ],
            axis=dim,
        )
    return cells


def batched(left_op, sources, right_op, factor_values):
    middle = jnp.einsum("ij,sjk->sik", left_op, sources, preferred_element_type=jnp.float32).astype(
        jnp.bfloat16
    )
    contribution = jnp.einsum("sik,lk->sil", middle, right_op, preferred_element_type=jnp.float32)
    return contribution * factor_values[:, None, None]


def plain_shards(wavefunction, left_ops, right_ops, charge, couple, amplitude):
    factor = amplitude * couple.astype(jnp.float32)
    sectors = wavefunction.shape[0]
    states = wavefunction.shape[1]
    extended = padded(wavefunction, (("sec", 0),), 1)

    def accumulate(accumulated, operands):
        left_op, right_op, sector_shift, factor_row = operands
        start = 1 - sector_shift
        sources = lax.dynamic_slice_in_dim(extended, start, sectors, 0)
        return (accumulated + batched(left_op, sources, right_op, factor_row), None)

    initial = jnp.zeros((sectors, states, states), jnp.float32)
    accumulated, _ = lax.scan(accumulate, initial, (left_ops, right_ops, charge, factor))
    return lax.psum_scatter(accumulated, "op", scatter_dimension=1, tiled=True)


def middle_of(k, small, own, left, sources, middles, first_target, targets, chip, core):
    charge, couple, amplitude = small
    states = sources.shape[-1]
    half = middles.shape[0] // (CORES * targets)
    shift = 1 - charge[own]
    wide = jnp.concatenate([sources[shift + t] for t in range(targets)], axis=1)
    rows = jnp.concatenate(
        [left[own, pl.ds(row_of(chip, owner, half), half)] for owner in (core, 1 - core)], axis=0
    )
    middle = jnp.dot(rows, wide, preferred_element_type=jnp.float32)
    for t in range(targets):
        at = first_target + t
        factor = amplitude[own, at] * couple[own, at].astype(jnp.float32)
        block = middle[:, t * states : (t + 1) * states].astype(jnp.bfloat16)
        block = (block.astype(jnp.float32) * factor).astype(jnp.bfloat16)
        for part in range(CORES):
            row = (part * targets + t) * half
            middles[row : row + half, k * states : (k + 1) * states] = block[part * half : (part + 1) * half]


def summed(right, middles, results):
    count = middles.shape[0]
    step = 256
    for low in range(0, count, step):
        high = min(low + step, count)
        total = lax.dot_general(
            right, middles[low:high, :], (((1,), (1,)), ((), ())), preferred_element_type=jnp.float32
        ).T
        first = 0
        for result in results:
            last = first + result.shape[0]
            start, end = max(low, first), min(high, last)
            if start < end:
                result[start - first : end - first, :] = total[start - low : end - low, :].astype(result.dtype)
            first = last


def halves(results):
    width = results.shape[0] // CORES
    return [results.at[pl.ds(part * width, width)] for part in range(CORES)]


def position():
    place = lax.axis_index("op")
    return lax.shift_right_logical(place, CORES - 1), place & (CORES - 1)


def row_of(chip, core, half):
    return pl.multiple_of((chip * CORES + core) * half, 32)


def begin(source, target, sem):
    copy = pltpu.make_async_copy(source, target, sem)
    copy.start()
    return copy


def inner_far_kernel(
    charge, couple, amplitude, left_far, right_far, cells_far,
    direct, keep, send, left, right, cells, charge_kept, couple_kept, amplitude_kept, middles,
    charge_here, couple_here, amplitude_here, small_sem, cell_sem, left_sem, right_sem,
):
    chip, core = position()
    operators = left.shape[0]
    sectors = cells.shape[0]
    targets = sectors - 2 * EDGE
    chip_rows = (direct.shape[0] + keep.shape[0] + send.shape[0]) // targets
    inside = range(EDGE - 1, sectors - EDGE + 1)

    def rows(k, place):
        at = pl.ds(pl.multiple_of(place * chip_rows, 64), chip_rows)
        return left_far.at[k, at], left.at[k, at]

    def cell(s):
        return begin(cells_far.at[s], cells.at[s], cell_sem.at[s])

    small = [
        begin(charge, charge_here, small_sem.at[0]),
        begin(couple, couple_here, small_sem.at[1]),
        begin(amplitude, amplitude_here, small_sem.at[2]),
    ]
    first = [cell(s) for s in inside]
    lefts = [begin(*rows(k, 1 - chip), left_sem.at[0, k]) for k in range(AHEAD)]
    for copy in small:
        copy.wait()
    lefts += [begin(*rows(k, 1 - chip), left_sem.at[0, k]) for k in range(AHEAD, operators)]
    for copy in first + lefts[:AHEAD]:
        copy.wait()
    rights = [begin(right_far.at[k], right.at[k], right_sem.at[k]) for k in range(operators)]
    later = [begin(*rows(k, chip), left_sem.at[1, k]) for k in range(operators)]
    later += [cell(s) for s in range(sectors) if s not in inside]
    later += [
        begin(charge, charge_kept, small_sem.at[3]),
        begin(couple, couple_kept, small_sem.at[4]),
        begin(amplitude, amplitude_kept, small_sem.at[5]),
    ]
    sources = cells.at[pl.ds(EDGE - 1, targets + 2)]
    here = (charge_here, couple_here, amplitude_here)
    for k in range(operators):
        if k == AHEAD:
            for copy in lefts[AHEAD:]:
                copy.wait()
        middle_of(k, here, k, left, sources, middles, EDGE, targets, 1 - chip, core)
    for copy in rights:
        copy.wait()
    near, far = halves(direct)
    summed(jnp.concatenate([right[k] for k in range(operators)], axis=1), middles, (near, keep, far, send))
    for copy in later:
        copy.wait()


def edge_products(groups, sources, middles, results, sectors, chip, core):
    k = 0
    first_target = (sectors - EDGE) * core
    for small, left, right in groups:
        for own in range(left.shape[0]):
            middle_of(k, small, own, left, sources, middles, first_target, EDGE, chip, core)
            k += 1
    wide = jnp.concatenate([right[own] for _, _, right in groups for own in range(right.shape[0])], axis=1)
    summed(wide, middles, results)


def edge_far_kernel(
    charge, couple, amplitude, charge_in, couple_in, amplitude_in, left, right, left_in, right_in,
    cells, halo, send, sources, middles, sem,
):
    chip, core = position()
    sectors = cells.shape[0]
    inside = EDGE + 1
    copies = [
        pltpu.make_async_copy(
            cells.at[pl.ds((sectors - inside) * core, inside)], sources.at[pl.ds(1 - core, inside)], sem.at[0]
        ),
        pltpu.make_async_copy(halo.at[0], sources.at[inside * core], sem.at[1]),
    ]
    for copy in copies:
        copy.start()
    for copy in copies:
        copy.wait()
    groups = (
        ((charge, couple, amplitude), left, right),
        ((charge_in, couple_in, amplitude_in), left_in, right_in),
    )
    edge_products(groups, sources, middles, halves(send), sectors, 1 - chip, core)


def own_kernel(
    charge, couple, amplitude, charge_in, couple_in, amplitude_in, left, right, left_in, right_in,
    cells, sources, inner_keep, edge_keep, send, edge_middles, inner_middles,
):
    chip, core = position()
    sectors = couple.shape[1]
    small = (charge, couple, amplitude)
    inner = sectors - 2 * EDGE
    inside = cells.at[pl.ds(EDGE - 1, inner + 2)]
    for k in range(left.shape[0]):
        middle_of(k, small, k, left, inside, inner_middles, EDGE, inner, chip, core)
    edge_rows = edge_keep.shape[0]
    inner_send = send.at[pl.ds(edge_rows, send.shape[0] - edge_rows)]
    wide = jnp.concatenate([right[k] for k in range(right.shape[0])], axis=1)
    summed(wide, inner_middles, (inner_keep, inner_send))
    groups = ((small, left, right), ((charge_in, couple_in, amplitude_in), left_in, right_in))
    results = (edge_keep, send.at[pl.ds(0, edge_rows)])
    edge_products(groups, sources, edge_middles, results, sectors, chip, core)


def mate_kernel(edge, own, later_far, direct_far, mate):
    both = edge + direct_far.shape[0] // CORES
    mate[:edge] = (own[:edge] + later_far[edge : CORES * edge].astype(jnp.float32)).astype(mate.dtype)
    mate[edge:both] = (own[edge:both] + direct_far[both - edge :].astype(jnp.float32)).astype(mate.dtype)
    mate[both:] = own[both:].astype(mate.dtype)


def sum_kernel(inner_own, near_own, direct_far, later_far, mate, sigma):
    core = lax.axis_index("op") & (CORES - 1)
    sectors = sigma.shape[0]
    far = sectors - EDGE
    direct = direct_far.shape[0] // CORES
    split = EDGE + direct

    def wide(value):
        return value.astype(jnp.float32)

    sigma[EDGE:split] = inner_own[:direct] + wide(direct_far[:direct]) + wide(mate[EDGE:split])
    sigma[split:far] = inner_own[direct:] + wide(later_far[CORES * EDGE :]) + wide(mate[split:])
    sigma[pl.ds(far * core, EDGE)] = near_own[...] + wide(later_far[:EDGE])
    sigma[pl.ds(far * (1 - core), EDGE)] = wide(mate[:EDGE])


SMALL = pl.BlockSpec(memory_space=pltpu.SMEM)
LARGE = pl.BlockSpec(memory_space=pl.ANY)
BLOCK = pl.BlockSpec(memory_space=pltpu.VMEM)
MIB = 1024 * 1024


def shards(wavefunction, left_ops, right_ops, charge, couple, amplitude):
    sec = lax.axis_size("sec")
    op = lax.axis_size("op")
    sectors, states = wavefunction.shape[:2]
    operators = left_ops.shape[0]
    half = states // op
    inner = sectors - 2 * EDGE
    wide, narrow = jnp.float32, jnp.bfloat16

    def shape(*dims, dtype=wide):
        return jax.ShapeDtypeStruct(dims, dtype)

    def run(kernel, ops, targets, operands, in_specs, outs, out_specs, scratch):
        return pl.pallas_call(
            kernel,
            out_shape=outs,
            in_specs=in_specs,
            out_specs=out_specs,
            scratch_shapes=[pltpu.VMEM((targets * CORES * half, ops * states), narrow)] + scratch,
            compiler_params=pltpu.CompilerParams(vmem_limit_bytes=28 * MIB),
            cost_estimate=pl.CostEstimate(
                flops=ops * targets * CORES * half * states * states * 4,
                bytes_accessed=ops * states * states * 4,
                transcendentals=0,
            ),
        )(*operands)

    def over_op(value, flip):
        return lax.ppermute(value, "op", [(i, i ^ flip) for i in range(op)])


    def per_target(value):
        return value.reshape(-1, half, states)

    ring = []
    for s in range(sec):
        for o in range(op):
            ring.append((s * op + o, (s + 1 if o % CORES == 0 else s - 1) % sec * op + o))
    core = lax.axis_index("op") & (CORES - 1)
    border = lax.dynamic_slice_in_dim(wavefunction, (sectors - 1) * (1 - core), 1, 0)
    halo = lax.ppermute(border, ("sec", "op"), ring)
    left_in = over_op(left_ops, 1)
    right_in = over_op(right_ops, 1)

    small = (charge, couple, amplitude)
    small_in = [over_op(value, 1) for value in small]

    def in_hbm(*values):
        return [pltpu.with_memory_space_constraint(value, pltpu.HBM) for value in values]

    direct_rows = inner // 2 * half
    reduced = shape(inner * half - direct_rows, states)
    direct, keep, send, left, right, cells, *here = run(
        inner_far_kernel,
        operators,
        inner,
        in_hbm(*small, left_ops, right_ops, wavefunction),
        [LARGE] * 6,
        [
            shape(CORES * direct_rows, states, dtype=narrow),
            reduced,
            reduced,
            pltpu.VMEM(left_ops.shape, narrow),
            pltpu.VMEM(right_ops.shape, narrow),
            pltpu.VMEM(wavefunction.shape, narrow),
            *[pltpu.VMEM(value.shape, value.dtype) for value in small],
        ],
        [BLOCK] * 9,
        [
            pltpu.SMEM(charge.shape, charge.dtype),
            pltpu.SMEM(couple.shape, couple.dtype),
            pltpu.SMEM(amplitude.shape, amplitude.dtype),
            pltpu.SemaphoreType.DMA((6,)),
            pltpu.SemaphoreType.DMA((sectors,)),
            pltpu.SemaphoreType.DMA((2, operators)),
            pltpu.SemaphoreType.DMA((operators,)),
        ],
    )
    direct_far = over_op(direct, CORES)
    send_in = over_op(send, 1)

    held = [*here, *small_in, left, right, left_in, right_in]
    held_specs = [SMALL] * 6 + [BLOCK] * 4
    edge_send, sources = run(
        edge_far_kernel,
        CORES * operators,
        EDGE,
        held + [cells, halo],
        held_specs + [BLOCK, BLOCK],
        [shape(CORES * EDGE * half, states, dtype=narrow), shape(EDGE + 2, states, states, dtype=narrow)],
        [BLOCK, BLOCK],
        [pltpu.SemaphoreType.DMA((2,))],
    )
    later = jnp.concatenate([edge_send, (keep + send_in).astype(narrow)], axis=0)
    later_far = over_op(later, CORES)
    edge_rows = EDGE * half
    inner_own, near_own, own_send = run(
        own_kernel,
        CORES * operators,
        EDGE,
        held + [cells, sources],
        held_specs + [BLOCK] * 2,
        [
            shape(inner * half, states),
            shape(edge_rows, states),
            shape(edge_rows + inner * half, states),
        ],
        [BLOCK] * 3,
        [pltpu.VMEM((inner * CORES * half, operators * states), narrow)],
    )
    mate = pl.pallas_call(
        functools.partial(mate_kernel, edge_rows),
        out_shape=shape(*own_send.shape, dtype=narrow),
        in_specs=[BLOCK] * 3,
        out_specs=BLOCK,
        compiler_params=pltpu.CompilerParams(vmem_limit_bytes=4 * MIB),
        name="mate_kernel",
    )(own_send, later_far, direct_far)
    mate = over_op(mate, 1)
    parts = (inner_own, near_own, direct_far, later_far, mate)
    return pl.pallas_call(
        sum_kernel,
        out_shape=shape(sectors, half, states),
        in_specs=[BLOCK] * len(parts),
        out_specs=BLOCK,
        compiler_params=pltpu.CompilerParams(vmem_limit_bytes=16 * MIB),
        name="total",
    )(*[per_target(part) for part in parts])


def solution(mesh):
    placed = (
        P("sec", None, None),
        P("op", None, None),
        P("op", None, None),
        P("op"),
        P("op", "sec"),
        P("op", "sec"),
    )
    two_chips = mesh.shape["op"] == CORES * CORES
    return jax.shard_map(
        shards if two_chips else plain_shards,
        mesh=mesh, in_specs=placed, out_specs=P("sec", "op", None), check_vma=False,
    )
```

```python
import functools

import jax
import jax.numpy as jnp
from jax import lax
from jax.experimental import pallas as pl
from jax.experimental.pallas import tpu as pltpu
from jax.sharding import PartitionSpec as P


CORES = 2
AHEAD = 2
EDGE = 2


def padded(cells, sides, width):
    for axis, dim in sides:
        count = lax.axis_size(axis)
        head = lax.slice_in_dim(cells, 0, width, axis=dim)
        tail = lax.slice_in_dim(cells, cells.shape[dim] - width, cells.shape[dim], axis=dim)
        cells = jnp.concatenate(
            [
                lax.ppermute(tail, axis, [(i, (i + 1) % count) for i in range(count)]),
                cells,
                lax.ppermute(head, axis, [((i + 1) % count, i) for i in range(count)]),
            ],
            axis=dim,
        )
    return cells


def batched(left_op, sources, right_op, factor_values):
    middle = jnp.einsum("ij,sjk->sik", left_op, sources, preferred_element_type=jnp.float32).astype(
        jnp.bfloat16
    )
    contribution = jnp.einsum("sik,lk->sil", middle, right_op, preferred_element_type=jnp.float32)
    return contribution * factor_values[:, None, None]


def plain_shards(wavefunction, left_ops, right_ops, charge, couple, amplitude):
    factor = amplitude * couple.astype(jnp.float32)
    sectors = wavefunction.shape[0]
    states = wavefunction.shape[1]
    extended = padded(wavefunction, (("sec", 0),), 1)

    def accumulate(accumulated, operands):
        left_op, right_op, sector_shift, factor_row = operands
        start = 1 - sector_shift
        sources = lax.dynamic_slice_in_dim(extended, start, sectors, 0)
        return (accumulated + batched(left_op, sources, right_op, factor_row), None)

    initial = jnp.zeros((sectors, states, states), jnp.float32)
    accumulated, _ = lax.scan(accumulate, initial, (left_ops, right_ops, charge, factor))
    return lax.psum_scatter(accumulated, "op", scatter_dimension=1, tiled=True)


def middle_of(k, small, own, left, sources, middles, first_target, targets, chip, core):
    charge, couple, amplitude = small
    states = sources.shape[-1]
    half = middles.shape[0] // (CORES * targets)
    shift = 1 - charge[own]
    wide = jnp.concatenate([sources[shift + t] for t in range(targets)], axis=1)
    rows = jnp.concatenate(
        [left[own, pl.ds(row_of(chip, owner, half), half)] for owner in (core, 1 - core)], axis=0
    )
    middle = jnp.dot(rows, wide, preferred_element_type=jnp.float32)
    for t in range(targets):
        at = first_target + t
        factor = amplitude[own, at] * couple[own, at].astype(jnp.float32)
        block = middle[:, t * states : (t + 1) * states].astype(jnp.bfloat16)
        block = (block.astype(jnp.float32) * factor).astype(jnp.bfloat16)
        for part in range(CORES):
            row = (part * targets + t) * half
            middles[row : row + half, k * states : (k + 1) * states] = block[part * half : (part + 1) * half]


def summed(right, middles, results):
    count = middles.shape[0]
    step = 256
    for low in range(0, count, step):
        high = min(low + step, count)
        total = lax.dot_general(
            right, middles[low:high, :], (((1,), (1,)), ((), ())), preferred_element_type=jnp.float32
        ).T
        first = 0
        for result in results:
            last = first + result.shape[0]
            start, end = max(low, first), min(high, last)
            if start < end:
                result[start - first : end - first, :] = total[start - low : end - low, :].astype(result.dtype)
            first = last


def halves(results):
    width = results.shape[0] // CORES
    return [results.at[pl.ds(part * width, width)] for part in range(CORES)]


def position():
    place = lax.axis_index("op")
    return lax.shift_right_logical(place, CORES - 1), place & (CORES - 1)


def row_of(chip, core, half):
    return pl.multiple_of((chip * CORES + core) * half, 32)


def begin(source, target, sem):
    copy = pltpu.make_async_copy(source, target, sem)
    copy.start()
    return copy


def inner_far_kernel(
    charge, couple, amplitude, left_far, right_far, cells_far,
    direct, keep, send, left, right, cells, charge_kept, couple_kept, amplitude_kept, middles,
    charge_here, couple_here, amplitude_here, small_sem, cell_sem, left_sem, right_sem,
):
    chip, core = position()
    operators = left.shape[0]
    sectors = cells.shape[0]
    targets = sectors - 2 * EDGE
    chip_rows = (direct.shape[0] + keep.shape[0] + send.shape[0]) // targets
    inside = range(EDGE - 1, sectors - EDGE + 1)

    def rows(k, place):
        at = pl.ds(pl.multiple_of(place * chip_rows, 64), chip_rows)
        return left_far.at[k, at], left.at[k, at]

    def cell(s):
        return begin(cells_far.at[s], cells.at[s], cell_sem.at[s])

    small = [
        begin(charge, charge_here, small_sem.at[0]),
        begin(couple, couple_here, small_sem.at[1]),
        begin(amplitude, amplitude_here, small_sem.at[2]),
    ]
    first = [cell(s) for s in inside]
    lefts = [begin(*rows(k, 1 - chip), left_sem.at[0, k]) for k in range(AHEAD)]
    for copy in small:
        copy.wait()
    lefts += [begin(*rows(k, 1 - chip), left_sem.at[0, k]) for k in range(AHEAD, operators)]
    for copy in first + lefts[:AHEAD]:
        copy.wait()
    rights = [begin(right_far.at[k], right.at[k], right_sem.at[k]) for k in range(operators)]
    later = [begin(*rows(k, chip), left_sem.at[1, k]) for k in range(operators)]
    later += [cell(s) for s in range(sectors) if s not in inside]
    later += [
        begin(charge, charge_kept, small_sem.at[3]),
        begin(couple, couple_kept, small_sem.at[4]),
        begin(amplitude, amplitude_kept, small_sem.at[5]),
    ]
    sources = cells.at[pl.ds(EDGE - 1, targets + 2)]
    here = (charge_here, couple_here, amplitude_here)
    for k in range(operators):
        if k == AHEAD:
            for copy in lefts[AHEAD:]:
                copy.wait()
        middle_of(k, here, k, left, sources, middles, EDGE, targets, 1 - chip, core)
    for copy in rights:
        copy.wait()
    near, far = halves(direct)
    summed(jnp.concatenate([right[k] for k in range(operators)], axis=1), middles, (near, keep, far, send))
    for copy in later:
        copy.wait()


def edge_products(groups, sources, middles, results, sectors, chip, core):
    k = 0
    first_target = (sectors - EDGE) * core
    for small, left, right in groups:
        for own in range(left.shape[0]):
            middle_of(k, small, own, left, sources, middles, first_target, EDGE, chip, core)
            k += 1
    wide = jnp.concatenate([right[own] for _, _, right in groups for own in range(right.shape[0])], axis=1)
    summed(wide, middles, results)


def edge_far_kernel(
    charge, couple, amplitude, charge_in, couple_in, amplitude_in, left, right, left_in, right_in,
    cells, halo, send, sources, middles, sem,
):
    chip, core = position()
    sectors = cells.shape[0]
    inside = EDGE + 1
    copies = [
        pltpu.make_async_copy(
            cells.at[pl.ds((sectors - inside) * core, inside)], sources.at[pl.ds(1 - core, inside)], sem.at[0]
        ),
        pltpu.make_async_copy(halo.at[0], sources.at[inside * core], sem.at[1]),
    ]
    for copy in copies:
        copy.start()
    for copy in copies:
        copy.wait()
    groups = (
        ((charge, couple, amplitude), left, right),
        ((charge_in, couple_in, amplitude_in), left_in, right_in),
    )
    edge_products(groups, sources, middles, halves(send), sectors, 1 - chip, core)


def own_kernel(
    charge, couple, amplitude, charge_in, couple_in, amplitude_in, left, right, left_in, right_in,
    cells, sources, inner_keep, edge_keep, send, edge_middles, inner_middles,
):
    chip, core = position()
    sectors = couple.shape[1]
    small = (charge, couple, amplitude)
    inner = sectors - 2 * EDGE
    inside = cells.at[pl.ds(EDGE - 1, inner + 2)]
    for k in range(left.shape[0]):
        middle_of(k, small, k, left, inside, inner_middles, EDGE, inner, chip, core)
    edge_rows = edge_keep.shape[0]
    inner_send = send.at[pl.ds(edge_rows, send.shape[0] - edge_rows)]
    wide = jnp.concatenate([right[k] for k in range(right.shape[0])], axis=1)
    summed(wide, inner_middles, (inner_keep, inner_send))
    groups = ((small, left, right), ((charge_in, couple_in, amplitude_in), left_in, right_in))
    results = (edge_keep, send.at[pl.ds(0, edge_rows)])
    edge_products(groups, sources, edge_middles, results, sectors, chip, core)


def mate_kernel(edge, own, direct_far, mate):
    both = edge + direct_far.shape[0] // CORES
    mate[:edge] = own[:edge].astype(mate.dtype)
    mate[edge:both] = (own[edge:both] + direct_far[both - edge :].astype(jnp.float32)).astype(mate.dtype)
    mate[both:] = own[both:].astype(mate.dtype)


def sum_kernel(inner_own, near_own, direct_far, later_far, mate, passed, sigma):
    core = lax.axis_index("op") & (CORES - 1)
    sectors = sigma.shape[0]
    far = sectors - EDGE
    direct = direct_far.shape[0] // CORES
    split = EDGE + direct

    def wide(value):
        return value.astype(jnp.float32)

    sigma[EDGE:split] = inner_own[:direct] + wide(direct_far[:direct]) + wide(mate[EDGE:split])
    sigma[split:far] = inner_own[direct:] + wide(later_far[CORES * EDGE :]) + wide(mate[split:])
    sigma[pl.ds(far * core, EDGE)] = near_own[...] + wide(later_far[:EDGE])
    sigma[pl.ds(far * (1 - core), EDGE)] = wide(mate[:EDGE]) + wide(passed[...])


SMALL = pl.BlockSpec(memory_space=pltpu.SMEM)
LARGE = pl.BlockSpec(memory_space=pl.ANY)
BLOCK = pl.BlockSpec(memory_space=pltpu.VMEM)
MIB = 1024 * 1024


def shards(wavefunction, left_ops, right_ops, charge, couple, amplitude):
    sec = lax.axis_size("sec")
    op = lax.axis_size("op")
    sectors, states = wavefunction.shape[:2]
    operators = left_ops.shape[0]
    half = states // op
    inner = sectors - 2 * EDGE
    wide, narrow = jnp.float32, jnp.bfloat16

    def shape(*dims, dtype=wide):
        return jax.ShapeDtypeStruct(dims, dtype)

    def run(kernel, ops, targets, operands, in_specs, outs, out_specs, scratch):
        return pl.pallas_call(
            kernel,
            out_shape=outs,
            in_specs=in_specs,
            out_specs=out_specs,
            scratch_shapes=[pltpu.VMEM((targets * CORES * half, ops * states), narrow)] + scratch,
            compiler_params=pltpu.CompilerParams(vmem_limit_bytes=28 * MIB),
            cost_estimate=pl.CostEstimate(
                flops=ops * targets * CORES * half * states * states * 4,
                bytes_accessed=ops * states * states * 4,
                transcendentals=0,
            ),
        )(*operands)

    def over_op(value, flip):
        return lax.ppermute(value, "op", [(i, i ^ flip) for i in range(op)])


    def per_target(value):
        return value.reshape(-1, half, states)

    ring = []
    for s in range(sec):
        for o in range(op):
            ring.append((s * op + o, (s + 1 if o % CORES == 0 else s - 1) % sec * op + o))
    core = lax.axis_index("op") & (CORES - 1)
    border = lax.dynamic_slice_in_dim(wavefunction, (sectors - 1) * (1 - core), 1, 0)
    halo = lax.ppermute(border, ("sec", "op"), ring)
    left_in = over_op(left_ops, 1)
    right_in = over_op(right_ops, 1)

    small = (charge, couple, amplitude)
    small_in = [over_op(value, 1) for value in small]

    def in_hbm(*values):
        return [pltpu.with_memory_space_constraint(value, pltpu.HBM) for value in values]

    direct_rows = inner // 2 * half
    reduced = shape(inner * half - direct_rows, states)
    direct, keep, send, left, right, cells, *here = run(
        inner_far_kernel,
        operators,
        inner,
        in_hbm(*small, left_ops, right_ops, wavefunction),
        [LARGE] * 6,
        [
            shape(CORES * direct_rows, states, dtype=narrow),
            reduced,
            reduced,
            pltpu.VMEM(left_ops.shape, narrow),
            pltpu.VMEM(right_ops.shape, narrow),
            pltpu.VMEM(wavefunction.shape, narrow),
            *[pltpu.VMEM(value.shape, value.dtype) for value in small],
        ],
        [BLOCK] * 9,
        [
            pltpu.SMEM(charge.shape, charge.dtype),
            pltpu.SMEM(couple.shape, couple.dtype),
            pltpu.SMEM(amplitude.shape, amplitude.dtype),
            pltpu.SemaphoreType.DMA((6,)),
            pltpu.SemaphoreType.DMA((sectors,)),
            pltpu.SemaphoreType.DMA((2, operators)),
            pltpu.SemaphoreType.DMA((operators,)),
        ],
    )
    direct_far = over_op(direct, CORES)
    send_in = over_op(send, 1)

    held = [*here, *small_in, left, right, left_in, right_in]
    held_specs = [SMALL] * 6 + [BLOCK] * 4
    edge_send, sources = run(
        edge_far_kernel,
        CORES * operators,
        EDGE,
        held + [cells, halo],
        held_specs + [BLOCK, BLOCK],
        [shape(CORES * EDGE * half, states, dtype=narrow), shape(EDGE + 2, states, states, dtype=narrow)],
        [BLOCK, BLOCK],
        [pltpu.SemaphoreType.DMA((2,))],
    )
    later = jnp.concatenate([edge_send, (keep + send_in).astype(narrow)], axis=0)
    later_far = over_op(later, CORES)
    edge_rows = EDGE * half
    inner_own, near_own, own_send = run(
        own_kernel,
        CORES * operators,
        EDGE,
        held + [cells, sources],
        held_specs + [BLOCK] * 2,
        [
            shape(inner * half, states),
            shape(edge_rows, states),
            shape(edge_rows + inner * half, states),
        ],
        [BLOCK] * 3,
        [pltpu.VMEM((inner * CORES * half, operators * states), narrow)],
    )
    mate = pl.pallas_call(
        functools.partial(mate_kernel, edge_rows),
        out_shape=shape(*own_send.shape, dtype=narrow),
        in_specs=[BLOCK] * 2,
        out_specs=BLOCK,
        compiler_params=pltpu.CompilerParams(vmem_limit_bytes=4 * MIB),
        name="mate_kernel",
    )(own_send, direct_far)
    mate = over_op(mate, 1)
    passed = over_op(later_far[edge_rows : CORES * edge_rows], 1)
    parts = (inner_own, near_own, direct_far, later_far, mate, passed)
    return pl.pallas_call(
        sum_kernel,
        out_shape=shape(sectors, half, states),
        in_specs=[BLOCK] * len(parts),
        out_specs=BLOCK,
        compiler_params=pltpu.CompilerParams(vmem_limit_bytes=16 * MIB),
        name="total",
    )(*[per_target(part) for part in parts])


def solution(mesh):
    placed = (
        P("sec", None, None),
        P("op", None, None),
        P("op", None, None),
        P("op"),
        P("op", "sec"),
        P("op", "sec"),
    )
    two_chips = mesh.shape["op"] == CORES * CORES
    return jax.shard_map(
        shards if two_chips else plain_shards,
        mesh=mesh, in_specs=placed, out_specs=P("sec", "op", None), check_vma=False,
    )
```

```python
import jax
import jax.numpy as jnp
from jax import lax
from jax.experimental import pallas as pl
from jax.experimental.pallas import tpu as pltpu
from jax.sharding import PartitionSpec as P


CORES = 2
AHEAD = 2
EDGE = 2


def padded(cells, sides, width):
    for axis, dim in sides:
        count = lax.axis_size(axis)
        head = lax.slice_in_dim(cells, 0, width, axis=dim)
        tail = lax.slice_in_dim(cells, cells.shape[dim] - width, cells.shape[dim], axis=dim)
        cells = jnp.concatenate(
            [
                lax.ppermute(tail, axis, [(i, (i + 1) % count) for i in range(count)]),
                cells,
                lax.ppermute(head, axis, [((i + 1) % count, i) for i in range(count)]),
            ],
            axis=dim,
        )
    return cells


def batched(left_op, sources, right_op, factor_values):
    middle = jnp.einsum("ij,sjk->sik", left_op, sources, preferred_element_type=jnp.float32).astype(
        jnp.bfloat16
    )
    contribution = jnp.einsum("sik,lk->sil", middle, right_op, preferred_element_type=jnp.float32)
    return contribution * factor_values[:, None, None]


def plain_shards(wavefunction, left_ops, right_ops, charge, couple, amplitude):
    factor = amplitude * couple.astype(jnp.float32)
    sectors = wavefunction.shape[0]
    states = wavefunction.shape[1]
    extended = padded(wavefunction, (("sec", 0),), 1)

    def accumulate(accumulated, operands):
        left_op, right_op, sector_shift, factor_row = operands
        start = 1 - sector_shift
        sources = lax.dynamic_slice_in_dim(extended, start, sectors, 0)
        return (accumulated + batched(left_op, sources, right_op, factor_row), None)

    initial = jnp.zeros((sectors, states, states), jnp.float32)
    accumulated, _ = lax.scan(accumulate, initial, (left_ops, right_ops, charge, factor))
    return lax.psum_scatter(accumulated, "op", scatter_dimension=1, tiled=True)


def middle_of(k, table, own, left, sources, middles, first_target, targets, chip, core):
    states = sources.shape[-1]
    half = middles.shape[0] // (CORES * targets)
    shift = 1 - table[table.shape[0] - 1, own].astype(jnp.int32)
    wide = jnp.concatenate([sources[shift + t] for t in range(targets)], axis=1)
    rows = jnp.concatenate(
        [left[own, pl.ds(row_of(chip, owner, half), half)] for owner in (core, 1 - core)], axis=0
    )
    middle = jnp.dot(rows, wide, preferred_element_type=jnp.float32)
    for t in range(targets):
        factor = table[own, first_target + t]
        block = middle[:, t * states : (t + 1) * states].astype(jnp.bfloat16)
        block = (block.astype(jnp.float32) * factor).astype(jnp.bfloat16)
        for part in range(CORES):
            row = (part * targets + t) * half
            middles[row : row + half, k * states : (k + 1) * states] = block[part * half : (part + 1) * half]


def summed(right, middles, results):
    count = middles.shape[0]
    step = 256
    for low in range(0, count, step):
        high = min(low + step, count)
        total = lax.dot_general(
            right, middles[low:high, :], (((1,), (1,)), ((), ())), preferred_element_type=jnp.float32
        ).T
        first = 0
        for result in results:
            last = first + result.shape[0]
            start, end = max(low, first), min(high, last)
            if start < end:
                result[start - first : end - first, :] = total[start - low : end - low, :].astype(result.dtype)
            first = last


def halves(results):
    width = results.shape[0] // CORES
    return [results.at[pl.ds(part * width, width)] for part in range(CORES)]


def position():
    place = lax.axis_index("op")
    return lax.shift_right_logical(place, CORES - 1), place & (CORES - 1)


def row_of(chip, core, half):
    return pl.multiple_of((chip * CORES + core) * half, 32)


def begin(source, target, sem):
    copy = pltpu.make_async_copy(source, target, sem)
    copy.start()
    return copy


def first_kernel(
    charge, couple, amplitude, cells_far, border, table, charge_here, couple_here, amplitude_here, sem
):
    _, core = position()
    operators, sectors = couple.shape
    copies = [
        begin(charge, charge_here.at[0], sem.at[0]),
        begin(couple, couple_here, sem.at[1]),
        begin(amplitude, amplitude_here, sem.at[2]),
        begin(cells_far.at[(sectors - 1) * (1 - core)], border.at[0], sem.at[3]),
    ]
    for copy in copies:
        copy.wait()
    table[:operators, :sectors] = amplitude_here[...] * couple_here[...].astype(jnp.float32)
    table[operators:, :operators] = charge_here[...].astype(jnp.float32)


def inner_far_kernel(
    table, left_far, right_far, cells_far, direct, keep, send, left, right, cells, middles,
    cell_sem, left_sem, right_sem,
):
    chip, core = position()
    operators = left.shape[0]
    sectors = cells.shape[0]
    targets = sectors - 2 * EDGE
    chip_rows = (direct.shape[0] + keep.shape[0] + send.shape[0]) // targets
    inside = range(EDGE - 1, sectors - EDGE + 1)

    def rows(k, place):
        at = pl.ds(pl.multiple_of(place * chip_rows, 64), chip_rows)
        return left_far.at[k, at], left.at[k, at]

    def cell(s):
        return begin(cells_far.at[s], cells.at[s], cell_sem.at[s])

    first = [cell(s) for s in inside]
    lefts = [begin(*rows(k, 1 - chip), left_sem.at[0, k]) for k in range(operators)]
    for copy in first + lefts[:AHEAD]:
        copy.wait()
    rights = [begin(right_far.at[k], right.at[k], right_sem.at[k]) for k in range(operators)]
    later = [begin(*rows(k, chip), left_sem.at[1, k]) for k in range(operators)]
    later += [cell(s) for s in range(sectors) if s not in inside]
    sources = cells.at[pl.ds(EDGE - 1, targets + 2)]
    for k in range(operators):
        if k == AHEAD:
            for copy in lefts[AHEAD:]:
                copy.wait()
        middle_of(k, table, k, left, sources, middles, EDGE, targets, 1 - chip, core)
    for copy in rights:
        copy.wait()
    near, far = halves(direct)
    summed(jnp.concatenate([right[k] for k in range(operators)], axis=1), middles, (near, keep, far, send))
    for copy in later:
        copy.wait()


def inner_own_kernel(table, left, right, cells, keep, send, middles):
    chip, core = position()
    operators = left.shape[0]
    targets = cells.shape[0] - 2 * EDGE
    inside = cells.at[pl.ds(EDGE - 1, targets + 2)]
    for k in range(operators):
        middle_of(k, table, k, left, inside, middles, EDGE, targets, chip, core)
    summed(jnp.concatenate([right[k] for k in range(operators)], axis=1), middles, (keep, send))


def edge_products(groups, sources, middles, results, sectors, chip, core):
    k = 0
    first_target = (sectors - EDGE) * core
    for table, left, right in groups:
        for own in range(left.shape[0]):
            middle_of(k, table, own, left, sources, middles, first_target, EDGE, chip, core)
            k += 1
    wide = jnp.concatenate([right[own] for _, _, right in groups for own in range(right.shape[0])], axis=1)
    summed(wide, middles, results)


def edge_far_kernel(
    table, table_in, left, right, left_in, right_in, cells, halo, send, sources, middles, sem,
):
    chip, core = position()
    sectors = cells.shape[0]
    inside = EDGE + 1
    copies = [
        pltpu.make_async_copy(
            cells.at[pl.ds((sectors - inside) * core, inside)], sources.at[pl.ds(1 - core, inside)], sem.at[0]
        ),
        pltpu.make_async_copy(halo.at[0], sources.at[inside * core], sem.at[1]),
    ]
    for copy in copies:
        copy.start()
    for copy in copies:
        copy.wait()
    groups = ((table, left, right), (table_in, left_in, right_in))
    edge_products(groups, sources, middles, halves(send), sectors, 1 - chip, core)


def edge_own(
    sectors, table, table_in, left, right, left_in, right_in, sources, keep, send, middles
):
    chip, core = position()
    groups = ((table, left, right), (table_in, left_in, right_in))
    edge_products(groups, sources, middles, (keep, send), sectors, chip, core)


def sum_kernel(inner_own, inner_chip, direct_far, later_far, near_own, other, sigma):
    core = lax.axis_index("op") & (CORES - 1)
    sectors = sigma.shape[0]
    far = sectors - EDGE
    split = EDGE + direct_far.shape[0] // CORES
    direct = split - EDGE
    sigma[EDGE:split] = inner_own[:direct] + inner_chip[:direct] + direct_far[:direct].astype(jnp.float32)
    sigma[split:far] = inner_own[direct:] + inner_chip[direct:] + later_far[CORES * EDGE :].astype(jnp.float32)
    sigma[pl.ds(far * core, EDGE)] = near_own[...] + later_far[:EDGE].astype(jnp.float32)
    sigma[pl.ds(far * (1 - core), EDGE)] = other[...]


SMALL = pl.BlockSpec(memory_space=pltpu.SMEM)
LARGE = pl.BlockSpec(memory_space=pl.ANY)
BLOCK = pl.BlockSpec(memory_space=pltpu.VMEM)
MIB = 1024 * 1024


def shards(wavefunction, left_ops, right_ops, charge, couple, amplitude):
    sec = lax.axis_size("sec")
    op = lax.axis_size("op")
    sectors, states = wavefunction.shape[:2]
    operators = left_ops.shape[0]
    half = states // op
    inner = sectors - 2 * EDGE
    wide, narrow = jnp.float32, jnp.bfloat16

    def shape(*dims, dtype=wide):
        return jax.ShapeDtypeStruct(dims, dtype)

    def run(kernel, ops, targets, operands, in_specs, outs, out_specs, scratch):
        return pl.pallas_call(
            kernel,
            out_shape=outs,
            in_specs=in_specs,
            out_specs=out_specs,
            scratch_shapes=[pltpu.VMEM((targets * CORES * half, ops * states), narrow)] + scratch,
            compiler_params=pltpu.CompilerParams(vmem_limit_bytes=20 * MIB),
            cost_estimate=pl.CostEstimate(
                flops=ops * targets * CORES * half * states * states * 4,
                bytes_accessed=ops * states * states * 4,
                transcendentals=0,
            ),
        )(*operands)

    def over_op(value, flip):
        return lax.ppermute(value, "op", [(i, i ^ flip) for i in range(op)])


    def per_target(value):
        return value.reshape(-1, half, states)

    ring = []
    for s in range(sec):
        for o in range(op):
            ring.append((s * op + o, (s + 1 if o % CORES == 0 else s - 1) % sec * op + o))

    def in_hbm(*values):
        return [pltpu.with_memory_space_constraint(value, pltpu.HBM) for value in values]

    border, table = pl.pallas_call(
        first_kernel,
        out_shape=[
            pltpu.VMEM((1, states, states), narrow),
            pltpu.VMEM((operators + 1, max(operators, sectors)), wide),
        ],
        in_specs=[LARGE] * 4,
        out_specs=[BLOCK] * 2,
        scratch_shapes=[
            pltpu.VMEM((1, operators), charge.dtype),
            pltpu.VMEM(couple.shape, couple.dtype),
            pltpu.VMEM(amplitude.shape, amplitude.dtype),
            pltpu.SemaphoreType.DMA((4,)),
        ],
        compiler_params=pltpu.CompilerParams(vmem_limit_bytes=4 * MIB),
        name="first_kernel",
    )(*in_hbm(charge, couple, amplitude, wavefunction))
    halo = lax.ppermute(border, ("sec", "op"), ring)
    left_in = over_op(left_ops, 1)
    right_in = over_op(right_ops, 1)

    table_in = over_op(table, 1)

    direct_rows = inner // 2 * half
    reduced = shape(inner * half - direct_rows, states)
    direct, keep, send, left, right, cells = run(
        inner_far_kernel,
        operators,
        inner,
        [table, *in_hbm(left_ops, right_ops, wavefunction)],
        [SMALL] + [LARGE] * 3,
        [
            shape(CORES * direct_rows, states, dtype=narrow),
            reduced,
            reduced,
            pltpu.VMEM(left_ops.shape, narrow),
            pltpu.VMEM(right_ops.shape, narrow),
            pltpu.VMEM(wavefunction.shape, narrow),
        ],
        [BLOCK] * 6,
        [
            pltpu.SemaphoreType.DMA((sectors,)),
            pltpu.SemaphoreType.DMA((2, operators)),
            pltpu.SemaphoreType.DMA((operators,)),
        ],
    )
    direct_far = over_op(direct, CORES)
    send_in = over_op(send, 1)

    held = [table, table_in, left, right, left_in, right_in]
    held_specs = [SMALL] * 2 + [BLOCK] * 4
    edge_send, sources = run(
        edge_far_kernel,
        CORES * operators,
        EDGE,
        held + [cells, halo],
        held_specs + [BLOCK, BLOCK],
        [shape(CORES * EDGE * half, states, dtype=narrow), shape(EDGE + 2, states, states, dtype=narrow)],
        [BLOCK, BLOCK],
        [pltpu.SemaphoreType.DMA((2,))],
    )
    later = jnp.concatenate([edge_send, (keep + send_in).astype(narrow)], axis=0)
    later_far = over_op(later, CORES)
    block = shape(inner * half, states)
    inner_own, inner_send = run(
        inner_own_kernel,
        operators,
        inner,
        [table, left, right, cells],
        [SMALL] + [BLOCK] * 3,
        [block, block],
        [BLOCK, BLOCK],
        [],
    )
    mate = inner_send[:direct_rows] + direct_far[direct_rows:].astype(wide)
    inner_chip = over_op(jnp.concatenate([mate, inner_send[direct_rows:]], axis=0), 1)
    edge_wide = shape(EDGE * half, states)

    def edge_own_kernel(*refs):
        edge_own(sectors, *refs)

    near_own, near_mate = run(
        edge_own_kernel,
        CORES * operators,
        EDGE,
        held + [sources],
        held_specs + [BLOCK],
        [edge_wide, edge_wide],
        [BLOCK, BLOCK],
        [],
    )
    passed = later_far[EDGE * half : CORES * EDGE * half].astype(wide)
    other = over_op(near_mate + passed, 1)
    parts = (inner_own, inner_chip, direct_far, later_far, near_own, other)
    return pl.pallas_call(
        sum_kernel,
        out_shape=shape(sectors, half, states),
        in_specs=[BLOCK] * len(parts),
        out_specs=BLOCK,
        compiler_params=pltpu.CompilerParams(vmem_limit_bytes=16 * MIB),
        name="total",
    )(*[per_target(part) for part in parts])


def solution(mesh):
    placed = (
        P("sec", None, None),
        P("op", None, None),
        P("op", None, None),
        P("op"),
        P("op", "sec"),
        P("op", "sec"),
    )
    two_chips = mesh.shape["op"] == CORES * CORES
    return jax.shard_map(
        shards if two_chips else plain_shards,
        mesh=mesh, in_specs=placed, out_specs=P("sec", "op", None), check_vma=False,
    )
```

```python
import jax
import jax.numpy as jnp
from jax import lax
from jax.experimental import pallas as pl
from jax.experimental.pallas import tpu as pltpu
from jax.sharding import PartitionSpec as P


CORES = 2
AHEAD = 2
EDGE = 2


def padded(cells, sides, width):
    for axis, dim in sides:
        count = lax.axis_size(axis)
        head = lax.slice_in_dim(cells, 0, width, axis=dim)
        tail = lax.slice_in_dim(cells, cells.shape[dim] - width, cells.shape[dim], axis=dim)
        cells = jnp.concatenate(
            [
                lax.ppermute(tail, axis, [(i, (i + 1) % count) for i in range(count)]),
                cells,
                lax.ppermute(head, axis, [((i + 1) % count, i) for i in range(count)]),
            ],
            axis=dim,
        )
    return cells


def batched(left_op, sources, right_op, factor_values):
    middle = jnp.einsum("ij,sjk->sik", left_op, sources, preferred_element_type=jnp.float32).astype(
        jnp.bfloat16
    )
    contribution = jnp.einsum("sik,lk->sil", middle, right_op, preferred_element_type=jnp.float32)
    return contribution * factor_values[:, None, None]


def plain_shards(wavefunction, left_ops, right_ops, charge, couple, amplitude):
    factor = amplitude * couple.astype(jnp.float32)
    sectors = wavefunction.shape[0]
    states = wavefunction.shape[1]
    extended = padded(wavefunction, (("sec", 0),), 1)

    def accumulate(accumulated, operands):
        left_op, right_op, sector_shift, factor_row = operands
        start = 1 - sector_shift
        sources = lax.dynamic_slice_in_dim(extended, start, sectors, 0)
        return (accumulated + batched(left_op, sources, right_op, factor_row), None)

    initial = jnp.zeros((sectors, states, states), jnp.float32)
    accumulated, _ = lax.scan(accumulate, initial, (left_ops, right_ops, charge, factor))
    return lax.psum_scatter(accumulated, "op", scatter_dimension=1, tiled=True)


def middle_of(k, table, own, left, sources, middles, first_target, targets, chip, core):
    states = sources.shape[-1]
    half = middles.shape[0] // (CORES * targets)
    shift = 1 - table[table.shape[0] - 1, own].astype(jnp.int32)
    wide = jnp.concatenate([sources[shift + t] for t in range(targets)], axis=1)
    rows = jnp.concatenate(
        [left[own, pl.ds(row_of(chip, owner, half), half)] for owner in (core, 1 - core)], axis=0
    )
    middle = jnp.dot(rows, wide, preferred_element_type=jnp.float32)
    for t in range(targets):
        factor = table[own, first_target + t]
        block = middle[:, t * states : (t + 1) * states].astype(jnp.bfloat16)
        block = (block.astype(jnp.float32) * factor).astype(jnp.bfloat16)
        for part in range(CORES):
            row = (part * targets + t) * half
            middles[row : row + half, k * states : (k + 1) * states] = block[part * half : (part + 1) * half]


def summed(right, middles, results):
    count = middles.shape[0]
    step = 256
    for low in range(0, count, step):
        high = min(low + step, count)
        total = lax.dot_general(
            right, middles[low:high, :], (((1,), (1,)), ((), ())), preferred_element_type=jnp.float32
        ).T
        first = 0
        for result in results:
            last = first + result.shape[0]
            start, end = max(low, first), min(high, last)
            if start < end:
                result[start - first : end - first, :] = total[start - low : end - low, :].astype(result.dtype)
            first = last


def halves(results):
    width = results.shape[0] // CORES
    return [results.at[pl.ds(part * width, width)] for part in range(CORES)]


def position():
    place = lax.axis_index("op")
    return lax.shift_right_logical(place, CORES - 1), place & (CORES - 1)


def row_of(chip, core, half):
    return pl.multiple_of((chip * CORES + core) * half, 32)


def begin(source, target, sem):
    copy = pltpu.make_async_copy(source, target, sem)
    copy.start()
    return copy


def first_kernel(
    charge, couple, amplitude, cells_far, border, table, charge_here, couple_here, amplitude_here, sem
):
    _, core = position()
    operators, sectors = couple.shape
    copies = [
        begin(charge, charge_here.at[0], sem.at[0]),
        begin(couple, couple_here, sem.at[1]),
        begin(amplitude, amplitude_here, sem.at[2]),
        begin(cells_far.at[(sectors - 1) * (1 - core)], border.at[0], sem.at[3]),
    ]
    for copy in copies:
        copy.wait()
    table[:operators, :sectors] = amplitude_here[...] * couple_here[...].astype(jnp.float32)
    table[operators:, :operators] = charge_here[...].astype(jnp.float32)


def inner_far_kernel(
    table_kept, left_far, right_far, cells_far, direct, keep, send, left, right, cells, middles,
    table, table_sem, cell_sem, left_sem, right_sem,
):
    chip, core = position()
    operators = left.shape[0]
    sectors = cells.shape[0]
    targets = sectors - 2 * EDGE
    chip_rows = (direct.shape[0] + keep.shape[0] + send.shape[0]) // targets
    inside = range(EDGE - 1, sectors - EDGE + 1)

    def rows(k, place):
        at = pl.ds(pl.multiple_of(place * chip_rows, 64), chip_rows)
        return left_far.at[k, at], left.at[k, at]

    def cell(s):
        return begin(cells_far.at[s], cells.at[s], cell_sem.at[s])

    first = [cell(s) for s in inside]
    lefts = [begin(*rows(k, 1 - chip), left_sem.at[0, k]) for k in range(AHEAD)]
    begin(table_kept, table, table_sem).wait()
    most = len(first) // 2 + 1
    for copy in first[:most]:
        copy.wait()
    lefts += [begin(*rows(k, 1 - chip), left_sem.at[0, k]) for k in range(AHEAD, operators)]
    for copy in first[most:] + lefts[:AHEAD]:
        copy.wait()
    rights = [begin(right_far.at[k], right.at[k], right_sem.at[k]) for k in range(operators)]
    later = [begin(*rows(k, chip), left_sem.at[1, k]) for k in range(operators)]
    later += [cell(s) for s in range(sectors) if s not in inside]
    sources = cells.at[pl.ds(EDGE - 1, targets + 2)]
    for k in range(operators):
        if k == AHEAD:
            for copy in lefts[AHEAD:]:
                copy.wait()
        middle_of(k, table, k, left, sources, middles, EDGE, targets, 1 - chip, core)
    for copy in rights:
        copy.wait()
    near, far = halves(direct)
    summed(jnp.concatenate([right[k] for k in range(operators)], axis=1), middles, (near, keep, far, send))
    for copy in later:
        copy.wait()


def inner_own_kernel(table, left, right, cells, keep, send, middles):
    chip, core = position()
    operators = left.shape[0]
    targets = cells.shape[0] - 2 * EDGE
    inside = cells.at[pl.ds(EDGE - 1, targets + 2)]
    for k in range(operators):
        middle_of(k, table, k, left, inside, middles, EDGE, targets, chip, core)
    summed(jnp.concatenate([right[k] for k in range(operators)], axis=1), middles, (keep, send))


def edge_products(groups, sources, middles, results, sectors, chip, core):
    k = 0
    first_target = (sectors - EDGE) * core
    for table, left, right in groups:
        for own in range(left.shape[0]):
            middle_of(k, table, own, left, sources, middles, first_target, EDGE, chip, core)
            k += 1
    wide = jnp.concatenate([right[own] for _, _, right in groups for own in range(right.shape[0])], axis=1)
    summed(wide, middles, results)


def edge_far_kernel(
    table, table_in, left, right, left_in, right_in, cells, halo, send, sources, middles, sem,
):
    chip, core = position()
    sectors = cells.shape[0]
    inside = EDGE + 1
    copies = [
        pltpu.make_async_copy(
            cells.at[pl.ds((sectors - inside) * core, inside)], sources.at[pl.ds(1 - core, inside)], sem.at[0]
        ),
        pltpu.make_async_copy(halo.at[0], sources.at[inside * core], sem.at[1]),
    ]
    for copy in copies:
        copy.start()
    for copy in copies:
        copy.wait()
    groups = ((table, left, right), (table_in, left_in, right_in))
    edge_products(groups, sources, middles, halves(send), sectors, 1 - chip, core)


def edge_own(
    sectors, table, table_in, left, right, left_in, right_in, sources, keep, send, middles
):
    chip, core = position()
    groups = ((table, left, right), (table_in, left_in, right_in))
    edge_products(groups, sources, middles, (keep, send), sectors, chip, core)


def sum_kernel(inner_own, inner_chip, direct_far, later_far, near_own, other, sigma):
    core = lax.axis_index("op") & (CORES - 1)
    sectors = sigma.shape[0]
    far = sectors - EDGE
    split = EDGE + direct_far.shape[0] // CORES
    direct = split - EDGE
    sigma[EDGE:split] = inner_own[:direct] + inner_chip[:direct] + direct_far[:direct].astype(jnp.float32)
    sigma[split:far] = inner_own[direct:] + inner_chip[direct:] + later_far[CORES * EDGE :].astype(jnp.float32)
    sigma[pl.ds(far * core, EDGE)] = near_own[...] + later_far[:EDGE].astype(jnp.float32)
    sigma[pl.ds(far * (1 - core), EDGE)] = other[...]


SMALL = pl.BlockSpec(memory_space=pltpu.SMEM)
LARGE = pl.BlockSpec(memory_space=pl.ANY)
BLOCK = pl.BlockSpec(memory_space=pltpu.VMEM)
MIB = 1024 * 1024


def shards(wavefunction, left_ops, right_ops, charge, couple, amplitude):
    sec = lax.axis_size("sec")
    op = lax.axis_size("op")
    sectors, states = wavefunction.shape[:2]
    operators = left_ops.shape[0]
    half = states // op
    inner = sectors - 2 * EDGE
    wide, narrow = jnp.float32, jnp.bfloat16

    def shape(*dims, dtype=wide):
        return jax.ShapeDtypeStruct(dims, dtype)

    def run(kernel, ops, targets, operands, in_specs, outs, out_specs, scratch):
        return pl.pallas_call(
            kernel,
            out_shape=outs,
            in_specs=in_specs,
            out_specs=out_specs,
            scratch_shapes=[pltpu.VMEM((targets * CORES * half, ops * states), narrow)] + scratch,
            compiler_params=pltpu.CompilerParams(vmem_limit_bytes=20 * MIB),
            cost_estimate=pl.CostEstimate(
                flops=ops * targets * CORES * half * states * states * 4,
                bytes_accessed=ops * states * states * 4,
                transcendentals=0,
            ),
        )(*operands)

    def over_op(value, flip):
        return lax.ppermute(value, "op", [(i, i ^ flip) for i in range(op)])


    def per_target(value):
        return value.reshape(-1, half, states)

    ring = []
    for s in range(sec):
        for o in range(op):
            ring.append((s * op + o, (s + 1 if o % CORES == 0 else s - 1) % sec * op + o))

    def in_hbm(*values):
        return [pltpu.with_memory_space_constraint(value, pltpu.HBM) for value in values]

    border, table = pl.pallas_call(
        first_kernel,
        out_shape=[
            pltpu.VMEM((1, states, states), narrow),
            pltpu.VMEM((operators + 1, max(operators, sectors)), wide),
        ],
        in_specs=[LARGE] * 4,
        out_specs=[BLOCK] * 2,
        scratch_shapes=[
            pltpu.VMEM((1, operators), charge.dtype),
            pltpu.VMEM(couple.shape, couple.dtype),
            pltpu.VMEM(amplitude.shape, amplitude.dtype),
            pltpu.SemaphoreType.DMA((4,)),
        ],
        compiler_params=pltpu.CompilerParams(vmem_limit_bytes=4 * MIB),
        name="first_kernel",
    )(*in_hbm(charge, couple, amplitude, wavefunction))
    halo = lax.ppermute(border, ("sec", "op"), ring)
    left_in = over_op(left_ops, 1)
    right_in = over_op(right_ops, 1)

    table_in = over_op(table, 1)

    direct_rows = inner // 2 * half
    reduced = shape(inner * half - direct_rows, states)
    direct, keep, send, left, right, cells = run(
        inner_far_kernel,
        operators,
        inner,
        [table, *in_hbm(left_ops, right_ops, wavefunction)],
        [BLOCK] + [LARGE] * 3,
        [
            shape(CORES * direct_rows, states, dtype=narrow),
            reduced,
            reduced,
            pltpu.VMEM(left_ops.shape, narrow),
            pltpu.VMEM(right_ops.shape, narrow),
            pltpu.VMEM(wavefunction.shape, narrow),
        ],
        [BLOCK] * 6,
        [
            pltpu.SMEM(table.shape, table.dtype),
            pltpu.SemaphoreType.DMA,
            pltpu.SemaphoreType.DMA((sectors,)),
            pltpu.SemaphoreType.DMA((2, operators)),
            pltpu.SemaphoreType.DMA((operators,)),
        ],
    )
    direct_far = over_op(direct, CORES)
    send_in = over_op(send, 1)

    held = [table, table_in, left, right, left_in, right_in]
    held_specs = [SMALL] * 2 + [BLOCK] * 4
    edge_send, sources = run(
        edge_far_kernel,
        CORES * operators,
        EDGE,
        held + [cells, halo],
        held_specs + [BLOCK, BLOCK],
        [shape(CORES * EDGE * half, states, dtype=narrow), shape(EDGE + 2, states, states, dtype=narrow)],
        [BLOCK, BLOCK],
        [pltpu.SemaphoreType.DMA((2,))],
    )
    later = jnp.concatenate([edge_send, (keep + send_in).astype(narrow)], axis=0)
    later_far = over_op(later, CORES)
    block = shape(inner * half, states)
    inner_own, inner_send = run(
        inner_own_kernel,
        operators,
        inner,
        [table, left, right, cells],
        [SMALL] + [BLOCK] * 3,
        [block, block],
        [BLOCK, BLOCK],
        [],
    )
    mate = inner_send[:direct_rows] + direct_far[direct_rows:].astype(wide)
    inner_chip = over_op(jnp.concatenate([mate, inner_send[direct_rows:]], axis=0), 1)
    edge_wide = shape(EDGE * half, states)

    def edge_own_kernel(*refs):
        edge_own(sectors, *refs)

    near_own, near_mate = run(
        edge_own_kernel,
        CORES * operators,
        EDGE,
        held + [sources],
        held_specs + [BLOCK],
        [edge_wide, edge_wide],
        [BLOCK, BLOCK],
        [],
    )
    passed = later_far[EDGE * half : CORES * EDGE * half].astype(wide)
    other = over_op(near_mate + passed, 1)
    parts = (inner_own, inner_chip, direct_far, later_far, near_own, other)
    return pl.pallas_call(
        sum_kernel,
        out_shape=shape(sectors, half, states),
        in_specs=[BLOCK] * len(parts),
        out_specs=BLOCK,
        compiler_params=pltpu.CompilerParams(vmem_limit_bytes=16 * MIB),
        name="total",
    )(*[per_target(part) for part in parts])


def solution(mesh):
    placed = (
        P("sec", None, None),
        P("op", None, None),
        P("op", None, None),
        P("op"),
        P("op", "sec"),
        P("op", "sec"),
    )
    two_chips = mesh.shape["op"] == CORES * CORES
    return jax.shard_map(
        shards if two_chips else plain_shards,
        mesh=mesh, in_specs=placed, out_specs=P("sec", "op", None), check_vma=False,
    )
```

```python
import jax
import jax.numpy as jnp
from jax import lax
from jax.experimental import pallas as pl
from jax.experimental.pallas import tpu as pltpu
from jax.sharding import PartitionSpec as P


CORES = 2
EDGE = 2


def padded(cells, sides, width):
    for axis, dim in sides:
        count = lax.axis_size(axis)
        head = lax.slice_in_dim(cells, 0, width, axis=dim)
        tail = lax.slice_in_dim(cells, cells.shape[dim] - width, cells.shape[dim], axis=dim)
        cells = jnp.concatenate(
            [
                lax.ppermute(tail, axis, [(i, (i + 1) % count) for i in range(count)]),
                cells,
                lax.ppermute(head, axis, [((i + 1) % count, i) for i in range(count)]),
            ],
            axis=dim,
        )
    return cells


def batched(left_op, sources, right_op, factor_values):
    middle = jnp.einsum("ij,sjk->sik", left_op, sources, preferred_element_type=jnp.float32).astype(
        jnp.bfloat16
    )
    contribution = jnp.einsum("sik,lk->sil", middle, right_op, preferred_element_type=jnp.float32)
    return contribution * factor_values[:, None, None]


def plain_shards(wavefunction, left_ops, right_ops, charge, couple, amplitude):
    factor = amplitude * couple.astype(jnp.float32)
    sectors = wavefunction.shape[0]
    states = wavefunction.shape[1]
    extended = padded(wavefunction, (("sec", 0),), 1)

    def accumulate(accumulated, operands):
        left_op, right_op, sector_shift, factor_row = operands
        start = 1 - sector_shift
        sources = lax.dynamic_slice_in_dim(extended, start, sectors, 0)
        return (accumulated + batched(left_op, sources, right_op, factor_row), None)

    initial = jnp.zeros((sectors, states, states), jnp.float32)
    accumulated, _ = lax.scan(accumulate, initial, (left_ops, right_ops, charge, factor))
    return lax.psum_scatter(accumulated, "op", scatter_dimension=1, tiled=True)


def middle_of(k, table, own, left, sources, middles, first_target, targets, chip, core):
    states = sources.shape[-1]
    half = middles.shape[0] // (CORES * targets)
    shift = 1 - table[table.shape[0] - 1, own].astype(jnp.int32)
    wide = jnp.concatenate([sources[shift + t] for t in range(targets)], axis=1)
    rows = jnp.concatenate(
        [left[own, pl.ds(row_of(chip, owner, half), half)] for owner in (core, 1 - core)], axis=0
    )
    middle = jnp.dot(rows, wide, preferred_element_type=jnp.float32)
    for t in range(targets):
        factor = table[own, first_target + t]
        block = middle[:, t * states : (t + 1) * states].astype(jnp.bfloat16)
        block = (block.astype(jnp.float32) * factor).astype(jnp.bfloat16)
        for part in range(CORES):
            row = (part * targets + t) * half
            middles[row : row + half, k * states : (k + 1) * states] = block[part * half : (part + 1) * half]


def summed(right, middles, results):
    count = middles.shape[0]
    step = 256
    for low in range(0, count, step):
        high = min(low + step, count)
        total = lax.dot_general(
            right, middles[low:high, :], (((1,), (1,)), ((), ())), preferred_element_type=jnp.float32
        ).T
        first = 0
        for result in results:
            last = first + result.shape[0]
            start, end = max(low, first), min(high, last)
            if start < end:
                result[start - first : end - first, :] = total[start - low : end - low, :].astype(result.dtype)
            first = last


def halves(results):
    width = results.shape[0] // CORES
    return [results.at[pl.ds(part * width, width)] for part in range(CORES)]


def position():
    place = lax.axis_index("op")
    return lax.shift_right_logical(place, CORES - 1), place & (CORES - 1)


def row_of(chip, core, half):
    return pl.multiple_of((chip * CORES + core) * half, 32)


def begin(source, target, sem):
    copy = pltpu.make_async_copy(source, target, sem)
    copy.start()
    return copy


def first_kernel(
    charge, couple, amplitude, cells_far, border, table, charge_here, couple_here, amplitude_here, sem
):
    _, core = position()
    operators, sectors = couple.shape
    copies = [
        begin(charge, charge_here.at[0], sem.at[0]),
        begin(couple, couple_here, sem.at[1]),
        begin(amplitude, amplitude_here, sem.at[2]),
        begin(cells_far.at[(sectors - 1) * (1 - core)], border.at[0], sem.at[3]),
    ]
    for copy in copies:
        copy.wait()
    table[:operators, :sectors] = amplitude_here[...] * couple_here[...].astype(jnp.float32)
    table[operators:, :operators] = charge_here[...].astype(jnp.float32)


def inner_far_kernel(
    table_kept, left, right_far, cells_far, direct, keep, send, right, cells, middles,
    table, table_sem, cell_sem, right_sem,
):
    chip, core = position()
    operators = left.shape[0]
    sectors = cells.shape[0]
    targets = sectors - 2 * EDGE
    inside = range(EDGE - 1, sectors - EDGE + 1)

    def cell(s):
        return begin(cells_far.at[s], cells.at[s], cell_sem.at[s])

    first = [cell(s) for s in inside]
    begin(table_kept, table, table_sem).wait()
    for copy in first[:-1]:
        copy.wait()
    rights = [begin(right_far.at[k], right.at[k], right_sem.at[k]) for k in range(operators)]
    later = [cell(s) for s in range(sectors) if s not in inside]
    first[-1].wait()
    sources = cells.at[pl.ds(EDGE - 1, targets + 2)]
    for k in range(operators):
        middle_of(k, table, k, left, sources, middles, EDGE, targets, 1 - chip, core)
    for copy in rights:
        copy.wait()
    near, far = halves(direct)
    summed(jnp.concatenate([right[k] for k in range(operators)], axis=1), middles, (near, keep, far, send))
    for copy in later:
        copy.wait()


def inner_own_kernel(table, left, right, cells, keep, send, middles):
    chip, core = position()
    operators = left.shape[0]
    targets = cells.shape[0] - 2 * EDGE
    inside = cells.at[pl.ds(EDGE - 1, targets + 2)]
    for k in range(operators):
        middle_of(k, table, k, left, inside, middles, EDGE, targets, chip, core)
    summed(jnp.concatenate([right[k] for k in range(operators)], axis=1), middles, (keep, send))


def edge_products(groups, sources, middles, results, sectors, chip, core):
    k = 0
    first_target = (sectors - EDGE) * core
    for table, left, right in groups:
        for own in range(left.shape[0]):
            middle_of(k, table, own, left, sources, middles, first_target, EDGE, chip, core)
            k += 1
    wide = jnp.concatenate([right[own] for _, _, right in groups for own in range(right.shape[0])], axis=1)
    summed(wide, middles, results)


def edge_far_kernel(
    table, table_in, left, right, left_in, right_in, cells, halo, send, sources, middles, sem,
):
    chip, core = position()
    sectors = cells.shape[0]
    inside = EDGE + 1
    copies = [
        pltpu.make_async_copy(
            cells.at[pl.ds((sectors - inside) * core, inside)], sources.at[pl.ds(1 - core, inside)], sem.at[0]
        ),
        pltpu.make_async_copy(halo.at[0], sources.at[inside * core], sem.at[1]),
    ]
    for copy in copies:
        copy.start()
    for copy in copies:
        copy.wait()
    groups = ((table, left, right), (table_in, left_in, right_in))
    edge_products(groups, sources, middles, halves(send), sectors, 1 - chip, core)


def edge_own(
    sectors, table, table_in, left, right, left_in, right_in, sources, keep, send, middles
):
    chip, core = position()
    groups = ((table, left, right), (table_in, left_in, right_in))
    edge_products(groups, sources, middles, (keep, send), sectors, chip, core)


def sum_kernel(inner_own, inner_chip, direct_far, later_far, near_own, other, sigma):
    core = lax.axis_index("op") & (CORES - 1)
    sectors = sigma.shape[0]
    far = sectors - EDGE
    split = EDGE + direct_far.shape[0] // CORES
    direct = split - EDGE
    sigma[EDGE:split] = inner_own[:direct] + inner_chip[:direct] + direct_far[:direct].astype(jnp.float32)
    sigma[split:far] = inner_own[direct:] + inner_chip[direct:] + later_far[CORES * EDGE :].astype(jnp.float32)
    sigma[pl.ds(far * core, EDGE)] = near_own[...] + later_far[:EDGE].astype(jnp.float32)
    sigma[pl.ds(far * (1 - core), EDGE)] = other[...]


SMALL = pl.BlockSpec(memory_space=pltpu.SMEM)
LARGE = pl.BlockSpec(memory_space=pl.ANY)
BLOCK = pl.BlockSpec(memory_space=pltpu.VMEM)
MIB = 1024 * 1024


def shards(wavefunction, left_ops, right_ops, charge, couple, amplitude):
    sec = lax.axis_size("sec")
    op = lax.axis_size("op")
    sectors, states = wavefunction.shape[:2]
    operators = left_ops.shape[0]
    half = states // op
    inner = sectors - 2 * EDGE
    wide, narrow = jnp.float32, jnp.bfloat16

    def shape(*dims, dtype=wide):
        return jax.ShapeDtypeStruct(dims, dtype)

    def run(kernel, ops, targets, operands, in_specs, outs, out_specs, scratch):
        return pl.pallas_call(
            kernel,
            out_shape=outs,
            in_specs=in_specs,
            out_specs=out_specs,
            scratch_shapes=[pltpu.VMEM((targets * CORES * half, ops * states), narrow)] + scratch,
            compiler_params=pltpu.CompilerParams(vmem_limit_bytes=20 * MIB),
            cost_estimate=pl.CostEstimate(
                flops=ops * targets * CORES * half * states * states * 4,
                bytes_accessed=ops * states * states * 4,
                transcendentals=0,
            ),
        )(*operands)

    def over_op(value, flip):
        return lax.ppermute(value, "op", [(i, i ^ flip) for i in range(op)])


    def per_target(value):
        return value.reshape(-1, half, states)

    ring = []
    for s in range(sec):
        for o in range(op):
            ring.append((s * op + o, (s + 1 if o % CORES == 0 else s - 1) % sec * op + o))

    def in_hbm(*values):
        return [pltpu.with_memory_space_constraint(value, pltpu.HBM) for value in values]

    border, table = pl.pallas_call(
        first_kernel,
        out_shape=[
            pltpu.VMEM((1, states, states), narrow),
            pltpu.VMEM((operators + 1, max(operators, sectors)), wide),
        ],
        in_specs=[LARGE] * 4,
        out_specs=[BLOCK] * 2,
        scratch_shapes=[
            pltpu.VMEM((1, operators), charge.dtype),
            pltpu.VMEM(couple.shape, couple.dtype),
            pltpu.VMEM(amplitude.shape, amplitude.dtype),
            pltpu.SemaphoreType.DMA((4,)),
        ],
        compiler_params=pltpu.CompilerParams(vmem_limit_bytes=4 * MIB),
        name="first_kernel",
    )(*in_hbm(charge, couple, amplitude, wavefunction))
    halo = lax.ppermute(border, ("sec", "op"), ring)
    left_in = over_op(left_ops, 1)
    right_in = over_op(right_ops, 1)

    table_in = over_op(table, 1)

    direct_rows = inner // 2 * half
    reduced = shape(inner * half - direct_rows, states)
    direct, keep, send, right, cells = run(
        inner_far_kernel,
        operators,
        inner,
        [table, left_ops, *in_hbm(right_ops, wavefunction)],
        [BLOCK] * 2 + [LARGE] * 2,
        [
            shape(CORES * direct_rows, states, dtype=narrow),
            reduced,
            reduced,
            pltpu.VMEM(right_ops.shape, narrow),
            pltpu.VMEM(wavefunction.shape, narrow),
        ],
        [BLOCK] * 5,
        [
            pltpu.SMEM(table.shape, table.dtype),
            pltpu.SemaphoreType.DMA,
            pltpu.SemaphoreType.DMA((sectors,)),
            pltpu.SemaphoreType.DMA((operators,)),
        ],
    )
    direct_far = over_op(direct, CORES)
    send_in = over_op(send, 1)

    held = [table, table_in, left_ops, right, left_in, right_in]
    held_specs = [SMALL] * 2 + [BLOCK] * 4
    edge_send, sources = run(
        edge_far_kernel,
        CORES * operators,
        EDGE,
        held + [cells, halo],
        held_specs + [BLOCK, BLOCK],
        [shape(CORES * EDGE * half, states, dtype=narrow), shape(EDGE + 2, states, states, dtype=narrow)],
        [BLOCK, BLOCK],
        [pltpu.SemaphoreType.DMA((2,))],
    )
    later = jnp.concatenate([edge_send, (keep + send_in).astype(narrow)], axis=0)
    later_far = over_op(later, CORES)
    block = shape(inner * half, states)
    inner_own, inner_send = run(
        inner_own_kernel,
        operators,
        inner,
        [table, left_ops, right, cells],
        [SMALL] + [BLOCK] * 3,
        [block, block],
        [BLOCK, BLOCK],
        [],
    )
    mate = inner_send[:direct_rows] + direct_far[direct_rows:].astype(wide)
    inner_chip = over_op(jnp.concatenate([mate, inner_send[direct_rows:]], axis=0), 1)
    edge_wide = shape(EDGE * half, states)

    def edge_own_kernel(*refs):
        edge_own(sectors, *refs)

    near_own, near_mate = run(
        edge_own_kernel,
        CORES * operators,
        EDGE,
        held + [sources],
        held_specs + [BLOCK],
        [edge_wide, edge_wide],
        [BLOCK, BLOCK],
        [],
    )
    passed = later_far[EDGE * half : CORES * EDGE * half].astype(wide)
    other = over_op(near_mate + passed, 1)
    parts = (inner_own, inner_chip, direct_far, later_far, near_own, other)
    return pl.pallas_call(
        sum_kernel,
        out_shape=shape(sectors, half, states),
        in_specs=[BLOCK] * len(parts),
        out_specs=BLOCK,
        compiler_params=pltpu.CompilerParams(vmem_limit_bytes=16 * MIB),
        name="total",
    )(*[per_target(part) for part in parts])


def solution(mesh):
    placed = (
        P("sec", None, None),
        P("op", None, None),
        P("op", None, None),
        P("op"),
        P("op", "sec"),
        P("op", "sec"),
    )
    two_chips = mesh.shape["op"] == CORES * CORES
    return jax.shard_map(
        shards if two_chips else plain_shards,
        mesh=mesh, in_specs=placed, out_specs=P("sec", "op", None), check_vma=False,
    )
```

```python
import jax
import jax.numpy as jnp
from jax import lax
from jax.experimental import pallas as pl
from jax.experimental.pallas import tpu as pltpu
from jax.sharding import PartitionSpec as P


CORES = 2
EDGE = 2


def padded(cells, sides, width):
    for axis, dim in sides:
        count = lax.axis_size(axis)
        head = lax.slice_in_dim(cells, 0, width, axis=dim)
        tail = lax.slice_in_dim(cells, cells.shape[dim] - width, cells.shape[dim], axis=dim)
        cells = jnp.concatenate(
            [
                lax.ppermute(tail, axis, [(i, (i + 1) % count) for i in range(count)]),
                cells,
                lax.ppermute(head, axis, [((i + 1) % count, i) for i in range(count)]),
            ],
            axis=dim,
        )
    return cells


def batched(left_op, sources, right_op, factor_values):
    middle = jnp.einsum("ij,sjk->sik", left_op, sources, preferred_element_type=jnp.float32).astype(
        jnp.bfloat16
    )
    contribution = jnp.einsum("sik,lk->sil", middle, right_op, preferred_element_type=jnp.float32)
    return contribution * factor_values[:, None, None]


def plain_shards(wavefunction, left_ops, right_ops, charge, couple, amplitude):
    factor = amplitude * couple.astype(jnp.float32)
    sectors = wavefunction.shape[0]
    states = wavefunction.shape[1]
    extended = padded(wavefunction, (("sec", 0),), 1)

    def accumulate(accumulated, operands):
        left_op, right_op, sector_shift, factor_row = operands
        start = 1 - sector_shift
        sources = lax.dynamic_slice_in_dim(extended, start, sectors, 0)
        return (accumulated + batched(left_op, sources, right_op, factor_row), None)

    initial = jnp.zeros((sectors, states, states), jnp.float32)
    accumulated, _ = lax.scan(accumulate, initial, (left_ops, right_ops, charge, factor))
    return lax.psum_scatter(accumulated, "op", scatter_dimension=1, tiled=True)


def middle_of(k, table, own, left, sources, middles, first_target, targets, chip, core):
    states = sources.shape[-1]
    half = middles.shape[0] // (CORES * targets)
    shift = 1 - table[table.shape[0] - 1, own].astype(jnp.int32)
    wide = jnp.concatenate([sources[shift + t] for t in range(targets)], axis=1)
    rows = jnp.concatenate(
        [left[own, pl.ds(row_of(chip, owner, half), half)] for owner in (core, 1 - core)], axis=0
    )
    middle = jnp.dot(rows, wide, preferred_element_type=jnp.float32)
    for t in range(targets):
        factor = table[own, first_target + t]
        block = middle[:, t * states : (t + 1) * states].astype(jnp.bfloat16)
        block = (block.astype(jnp.float32) * factor).astype(jnp.bfloat16)
        for part in range(CORES):
            row = (part * targets + t) * half
            middles[row : row + half, k * states : (k + 1) * states] = block[part * half : (part + 1) * half]


def summed(right, middles, results):
    count = middles.shape[0]
    step = 256
    for low in range(0, count, step):
        high = min(low + step, count)
        total = lax.dot_general(
            right, middles[low:high, :], (((1,), (1,)), ((), ())), preferred_element_type=jnp.float32
        ).T
        first = 0
        for result in results:
            last = first + result.shape[0]
            start, end = max(low, first), min(high, last)
            if start < end:
                result[start - first : end - first, :] = total[start - low : end - low, :].astype(result.dtype)
            first = last


def halves(results):
    width = results.shape[0] // CORES
    return [results.at[pl.ds(part * width, width)] for part in range(CORES)]


def position():
    place = lax.axis_index("op")
    return lax.shift_right_logical(place, CORES - 1), place & (CORES - 1)


def row_of(chip, core, half):
    return pl.multiple_of((chip * CORES + core) * half, 32)


def begin(source, target, sem):
    copy = pltpu.make_async_copy(source, target, sem)
    copy.start()
    return copy


def first_kernel(
    charge, couple, amplitude, cells_far, border, table, charge_here, couple_here, amplitude_here, sem
):
    _, core = position()
    operators, sectors = couple.shape
    copies = [
        begin(charge, charge_here.at[0], sem.at[0]),
        begin(couple, couple_here, sem.at[1]),
        begin(amplitude, amplitude_here, sem.at[2]),
        begin(cells_far.at[(sectors - 1) * (1 - core)], border.at[0], sem.at[3]),
    ]
    for copy in copies:
        copy.wait()
    table[:operators, :sectors] = amplitude_here[...] * couple_here[...].astype(jnp.float32)
    table[operators:, :operators] = charge_here[...].astype(jnp.float32)


def inner_far_kernel(
    table_kept, left, right_far, cells_far, direct, keep, send, right, cells, middles,
    table, table_sem, cell_sem, right_sem,
):
    chip, core = position()
    operators = left.shape[0]
    sectors = cells.shape[0]
    targets = sectors - 2 * EDGE
    inside = range(EDGE - 1, sectors - EDGE + 1)

    def cell(s):
        return begin(cells_far.at[s], cells.at[s], cell_sem.at[s])

    first = [cell(s) for s in inside]
    begin(table_kept, table, table_sem).wait()
    for copy in first[: len(first) // 2]:
        copy.wait()
    rights = [begin(right_far.at[k], right.at[k], right_sem.at[k]) for k in range(operators)]
    later = [cell(s) for s in range(sectors) if s not in inside]
    for copy in first[len(first) // 2 :]:
        copy.wait()
    sources = cells.at[pl.ds(EDGE - 1, targets + 2)]
    for k in range(operators):
        middle_of(k, table, k, left, sources, middles, EDGE, targets, 1 - chip, core)
    for copy in rights:
        copy.wait()
    near, far = halves(direct)
    summed(jnp.concatenate([right[k] for k in range(operators)], axis=1), middles, (near, keep, far, send))
    for copy in later:
        copy.wait()


def inner_own_kernel(table, left, right, cells, keep, send, middles):
    chip, core = position()
    operators = left.shape[0]
    targets = cells.shape[0] - 2 * EDGE
    inside = cells.at[pl.ds(EDGE - 1, targets + 2)]
    for k in range(operators):
        middle_of(k, table, k, left, inside, middles, EDGE, targets, chip, core)
    summed(jnp.concatenate([right[k] for k in range(operators)], axis=1), middles, (keep, send))


def edge_products(groups, sources, middles, results, sectors, chip, core):
    k = 0
    first_target = (sectors - EDGE) * core
    for table, left, right in groups:
        for own in range(left.shape[0]):
            middle_of(k, table, own, left, sources, middles, first_target, EDGE, chip, core)
            k += 1
    wide = jnp.concatenate([right[own] for _, _, right in groups for own in range(right.shape[0])], axis=1)
    summed(wide, middles, results)


def edge_far_kernel(
    table, table_in, left, right, left_in, right_in, cells, halo, send, sources, middles, sem,
):
    chip, core = position()
    sectors = cells.shape[0]
    inside = EDGE + 1
    copies = [
        pltpu.make_async_copy(
            cells.at[pl.ds((sectors - inside) * core, inside)], sources.at[pl.ds(1 - core, inside)], sem.at[0]
        ),
        pltpu.make_async_copy(halo.at[0], sources.at[inside * core], sem.at[1]),
    ]
    for copy in copies:
        copy.start()
    for copy in copies:
        copy.wait()
    groups = ((table, left, right), (table_in, left_in, right_in))
    edge_products(groups, sources, middles, halves(send), sectors, 1 - chip, core)


def edge_own(
    sectors, table, table_in, left, right, left_in, right_in, sources, keep, send, middles
):
    chip, core = position()
    groups = ((table, left, right), (table_in, left_in, right_in))
    edge_products(groups, sources, middles, (keep, send), sectors, chip, core)


def sum_kernel(inner_own, inner_chip, direct_far, later_far, near_own, other, sigma):
    core = lax.axis_index("op") & (CORES - 1)
    sectors = sigma.shape[0]
    far = sectors - EDGE
    split = EDGE + direct_far.shape[0] // CORES
    direct = split - EDGE
    sigma[EDGE:split] = inner_own[:direct] + inner_chip[:direct] + direct_far[:direct].astype(jnp.float32)
    sigma[split:far] = inner_own[direct:] + inner_chip[direct:] + later_far[CORES * EDGE :].astype(jnp.float32)
    sigma[pl.ds(far * core, EDGE)] = near_own[...] + later_far[:EDGE].astype(jnp.float32)
    sigma[pl.ds(far * (1 - core), EDGE)] = other[...]


SMALL = pl.BlockSpec(memory_space=pltpu.SMEM)
LARGE = pl.BlockSpec(memory_space=pl.ANY)
BLOCK = pl.BlockSpec(memory_space=pltpu.VMEM)
MIB = 1024 * 1024


def shards(wavefunction, left_ops, right_ops, charge, couple, amplitude):
    sec = lax.axis_size("sec")
    op = lax.axis_size("op")
    sectors, states = wavefunction.shape[:2]
    operators = left_ops.shape[0]
    half = states // op
    inner = sectors - 2 * EDGE
    wide, narrow = jnp.float32, jnp.bfloat16

    def shape(*dims, dtype=wide):
        return jax.ShapeDtypeStruct(dims, dtype)

    def run(kernel, ops, targets, operands, in_specs, outs, out_specs, scratch):
        return pl.pallas_call(
            kernel,
            out_shape=outs,
            in_specs=in_specs,
            out_specs=out_specs,
            scratch_shapes=[pltpu.VMEM((targets * CORES * half, ops * states), narrow)] + scratch,
            compiler_params=pltpu.CompilerParams(vmem_limit_bytes=20 * MIB),
            cost_estimate=pl.CostEstimate(
                flops=ops * targets * CORES * half * states * states * 4,
                bytes_accessed=ops * states * states * 4,
                transcendentals=0,
            ),
        )(*operands)

    def over_op(value, flip):
        return lax.ppermute(value, "op", [(i, i ^ flip) for i in range(op)])


    def per_target(value):
        return value.reshape(-1, half, states)

    ring = []
    for s in range(sec):
        for o in range(op):
            ring.append((s * op + o, (s + 1 if o % CORES == 0 else s - 1) % sec * op + o))

    def in_hbm(*values):
        return [pltpu.with_memory_space_constraint(value, pltpu.HBM) for value in values]

    border, table = pl.pallas_call(
        first_kernel,
        out_shape=[
            pltpu.VMEM((1, states, states), narrow),
            pltpu.VMEM((operators + 1, max(operators, sectors)), wide),
        ],
        in_specs=[LARGE] * 4,
        out_specs=[BLOCK] * 2,
        scratch_shapes=[
            pltpu.VMEM((1, operators), charge.dtype),
            pltpu.VMEM(couple.shape, couple.dtype),
            pltpu.VMEM(amplitude.shape, amplitude.dtype),
            pltpu.SemaphoreType.DMA((4,)),
        ],
        compiler_params=pltpu.CompilerParams(vmem_limit_bytes=4 * MIB),
        name="first_kernel",
    )(*in_hbm(charge, couple, amplitude, wavefunction))
    halo = lax.ppermute(border, ("sec", "op"), ring)
    left_in = over_op(left_ops, 1)
    right_in = over_op(right_ops, 1)

    table_in = over_op(table, 1)

    direct_rows = inner // 2 * half
    reduced = shape(inner * half - direct_rows, states)
    direct, keep, send, right, cells = run(
        inner_far_kernel,
        operators,
        inner,
        [table, left_ops, *in_hbm(right_ops, wavefunction)],
        [BLOCK] * 2 + [LARGE] * 2,
        [
            shape(CORES * direct_rows, states, dtype=narrow),
            reduced,
            reduced,
            pltpu.VMEM(right_ops.shape, narrow),
            pltpu.VMEM(wavefunction.shape, narrow),
        ],
        [BLOCK] * 5,
        [
            pltpu.SMEM(table.shape, table.dtype),
            pltpu.SemaphoreType.DMA,
            pltpu.SemaphoreType.DMA((sectors,)),
            pltpu.SemaphoreType.DMA((operators,)),
        ],
    )
    direct_far = over_op(direct, CORES)
    send_in = over_op(send, 1)

    held = [table, table_in, left_ops, right, left_in, right_in]
    held_specs = [SMALL] * 2 + [BLOCK] * 4
    edge_send, sources = run(
        edge_far_kernel,
        CORES * operators,
        EDGE,
        held + [cells, halo],
        held_specs + [BLOCK, BLOCK],
        [shape(CORES * EDGE * half, states, dtype=narrow), shape(EDGE + 2, states, states, dtype=narrow)],
        [BLOCK, BLOCK],
        [pltpu.SemaphoreType.DMA((2,))],
    )
    later = jnp.concatenate([edge_send, (keep + send_in).astype(narrow)], axis=0)
    later_far = over_op(later, CORES)
    block = shape(inner * half, states)
    inner_own, inner_send = run(
        inner_own_kernel,
        operators,
        inner,
        [table, left_ops, right, cells],
        [SMALL] + [BLOCK] * 3,
        [block, block],
        [BLOCK, BLOCK],
        [],
    )
    mate = inner_send[:direct_rows] + direct_far[direct_rows:].astype(wide)
    inner_chip = over_op(jnp.concatenate([mate, inner_send[direct_rows:]], axis=0), 1)
    edge_wide = shape(EDGE * half, states)

    def edge_own_kernel(*refs):
        edge_own(sectors, *refs)

    near_own, near_mate = run(
        edge_own_kernel,
        CORES * operators,
        EDGE,
        held + [sources],
        held_specs + [BLOCK],
        [edge_wide, edge_wide],
        [BLOCK, BLOCK],
        [],
    )
    passed = later_far[EDGE * half : CORES * EDGE * half].astype(wide)
    other = over_op(near_mate + passed, 1)
    parts = (inner_own, inner_chip, direct_far, later_far, near_own, other)
    return pl.pallas_call(
        sum_kernel,
        out_shape=shape(sectors, half, states),
        in_specs=[BLOCK] * len(parts),
        out_specs=BLOCK,
        compiler_params=pltpu.CompilerParams(vmem_limit_bytes=16 * MIB),
        name="total",
    )(*[per_target(part) for part in parts])


def solution(mesh):
    placed = (
        P("sec", None, None),
        P("op", None, None),
        P("op", None, None),
        P("op"),
        P("op", "sec"),
        P("op", "sec"),
    )
    two_chips = mesh.shape["op"] == CORES * CORES
    return jax.shard_map(
        shards if two_chips else plain_shards,
        mesh=mesh, in_specs=placed, out_specs=P("sec", "op", None), check_vma=False,
    )
```
